32 devices in a mesh: member: 2 (over y), lat: 4 (over z), lev: 2 (over x), fld: 2 (over core).
Axes of the slice: x: 2, y: 2, z: 4, core: 2. Of those that a mesh axis runs over, the one named last changes fastest.
Arguments:
- grid_state: bfloat16 [4, 48, 480, 1920], P(('member', 'fld'), 'lev', 'lat'), parts along dimension 0, may hold values from -6 to 6
- lat_order: int32 [480], replicated, may hold values from 0 to 479, each once
- slot_wave: int32 [384], replicated, may hold values from 0 to 383, each once
- truncation: int32 [384], replicated, may hold values from 288 to 383, as said below
- zonal_wind: float32 [480], replicated, may hold values from -3 to 3
- zonal_rate: float32 [480], replicated, may hold values from 0.0003 to 0.003
- quad_weight: float32 [480], replicated, may hold values from 0.02 to 0.09
- legendre: bfloat16 [384, 384, 480], P(('lat', 'lev')), may hold values from -5 to 5
- vert_modes: float32 [48, 48], replicated, may hold values from -0.875 to 0.875
- vert_project: float32 [48, 48], replicated, may hold values from -0.875 to 0.875
- mode_rates: float32 [48], replicated, may hold values from 0.5 to 8
- thermal_into_spread_matrix: float32 [48, 48], replicated, may hold values from -0.875 to 0.875
- pressure_balance_matrix: float32 [48, 48], replicated, may hold values from -0.875 to 0.875
Outputs:
- grid_new: bfloat16 [4, 48, 480, 1920], P(('member', 'fld'), 'lev', 'lat'), parts along dimension 0
The draws below stay inside these ranges and needn't reach their ends.
There are 2 independent parts, one for each index of `member`. The reference program is written for one: setup_inputs(seed, part) draws one part's arguments, and reference() takes and returns one part's arrays. A program takes and returns all parts, laid end to end along the dimension named above; an argument that names none is the same for every part. Nothing has to cross between parts.
Inputs may be any that keep to these rules, and one draw needn't show every extreme that they name: `lat_order`: each latitude once. `slot_wave`: each wavenumber once. truncation[m] is never below m, and truncation[383] = 383.
All inputs are finite; a program needn't handle non-finite values.
Results may differ from the reference program's by a relative error of at most 0.0071.
Values may be sent and summed in bfloat16 or wider, within the bound.
No kernel may reach another device: no remote copies, remote signals or barrier semaphores. Data moves between devices by JAX's collectives and lax.ppermute only.
A program may use at most 128 MiB of HBM per device.

```python
import math
import jax
import jax.numpy as jnp
from jax import lax

COUPLED_UNKNOWNS = 2
HEIGHT_LAYERS = 48
NLAT = 480
NLON = 1920
EAST_MODES = 384


def draw_truncation(key, part):
    wavenums = jnp.arange(EAST_MODES, dtype=jnp.int32)
    spare = EAST_MODES - 1 - wavenums
    cutoff = jax.random.randint(key, (EAST_MODES,), 0, spare // 4 + 1)
    return (EAST_MODES - 1 - cutoff).astype(jnp.int32)


def level_of(key, shape, cuts, low, top_value):
    factor_of = 1.0
    for dim, parts in cuts:
        steps = jax.random.uniform(jax.random.fold_in(jax.random.fold_in(key, 6), dim), (parts,), jnp.float32, low / len(cuts), top_value / len(cuts))
        factor_of = factor_of * jnp.repeat(jnp.exp(steps), shape[dim] // parts).reshape((-1,) + (1,) * (len(shape) - 1 - dim))
    return factor_of


def noise(stream_key, shape, width, reach, cuts=(), kind=jnp.bfloat16):
    gain = level_of(stream_key, shape, cuts, -0.22, 0.18) if cuts else 1.0
    result = jax.random.normal(stream_key, shape, jnp.float32) * width * gain
    return jnp.minimum(jnp.maximum(result, -reach), reach).astype(kind)


def setup_inputs(seed: int = 0, part: int = 0) -> dict:
    streams_of = jax.random.split(jax.random.key(seed), 14)
    part_splits = jax.random.split(jax.random.fold_in(streams_of[13], part), 14)
    grid_state = noise(part_splits[0], (COUPLED_UNKNOWNS, HEIGHT_LAYERS, NLAT, NLON), 1.0, 6.0, ((0, 2), (1, 2), (2, 4)))
    lat_order = jax.random.permutation(streams_of[1], NLAT).astype(jnp.int32)
    slot_wave = jax.random.permutation(streams_of[2], EAST_MODES).astype(jnp.int32)
    truncation = draw_truncation(jax.random.fold_in(streams_of[13], 71), part)
    zonal_wind = noise(streams_of[4], (NLAT,), 0.5, 3.0, (), jnp.float32)
    zonal_rate = jnp.clip(jnp.exp(jax.random.uniform(streams_of[5], (NLAT,), jnp.float32, math.log(0.0003), math.log(0.003))), 0.0003, 0.003)
    quad_weight = jnp.clip(jnp.exp(jax.random.uniform(streams_of[6], (NLAT,), jnp.float32, math.log(0.02), math.log(0.09))), 0.02, 0.09)
    legendre = noise(streams_of[7], (EAST_MODES, EAST_MODES, NLAT), 1.0, 5.0, ((0, 8),))
    vert_modes = noise(streams_of[8], (HEIGHT_LAYERS, HEIGHT_LAYERS), HEIGHT_LAYERS ** -0.5, 0.875, (), jnp.float32)
    vert_project = noise(streams_of[9], (HEIGHT_LAYERS, HEIGHT_LAYERS), HEIGHT_LAYERS ** -0.5, 0.875, (), jnp.float32)
    mode_rates = jnp.clip(jnp.exp(jax.random.uniform(streams_of[10], (HEIGHT_LAYERS,), jnp.float32, math.log(0.5), math.log(8.0))), 0.5, 8.0)
    thermal_into_spread_matrix = noise(streams_of[11], (HEIGHT_LAYERS, HEIGHT_LAYERS), HEIGHT_LAYERS ** -0.5, 0.875, (), jnp.float32)
    pressure_balance_matrix = noise(streams_of[12], (HEIGHT_LAYERS, HEIGHT_LAYERS), HEIGHT_LAYERS ** -0.5, 0.875, (), jnp.float32)
    return dict(grid_state=grid_state, lat_order=lat_order, slot_wave=slot_wave, truncation=truncation, zonal_wind=zonal_wind, zonal_rate=zonal_rate, quad_weight=quad_weight, legendre=legendre, vert_modes=vert_modes, vert_project=vert_project, mode_rates=mode_rates, thermal_into_spread_matrix=thermal_into_spread_matrix, pressure_balance_matrix=pressure_balance_matrix)


PRECISE = lax.Precision.HIGHEST


def dft_table(wavenums):
    columns = jnp.arange(NLON, dtype=jnp.int32)
    turns = (columns[:, None] * wavenums[None, :]) % NLON
    angles = turns.astype(jnp.float32) * (2.0 * jnp.pi / NLON)
    return jnp.stack([jnp.cos(angles), -jnp.sin(angles)], axis=1).astype(jnp.bfloat16)


def layer_eigen_basis(matrix, columns):
    return jnp.einsum("skcj,ij->skci", columns, matrix, precision=PRECISE)


def analyse_slot(pieces):
    return jnp.dot(pieces[0], pieces[1], preferred_element_type=jnp.float32)


def synth_slot(pieces):
    return lax.dot_general(pieces[0], pieces[1], (((0,), (0,)), ((), ())), preferred_element_type=jnp.float32)


def reference(grid_state, lat_order, slot_wave, truncation, zonal_wind, zonal_rate, quad_weight, legendre, vert_modes, vert_project, mode_rates, thermal_into_spread_matrix, pressure_balance_matrix):
    table = dft_table(slot_wave.astype(jnp.int32)).reshape(NLON, 2 * EAST_MODES)
    winds = zonal_wind[lat_order]
    rates = zonal_rate[lat_order]
    weights = quad_weight[lat_order]
    values = grid_state.astype(jnp.float32)
    flux = (values * (winds[None, None, :, None] + values)).astype(jnp.bfloat16)
    count_rows = COUPLED_UNKNOWNS * HEIGHT_LAYERS * NLAT
    plain = jnp.dot(grid_state.reshape(count_rows, NLON), table, preferred_element_type=jnp.float32) * NLON ** -0.5
    moved = jnp.dot(flux.reshape(count_rows, NLON), table, preferred_element_type=jnp.float32) * NLON ** -0.5
    plain = plain.reshape(COUPLED_UNKNOWNS, HEIGHT_LAYERS, NLAT, 2, EAST_MODES)
    moved = moved.reshape(COUPLED_UNKNOWNS, HEIGHT_LAYERS, NLAT, 2, EAST_MODES)
    wave_float = slot_wave.astype(jnp.float32)
    factor = rates[:, None] * wave_float[None, :]
    real_part = (plain[:, :, :, 0] + factor * moved[:, :, :, 1]) * weights[:, None]
    imag_part = (plain[:, :, :, 1] - factor * moved[:, :, :, 0]) * weights[:, None]
    fourier = jnp.stack([real_part, imag_part], axis=3).astype(jnp.bfloat16)
    position = jnp.zeros((NLAT,), jnp.int32).at[lat_order].set(jnp.arange(NLAT, dtype=jnp.int32))
    fourier = jnp.take(fourier, position, axis=2)
    gathered = jnp.transpose(fourier, (4, 2, 0, 3, 1)).reshape(EAST_MODES, NLAT, COUPLED_UNKNOWNS * 2 * HEIGHT_LAYERS)
    harmonic_current = lax.map(analyse_slot, (legendre, gathered))
    limits = truncation[slot_wave]
    counts = limits - slot_wave + 1
    degree = jnp.arange(EAST_MODES, dtype=jnp.int32)
    valid = degree[None, :] < counts[:, None]
    harmonic_current = jnp.where(valid[:, :, None], harmonic_current, jnp.float32(0.0))
    harmonic_current = harmonic_current.reshape(EAST_MODES, EAST_MODES, COUPLED_UNKNOWNS, 2, HEIGHT_LAYERS)
    outflow_rate_coeffs = harmonic_current[:, :, 0]
    thermal_coeffs = harmonic_current[:, :, 1]
    n_deg = (slot_wave[:, None] + degree[None, :]).astype(jnp.float32)
    elliptic_inverse_scale = (n_deg * (n_deg + 1.0) / (EAST_MODES * (EAST_MODES - 1)))[:, :, None, None]
    outflow_rate_source = outflow_rate_coeffs + elliptic_inverse_scale * layer_eigen_basis(thermal_into_spread_matrix, thermal_coeffs)
    projected = layer_eigen_basis(vert_project, outflow_rate_source) / (1.0 + elliptic_inverse_scale * mode_rates)
    outflow_rate_next = layer_eigen_basis(vert_modes, projected)
    thermal_next = thermal_coeffs - layer_eigen_basis(pressure_balance_matrix, outflow_rate_next)
    harmonic_next = jnp.stack([outflow_rate_next, thermal_next], axis=2).astype(jnp.bfloat16).reshape(EAST_MODES, EAST_MODES, COUPLED_UNKNOWNS * 2 * HEIGHT_LAYERS)
    back = lax.map(synth_slot, (legendre, harmonic_next)) * EAST_MODES ** -0.5
    back = jnp.take(back, lat_order, axis=1).astype(jnp.bfloat16)
    back = back.reshape(EAST_MODES, NLAT, COUPLED_UNKNOWNS, 2, HEIGHT_LAYERS)
    leading = jnp.transpose(back, (3, 0, 2, 4, 1)).reshape(2 * EAST_MODES, count_rows)
    grid_out = lax.dot_general(leading, table, (((0,), (1,)), ((), ())), preferred_element_type=jnp.float32) * EAST_MODES ** -0.5
    return grid_out.reshape(COUPLED_UNKNOWNS, HEIGHT_LAYERS, NLAT, NLON).astype(jnp.bfloat16)
```

```python
import functools

import jax
import jax.numpy as jnp
from jax import lax
from jax.experimental import pallas as pl
from jax.experimental.pallas import tpu as pltpu
from jax.sharding import PartitionSpec as P

PRECISE = lax.Precision.HIGHEST
BF16 = jnp.bfloat16
F32 = jnp.float32


def dft_table(wavenums, nlon):
    columns = jnp.arange(nlon, dtype=jnp.int32)
    turns = columns[:, None] * wavenums[None, :] % nlon
    angles = turns.astype(jnp.float32) * (2.0 * jnp.pi / nlon)
    return jnp.stack([jnp.cos(angles), -jnp.sin(angles)], axis=1).astype(jnp.bfloat16)


def pick_values(idents, source_table):
    hits = idents[:, None] == jnp.arange(source_table.shape[0], dtype=jnp.int32)[None, :]
    return jnp.sum(jnp.where(hits, source_table[None, :], 0), axis=1)


def layer_eigen_basis(matrix, columns):
    return jnp.einsum("skcj,ij->skci", columns, matrix, precision=PRECISE)


def analyse(legendre, fourier_data):
    return jnp.einsum("skl,slx->skx", legendre, fourier_data, preferred_element_type=jnp.float32)


def synthesise(legendre, coeffs):
    return jnp.einsum("skl,skx->slx", legendre, coeffs, preferred_element_type=jnp.float32)


def local_general(
    grid_state,
    lat_order,
    slot_wave,
    truncation,
    zonal_wind,
    zonal_rate,
    quad_weight,
    legendre,
    vert_modes,
    vert_project,
    mode_rates,
    thermal_into_spread_matrix,
    pressure_balance_matrix,
):
    levd, latd, nlon = (grid_state.shape[1], grid_state.shape[2], grid_state.shape[3])
    slots = legendre.shape[0]
    nmodes = slot_wave.shape[0]
    nlat = lat_order.shape[0]
    nlev = vert_modes.shape[0]
    lat_count = lax.axis_size("lat")
    lev_count = lax.axis_size("lev")
    lat_index = lax.axis_index("lat")
    lev_index = lax.axis_index("lev")
    unknown_position = lax.axis_index("fld")
    my_lats = lax.dynamic_slice_in_dim(lat_order, lat_index * latd, latd)
    onehot = (my_lats[:, None] == jnp.arange(nlat, dtype=jnp.int32)[None, :]).astype(jnp.float32)
    per_lat = jnp.dot(
        onehot, jnp.stack([zonal_wind, zonal_rate, quad_weight], axis=1), precision=PRECISE
    )
    values = grid_state[0].astype(jnp.float32)
    flux = (values * (per_lat[None, :, 0][:, :, None] + values)).astype(jnp.bfloat16)
    count_rows = levd * latd
    stacked = jnp.concatenate(
        [grid_state[0].reshape(count_rows, nlon), flux.reshape(count_rows, nlon)], axis=0
    )
    table = dft_table(slot_wave, nlon).reshape(nlon, 2 * nmodes)
    spectra = lax.dot_general(
        table, stacked, (((0,), (1,)), ((), ())), preferred_element_type=jnp.float32
    ) * nlon ** (-0.5)
    spectra = spectra.reshape(2, nmodes, 2 * count_rows)
    plain = spectra[:, :, :count_rows]
    moved = spectra[:, :, count_rows:]
    rate_row = jnp.tile(per_lat[:, 1], levd)[None, :]
    weight_row = jnp.tile(per_lat[:, 2], levd)[None, :]
    wave_float = slot_wave.astype(jnp.float32)[:, None]
    factor = rate_row * wave_float
    real_part = (plain[0] + factor * moved[1]) * weight_row
    imag_part = (plain[1] - factor * moved[0]) * weight_row
    fourier = jnp.stack([real_part, imag_part], axis=0).astype(jnp.bfloat16)
    arrived = lax.all_to_all(fourier, ("lat", "lev"), split_axis=1, concat_axis=2, tiled=True)
    arrived = arrived.reshape(2, slots, lat_count, lev_count, levd, latd)
    arranged = jnp.transpose(arrived, (1, 2, 5, 0, 3, 4))
    arranged = arranged.reshape(slots, nlat, 2 * nlev)
    position = jnp.zeros((nlat,), jnp.int32).at[lat_order].set(jnp.arange(nlat, dtype=jnp.int32))
    ordered = jnp.take(arranged, position, axis=1)
    owner_index = lat_index * lev_count + lev_index
    my_waves = lax.dynamic_slice_in_dim(slot_wave, owner_index * slots, slots)
    limits = pick_values(my_waves, truncation)
    counts = limits - my_waves + 1
    degree = jnp.arange(nmodes, dtype=jnp.int32)
    valid = (degree[None, :] < counts[:, None])[:, :, None]
    own_spec = jnp.where(valid, analyse(legendre, ordered), jnp.float32(0.0))
    joined_harmonic_unknowns = lax.all_gather(own_spec, "fld", axis=2, tiled=True)
    joined_harmonic_unknowns = joined_harmonic_unknowns.reshape(slots, nmodes, 2, 2, nlev)
    outflow_rate_coeffs = joined_harmonic_unknowns[:, :, 0]
    thermal_coeffs = joined_harmonic_unknowns[:, :, 1]
    n_deg = (my_waves[:, None] + degree[None, :]).astype(jnp.float32)
    elliptic_inverse_scale = (n_deg * (n_deg + 1.0) / (nmodes * (nmodes - 1)))[:, :, None, None]
    outflow_rate_source = outflow_rate_coeffs + elliptic_inverse_scale * layer_eigen_basis(
        thermal_into_spread_matrix, thermal_coeffs
    )
    projected = layer_eigen_basis(vert_project, outflow_rate_source) / (
        1.0 + elliptic_inverse_scale * mode_rates
    )
    outflow_rate_next = layer_eigen_basis(vert_modes, projected)
    thermal_next = thermal_coeffs - layer_eigen_basis(pressure_balance_matrix, outflow_rate_next)
    own_new = (
        jnp.where(unknown_position == 0, outflow_rate_next, thermal_next)
        .astype(jnp.bfloat16)
        .reshape(slots, nmodes, 2 * nlev)
    )
    back = synthesise(legendre, own_new) * nmodes ** (-0.5)
    back = jnp.take(back, lat_order, axis=1).astype(jnp.bfloat16)
    shaped = back.reshape(slots, lat_count, latd, 2, lev_count, levd)
    outgoing = jnp.transpose(shaped, (3, 0, 1, 4, 5, 2)).reshape(
        2, slots, lat_count * lev_count * count_rows
    )
    returned = lax.all_to_all(outgoing, ("lat", "lev"), split_axis=2, concat_axis=1, tiled=True)
    leading = returned.reshape(2 * nmodes, count_rows)
    grid_out = lax.dot_general(
        leading, table, (((0,), (1,)), ((), ())), preferred_element_type=jnp.float32
    ) * nmodes ** (-0.5)
    return grid_out.astype(jnp.bfloat16).reshape(1, levd, latd, nlon)


LANES = 128


def xor_order(array, index, axis):
    size = array.shape[axis]
    bits = size.bit_length() - 1
    shape = array.shape[:axis] + (2,) * bits + array.shape[axis + 1 :]
    out = array.reshape(shape)
    for b in range(bits):
        ax = axis + bits - 1 - b
        out = jnp.where((index >> b) & 1 == 1, jnp.flip(out, ax), out)
    return out.reshape(array.shape)


def table_kernel(nblk, hi_c, hi_s, lo_c, lo_s, out):
    rows = hi_c.shape[0]
    cl, sl = lo_c[...], lo_s[...]
    for b in range(nblk):
        ch, sh = hi_c[:, b : b + 1], hi_s[:, b : b + 1]
        cols = slice(b * LANES, (b + 1) * LANES)
        out[:rows, cols] = (ch * cl - sh * sl).astype(BF16)
        out[rows:, cols] = (-(sh * cl + ch * sl)).astype(BF16)


def make_table(waves, nlon):
    nblk = nlon // LANES
    scale = 2.0 * jnp.pi / nlon
    step_lo = jnp.arange(LANES, dtype=jnp.int32)
    step_hi = jnp.arange(LANES, dtype=jnp.int32) * LANES
    lo = (waves[:, None] * step_lo[None, :] % nlon).astype(F32) * scale
    hi = (waves[:, None] * step_hi[None, :] % nlon).astype(F32) * scale
    rows = waves.shape[0]
    return pl.pallas_call(
        functools.partial(table_kernel, nblk),
        out_shape=jax.ShapeDtypeStruct((2 * rows, nlon), BF16),
        name="table",
    )(jnp.cos(hi), jnp.sin(hi), jnp.cos(lo), jnp.sin(lo))


def dft_kernel(groups, vb, latd, x_ref, t_ref, wind_ref, lat_ref, wave_ref, *rest):
    outs, (xf, scr) = rest[:groups], rest[groups:]
    rows = t_ref.shape[0]
    half = rows // 2
    per = half // groups
    nblk = x_ref.shape[2] // LANES

    @pl.when(pl.program_id(0) == 0)
    def _():
        xf[...] = jnp.zeros_like(xf)

    wind = jnp.concatenate([wind_ref[...]] * nblk, axis=1)
    rate = lat_ref[0:1, :]
    weight = lat_ref[1:2, :]

    def body(v, carry):
        xv = x_ref[v]
        x32 = xv.astype(F32)
        xf[0:latd, :] = xv
        xf[LANES : LANES + latd, :] = (x32 * (wind + x32)).astype(BF16)
        both = lax.dot_general(
            t_ref[...], xf[...], (((1,), (1,)), ((), ())), preferred_element_type=F32
        )
        plain, moved = both[:, :LANES], both[:, LANES:]
        factor = wave_ref[...] * rate
        real = (plain[:half] + factor * moved[half:]) * weight
        imag = (plain[half:] - factor * moved[:half]) * weight
        scr[pl.ds(v, half, stride=vb), :] = real
        scr[pl.ds(half * vb + v, half, stride=vb), :] = imag
        return carry

    lax.fori_loop(0, vb, body, 0, unroll=2)
    for g in range(groups):
        for c in range(2):
            start = (c * half + g * per) * vb
            piece = scr[start : start + per * vb, :].reshape(per, vb, LANES)
            outs[g][:, c] = piece[:, :, :latd].astype(BF16)


def dft(x, table, wind, latrow, waves, groups):
    levd, latd, nlon = x.shape
    rows = table.shape[0]
    half = rows // 2
    per = half // groups
    vb = 8
    const = lambda i: (0, 0)
    block = pl.BlockSpec((per, 2, vb, latd), lambda i: (0, 0, i, 0))
    return pl.pallas_call(
        functools.partial(dft_kernel, groups, vb, latd),
        out_shape=[jax.ShapeDtypeStruct((per, 2, levd, latd), BF16)] * groups,
        grid=(levd // vb,),
        in_specs=[
            pl.BlockSpec((vb, latd, nlon), lambda i: (i, 0, 0)),
            pl.BlockSpec((rows, nlon), const),
            pl.BlockSpec((latd, LANES), const),
            pl.BlockSpec((2, LANES), const),
            pl.BlockSpec((half, LANES), const),
        ],
        out_specs=[block] * groups,
        scratch_shapes=[
            pltpu.VMEM((2 * LANES, nlon), BF16),
            pltpu.VMEM((rows * vb, LANES), F32),
        ],
        cost_estimate=pl.CostEstimate(
            flops=4 * rows * levd * latd * nlon,
            bytes_accessed=2 * levd * latd * (nlon + rows) + 2 * rows * nlon,
            transcendentals=0,
        ),
        name="dft",
    )(x, table, wind, latrow, jnp.broadcast_to(waves.astype(F32)[:, None], (half, LANES)))


def split3_dot(w3, x):
    hi = x.astype(BF16)
    lo = (x - hi.astype(F32)).astype(BF16)
    return jnp.dot(w3, jnp.concatenate([hi, lo, hi], axis=0), preferred_element_type=F32)


def legendre_kernel(
    groups, levs, latd, nmodes, info, leg_ref, perm_ref, w1_ref, w2_ref, mr_ref, *rest
):
    own = rest[:groups]
    other = rest[groups]
    outs = rest[groups + 1 : 2 * groups + 1]
    give = rest[2 * groups + 1]
    acc = rest[2 * groups + 2]
    levd = own[0].shape[2]
    nlev = levs * levd
    t = pl.program_id(0)

    @pl.when(t == 0)
    def _():
        acc[...] = jnp.zeros_like(acc)

    for rel in range(groups):
        dz, dx = rel // levs, rel % levs
        lanes = slice(dz * LANES, dz * LANES + latd)
        for c in range(2):
            row = c * 2 * nlev + dx * levd
            acc[row : row + levd, lanes] = own[rel][0, c].astype(F32)
            row += nlev
            acc[row : row + levd, lanes] = other[rel, 0, c].astype(F32)
    data = acc[...].astype(BF16)
    leg = jnp.dot(leg_ref[0], perm_ref[...], preferred_element_type=F32).astype(BF16)
    spec = lax.dot_general(data, leg, (((1,), (1,)), ((), ())), preferred_element_type=F32)
    k = lax.broadcasted_iota(jnp.int32, (1, nmodes), 1)
    wave, count, unknown = info[0, t], info[1, t], info[2, 0]
    n = (wave + k).astype(F32)
    h = n * (n + 1.0) / float(nmodes * (nmodes - 1))
    first = unknown == 0
    scale_own = jnp.where(first, 1.0, h)
    scale_other = jnp.where(first, h, 1.0)
    keep_own = jnp.where(first, 0.0, 1.0)
    keep_other = jnp.where(first, 1.0, 0.0)
    denom = 1.0 + h * mr_ref[...]
    spec = jnp.where(k < count, spec, 0.0)
    fresh = []
    for c in range(2):
        a = spec[c * 2 * nlev : c * 2 * nlev + nlev]
        b = spec[c * 2 * nlev + nlev : (c + 1) * 2 * nlev]
        src = split3_dot(w1_ref[...], jnp.concatenate([a * scale_own, b * scale_other], axis=0))
        q = src / denom
        new = split3_dot(w2_ref[...], q)
        fresh.append(new[:nlev] + keep_own * a)
        fresh.append(new[nlev:] + keep_other * b)
    fresh = jnp.concatenate(fresh, axis=0).astype(BF16)
    back = jnp.dot(fresh, leg, preferred_element_type=F32) * float(nmodes) ** (-0.5)
    for rel in range(groups):
        dz, dx = rel // levs, rel % levs
        lanes = slice(dz * LANES, dz * LANES + latd)
        for c in range(2):
            row = c * 2 * nlev + dx * levd
            outs[rel][0, c] = back[row : row + levd, lanes].astype(BF16)
            row += nlev
            give[rel, 0, c] = back[row : row + levd, lanes].astype(BF16)


def legendre_step(info, leg, first_slot, perm, w1, w2, rates, own, other, levs, nmodes):
    groups = len(own)
    count, _, levd, latd = other.shape[1:]
    nlat, lanes = perm.shape
    nlev = levs * levd
    const = lambda t, s: (0, 0)
    piece = pl.BlockSpec((1, 2, levd, latd), lambda t, s: (t, 0, 0, 0))
    stack = pl.BlockSpec((groups, 1, 2, levd, latd), lambda t, s: (0, t, 0, 0, 0))
    flops = count * 2 * (2 * nlev * 2 * nmodes * lanes * 2 + nmodes * nlat * lanes)
    return pl.pallas_call(
        functools.partial(legendre_kernel, groups, levs, latd, nmodes),
        out_shape=[jax.ShapeDtypeStruct((count, 2, levd, latd), BF16)] * groups
        + [jax.ShapeDtypeStruct((groups, count, 2, levd, latd), BF16)],
        grid_spec=pltpu.PrefetchScalarGridSpec(
            num_scalar_prefetch=1,
            grid=(count,),
            in_specs=[
                pl.BlockSpec((1, nmodes, nlat), lambda t, s: (s[3, 0] + t, 0, 0)),
                pl.BlockSpec((nlat, lanes), const),
                pl.BlockSpec(w1.shape, const),
                pl.BlockSpec(w2.shape, const),
                pl.BlockSpec(rates.shape, const),
            ]
            + [piece] * groups
            + [stack],
            out_specs=[piece] * groups + [stack],
            scratch_shapes=[pltpu.VMEM((4 * nlev, lanes), F32)],
        ),
        cost_estimate=pl.CostEstimate(
            flops=flops,
            bytes_accessed=count * 2 * (nmodes * nlat + 8 * nlev * lanes),
            transcendentals=0,
        ),
        name="legendre",
    )(info, leg, perm, w1, w2, rates, *own, other)


def inverse_kernel(spread, vb, latd, scale, t_ref, *rest):
    ins, rest = rest[: len(spread)], rest[len(spread) :]
    partial = rest[0] if len(rest) == 4 else None
    out, scr, lhs = rest[-3:]
    rows, nlon = t_ref.shape
    half = rows // 2
    for ref, (start, per) in zip(ins, spread):
        for c in range(2):
            at = (c * half + start) * vb
            scr[at : at + per * vb, :latd] = ref[:, c].astype(F32).reshape(per * vb, latd)
    for v in range(vb):
        col = scr[pl.ds(v, rows, stride=vb), :].astype(BF16)
        lhs[v * LANES : (v + 1) * LANES, :] = col.T
    step = 3 * LANES
    for j in range(0, nlon, step):
        cols = slice(j, j + step)
        grid = jnp.dot(lhs[...], t_ref[:, cols], preferred_element_type=F32) * scale
        for v in range(vb):
            piece = grid[v * LANES : v * LANES + latd]
            if partial is not None:
                piece = piece + partial[v, :, cols]
            out[v, :, cols] = piece.astype(out.dtype)


def inverse_dft(table, pieces, spread, partial, scale, out_dtype):
    levd, latd = pieces[0].shape[2:]
    rows, nlon = table.shape
    vb = 8
    grid_block = pl.BlockSpec((vb, latd, nlon), lambda i: (i, 0, 0))
    in_specs = [pl.BlockSpec((rows, nlon), lambda i: (0, 0))] + [
        pl.BlockSpec((p.shape[0], 2, vb, latd), lambda i: (0, 0, i, 0)) for p in pieces
    ]
    args = [table, *pieces]
    if partial is not None:
        in_specs.append(grid_block)
        args.append(partial)
    return pl.pallas_call(
        functools.partial(inverse_kernel, spread, vb, latd, scale),
        out_shape=jax.ShapeDtypeStruct((levd, latd, nlon), out_dtype),
        grid=(levd // vb,),
        in_specs=in_specs,
        out_specs=grid_block,
        scratch_shapes=[
            pltpu.VMEM((rows * vb, LANES), F32),
            pltpu.VMEM((vb * LANES, rows), BF16),
        ],
        cost_estimate=pl.CostEstimate(
            flops=2 * rows * levd * latd * nlon,
            bytes_accessed=2 * levd * latd * (nlon + rows) + 2 * rows * nlon,
            transcendentals=0,
        ),
        name="inverse_dft",
    )(*args)


def local_fast(
    chunks,
    grid_state,
    lat_order,
    slot_wave,
    truncation,
    zonal_wind,
    zonal_rate,
    quad_weight,
    legendre,
    vert_modes,
    vert_project,
    mode_rates,
    thermal_matrix,
    pressure_matrix,
):
    levd, latd, nlon = grid_state.shape[1:]
    slots = legendre.shape[0]
    nmodes = slot_wave.shape[0]
    nlat = lat_order.shape[0]
    nlev = vert_modes.shape[0]
    lats, levs = lax.axis_size("lat"), lax.axis_size("lev")
    groups = lats * levs
    z, x, f = lax.axis_index("lat"), lax.axis_index("lev"), lax.axis_index("fld")
    me = z * levs + x
    part = slots // (2 * chunks)

    waves = slot_wave.reshape(groups, 2, chunks, part)
    waves = xor_order(xor_order(waves, me, 0), f, 1)
    my_lats = lax.dynamic_slice_in_dim(lat_order, z * latd, latd)
    onehot = (my_lats[:, None] == jnp.arange(nlat, dtype=jnp.int32)[None, :]).astype(F32)
    per_lat = jnp.dot(
        onehot,
        jnp.stack([zonal_wind, zonal_rate, quad_weight * nlon ** (-0.5)], axis=1),
        precision=PRECISE,
    )
    wind = jnp.broadcast_to(per_lat[:, 0:1], (latd, LANES))
    latrow = jnp.pad(per_lat[:, 1:].T, ((0, 0), (0, LANES - latd)))

    first = f == 0
    mix = jnp.dot(vert_project, thermal_matrix, precision=PRECISE)
    drop = -jnp.dot(pressure_matrix, vert_modes, precision=PRECISE)
    by_col = lambda m: xor_order(m.reshape(nlev, levs, levd), x, 1).reshape(nlev, nlev)
    by_row = lambda m: xor_order(m.reshape(levs, levd, nlev), x, 0).reshape(nlev, nlev)
    w1 = by_col(jnp.where(first, vert_project, mix)), by_col(jnp.where(first, mix, vert_project))
    w1 = jnp.concatenate(w1, axis=1)
    w2 = by_row(jnp.where(first, vert_modes, drop)), by_row(jnp.where(first, drop, vert_modes))
    w2 = jnp.concatenate(w2, axis=0)

    def three(w):
        hi = lax.reduce_precision(w, 8, 7)
        lo = (w - hi).astype(BF16)
        hi = hi.astype(BF16)
        return jnp.concatenate([hi, hi, lo], axis=1)

    w1, w2 = three(w1), three(w2)
    rates = mode_rates[:, None]
    lat_rel = xor_order(lat_order.reshape(lats, latd), z, 0)
    lat_rel = jnp.pad(lat_rel, ((0, 0), (0, LANES - latd)), constant_values=-1).reshape(1, -1)
    perm = (jnp.arange(nlat, dtype=jnp.int32)[:, None] == lat_rel).astype(BF16)
    my_waves = waves[0, 0]
    limits = pick_values(my_waves.reshape(-1), truncation).reshape(chunks, part)
    counts = limits - my_waves + 1

    lat_lev = ("lat", "lev")

    def exchange(blocks):
        return [
            b if r == 0 else lax.ppermute(b, lat_lev, [(i, i ^ r) for i in range(groups)])
            for r, b in enumerate(blocks)
        ]

    def swap(block):
        return lax.ppermute(block, "fld", [(0, 1), (1, 0)])

    tables, arrived = [], []
    for i in range(chunks):
        w = waves[:, :, i].reshape(-1)
        table = make_table(w, nlon)
        tables.append(table)
        arrived.append(exchange(dft(grid_state[0], table, wind, latrow, w, groups)))
    returned = []
    for i in range(chunks):
        mine = arrived[i]
        other = swap(jnp.stack([a[part:] for a in mine]))
        start = f * (slots // 2) + i * part
        info = jnp.stack(
            [
                my_waves[i],
                counts[i],
                jnp.full((part,), f, jnp.int32),
                jnp.full((part,), start, jnp.int32),
            ]
        )
        res = legendre_step(
            info, legendre, start, perm, w1, w2, rates, mine, other, levs, nmodes
        )
        outs, give = res[:groups], res[groups]
        got = swap(give)
        sent = [jnp.concatenate([outs[r], got[r]], axis=0) for r in range(groups)]
        returned.append(exchange(sent))
    total = None
    for i in range(chunks):
        spread = tuple((r * 2 * part, 2 * part) for r in range(groups))
        last = i == chunks - 1
        total = inverse_dft(
            tables[i],
            returned[i],
            spread,
            total,
            float(nmodes) ** (-0.5),
            BF16 if last else F32,
        )
    return total[None]


def power_of_two(n):
    return n & (n - 1) == 0


def solution(mesh):
    in_specs = (
        P(("member", "fld"), "lev", "lat", None),
        P(),
        P(),
        P(),
        P(),
        P(),
        P(),
        P(("lat", "lev"), None, None),
        P(),
        P(),
        P(),
        P(),
        P(),
    )
    out_specs = P(("member", "fld"), "lev", "lat", None)
    lats, levs = mesh.shape["lat"], mesh.shape["lev"]

    def local(grid_state, *rest):
        legendre = rest[6]
        levd, latd, nlon = grid_state.shape[1:]
        chunks = 2
        fits = (
            mesh.shape["fld"] == 2
            and power_of_two(lats)
            and power_of_two(levs)
            and 1 < lats * levs <= 8
            and legendre.shape[0] % (2 * chunks) == 0
            and levd % 8 == 0
            and latd % 8 == 0
            and latd <= LANES
            and nlon % (3 * LANES) == 0
        )
        if fits:
            return local_fast(chunks, grid_state, *rest)
        return local_general(grid_state, *rest)

    return jax.shard_map(local, mesh=mesh, in_specs=in_specs, out_specs=out_specs, check_vma=False)
```

```python
import functools

import jax
import jax.numpy as jnp
from jax import lax
from jax.experimental import pallas as pl
from jax.experimental.pallas import tpu as pltpu
from jax.sharding import PartitionSpec as P


PRECISE = lax.Precision.HIGHEST
BF16 = jnp.bfloat16
F32 = jnp.float32


def dft_table(wavenums, nlon):
    columns = jnp.arange(nlon, dtype=jnp.int32)
    turns = columns[:, None] * wavenums[None, :] % nlon
    angles = turns.astype(jnp.float32) * (2.0 * jnp.pi / nlon)
    return jnp.stack([jnp.cos(angles), -jnp.sin(angles)], axis=1).astype(jnp.bfloat16)


def pick_values(idents, source_table):
    hits = idents[:, None] == jnp.arange(source_table.shape[0], dtype=jnp.int32)[None, :]
    return jnp.sum(jnp.where(hits, source_table[None, :], 0), axis=1)


def layer_eigen_basis(matrix, columns):
    return jnp.einsum("skcj,ij->skci", columns, matrix, precision=PRECISE)


def analyse(legendre, fourier_data):
    return jnp.einsum("skl,slx->skx", legendre, fourier_data, preferred_element_type=jnp.float32)


def synthesise(legendre, coeffs):
    return jnp.einsum("skl,skx->slx", legendre, coeffs, preferred_element_type=jnp.float32)


def local_general(
    grid_state,
    lat_order,
    slot_wave,
    truncation,
    zonal_wind,
    zonal_rate,
    quad_weight,
    legendre,
    vert_modes,
    vert_project,
    mode_rates,
    thermal_into_spread_matrix,
    pressure_balance_matrix,
):
    levd, latd, nlon = (grid_state.shape[1], grid_state.shape[2], grid_state.shape[3])
    slots = legendre.shape[0]
    nmodes = slot_wave.shape[0]
    nlat = lat_order.shape[0]
    nlev = vert_modes.shape[0]
    lat_count = lax.axis_size("lat")
    lev_count = lax.axis_size("lev")
    lat_index = lax.axis_index("lat")
    lev_index = lax.axis_index("lev")
    unknown_position = lax.axis_index("fld")
    my_lats = lax.dynamic_slice_in_dim(lat_order, lat_index * latd, latd)
    onehot = (my_lats[:, None] == jnp.arange(nlat, dtype=jnp.int32)[None, :]).astype(jnp.float32)
    per_lat = jnp.dot(
        onehot, jnp.stack([zonal_wind, zonal_rate, quad_weight], axis=1), precision=PRECISE
    )
    values = grid_state[0].astype(jnp.float32)
    flux = (values * (per_lat[None, :, 0][:, :, None] + values)).astype(jnp.bfloat16)
    count_rows = levd * latd
    stacked = jnp.concatenate(
        [grid_state[0].reshape(count_rows, nlon), flux.reshape(count_rows, nlon)], axis=0
    )
    table = dft_table(slot_wave, nlon).reshape(nlon, 2 * nmodes)
    spectra = lax.dot_general(
        table, stacked, (((0,), (1,)), ((), ())), preferred_element_type=jnp.float32
    ) * nlon ** (-0.5)
    spectra = spectra.reshape(2, nmodes, 2 * count_rows)
    plain = spectra[:, :, :count_rows]
    moved = spectra[:, :, count_rows:]
    rate_row = jnp.tile(per_lat[:, 1], levd)[None, :]
    weight_row = jnp.tile(per_lat[:, 2], levd)[None, :]
    wave_float = slot_wave.astype(jnp.float32)[:, None]
    factor = rate_row * wave_float
    real_part = (plain[0] + factor * moved[1]) * weight_row
    imag_part = (plain[1] - factor * moved[0]) * weight_row
    fourier = jnp.stack([real_part, imag_part], axis=0).astype(jnp.bfloat16)
    arrived = lax.all_to_all(fourier, ("lat", "lev"), split_axis=1, concat_axis=2, tiled=True)
    arrived = arrived.reshape(2, slots, lat_count, lev_count, levd, latd)
    arranged = jnp.transpose(arrived, (1, 2, 5, 0, 3, 4))
    arranged = arranged.reshape(slots, nlat, 2 * nlev)
    position = jnp.zeros((nlat,), jnp.int32).at[lat_order].set(jnp.arange(nlat, dtype=jnp.int32))
    ordered = jnp.take(arranged, position, axis=1)
    owner_index = lat_index * lev_count + lev_index
    my_waves = lax.dynamic_slice_in_dim(slot_wave, owner_index * slots, slots)
    limits = pick_values(my_waves, truncation)
    counts = limits - my_waves + 1
    degree = jnp.arange(nmodes, dtype=jnp.int32)
    valid = (degree[None, :] < counts[:, None])[:, :, None]
    own_spec = jnp.where(valid, analyse(legendre, ordered), jnp.float32(0.0))
    joined_harmonic_unknowns = lax.all_gather(own_spec, "fld", axis=2, tiled=True)
    joined_harmonic_unknowns = joined_harmonic_unknowns.reshape(slots, nmodes, 2, 2, nlev)
    outflow_rate_coeffs = joined_harmonic_unknowns[:, :, 0]
    thermal_coeffs = joined_harmonic_unknowns[:, :, 1]
    n_deg = (my_waves[:, None] + degree[None, :]).astype(jnp.float32)
    elliptic_inverse_scale = (n_deg * (n_deg + 1.0) / (nmodes * (nmodes - 1)))[:, :, None, None]
    outflow_rate_source = outflow_rate_coeffs + elliptic_inverse_scale * layer_eigen_basis(
        thermal_into_spread_matrix, thermal_coeffs
    )
    projected = layer_eigen_basis(vert_project, outflow_rate_source) / (
        1.0 + elliptic_inverse_scale * mode_rates
    )
    outflow_rate_next = layer_eigen_basis(vert_modes, projected)
    thermal_next = thermal_coeffs - layer_eigen_basis(pressure_balance_matrix, outflow_rate_next)
    own_new = (
        jnp.where(unknown_position == 0, outflow_rate_next, thermal_next)
        .astype(jnp.bfloat16)
        .reshape(slots, nmodes, 2 * nlev)
    )
    back = synthesise(legendre, own_new) * nmodes ** (-0.5)
    back = jnp.take(back, lat_order, axis=1).astype(jnp.bfloat16)
    shaped = back.reshape(slots, lat_count, latd, 2, lev_count, levd)
    outgoing = jnp.transpose(shaped, (3, 0, 1, 4, 5, 2)).reshape(
        2, slots, lat_count * lev_count * count_rows
    )
    returned = lax.all_to_all(outgoing, ("lat", "lev"), split_axis=2, concat_axis=1, tiled=True)
    leading = returned.reshape(2 * nmodes, count_rows)
    grid_out = lax.dot_general(
        leading, table, (((0,), (1,)), ((), ())), preferred_element_type=jnp.float32
    ) * nmodes ** (-0.5)
    return grid_out.astype(jnp.bfloat16).reshape(1, levd, latd, nlon)


LANES = 128
SHARES = (1, 1)


def xor_order(array, index, axis):
    size = array.shape[axis]
    bits = size.bit_length() - 1
    shape = array.shape[:axis] + (2,) * bits + array.shape[axis + 1 :]
    out = array.reshape(shape)
    for b in range(bits):
        ax = axis + bits - 1 - b
        out = jnp.where((index >> b) & 1 == 1, jnp.flip(out, ax), out)
    return out.reshape(array.shape)


def table_kernel(nblk, hi_c, hi_s, lo_c, lo_s, out):
    rows = hi_c.shape[0]
    cl, sl = lo_c[...], lo_s[...]
    for b in range(nblk):
        ch, sh = hi_c[:, b : b + 1], hi_s[:, b : b + 1]
        cols = slice(b * LANES, (b + 1) * LANES)
        out[:rows, cols] = (ch * cl - sh * sl).astype(BF16)
        out[rows:, cols] = (-(sh * cl + ch * sl)).astype(BF16)


def make_table(waves, nlon):
    nblk = nlon // LANES
    scale = 2.0 * jnp.pi / nlon
    step_lo = jnp.arange(LANES, dtype=jnp.int32)
    step_hi = jnp.arange(LANES, dtype=jnp.int32) * LANES
    lo = (waves[:, None] * step_lo[None, :] % nlon).astype(F32) * scale
    hi = (waves[:, None] * step_hi[None, :] % nlon).astype(F32) * scale
    rows = waves.shape[0]
    return pl.pallas_call(
        functools.partial(table_kernel, nblk),
        out_shape=jax.ShapeDtypeStruct((2 * rows, nlon), BF16),
        name="table",
    )(jnp.cos(hi), jnp.sin(hi), jnp.cos(lo), jnp.sin(lo))


def dft_kernel(groups, vb, latd, x_ref, t_ref, wind_ref, lat_ref, wave_ref, *rest):
    outs, (xf, scr) = rest[:groups], rest[groups:]
    rows = t_ref.shape[0]
    half = rows // 2
    per = half // groups
    nblk = x_ref.shape[2] // LANES

    @pl.when(pl.program_id(0) == 0)
    def _():
        xf[...] = jnp.zeros_like(xf)

    wind = jnp.concatenate([wind_ref[...]] * nblk, axis=1)
    rate = lat_ref[0:1, :]
    weight = lat_ref[1:2, :]

    def body(v, carry):
        xv = x_ref[v]
        x32 = xv.astype(F32)
        xf[0:latd, :] = xv
        xf[LANES : LANES + latd, :] = (x32 * (wind + x32)).astype(BF16)
        both = lax.dot_general(
            t_ref[...], xf[...], (((1,), (1,)), ((), ())), preferred_element_type=F32
        )
        plain, moved = both[:, :LANES], both[:, LANES:]
        factor = wave_ref[...] * rate
        real = (plain[:half] + factor * moved[half:]) * weight
        imag = (plain[half:] - factor * moved[:half]) * weight
        scr[pl.ds(v, half, stride=vb), :] = real
        scr[pl.ds(half * vb + v, half, stride=vb), :] = imag
        return carry

    lax.fori_loop(0, vb, body, 0, unroll=2)
    for g in range(groups):
        for c in range(2):
            start = (c * half + g * per) * vb
            piece = scr[start : start + per * vb, :].reshape(per, vb, LANES)
            outs[g][:, c] = piece[:, :, :latd].astype(BF16)


def dft(x, table, wind, latrow, waves, groups):
    levd, latd, nlon = x.shape
    rows = table.shape[0]
    half = rows // 2
    per = half // groups
    vb = 8
    const = lambda i: (0, 0)
    block = pl.BlockSpec((per, 2, vb, latd), lambda i: (0, 0, i, 0))
    return pl.pallas_call(
        functools.partial(dft_kernel, groups, vb, latd),
        out_shape=[jax.ShapeDtypeStruct((per, 2, levd, latd), BF16)] * groups,
        grid=(levd // vb,),
        in_specs=[
            pl.BlockSpec((vb, latd, nlon), lambda i: (i, 0, 0)),
            pl.BlockSpec((rows, nlon), const),
            pl.BlockSpec((latd, LANES), const),
            pl.BlockSpec((2, LANES), const),
            pl.BlockSpec((half, LANES), const),
        ],
        out_specs=[block] * groups,
        scratch_shapes=[
            pltpu.VMEM((2 * LANES, nlon), BF16),
            pltpu.VMEM((rows * vb, LANES), F32),
        ],
        cost_estimate=pl.CostEstimate(
            flops=4 * rows * levd * latd * nlon,
            bytes_accessed=2 * levd * latd * (nlon + rows) + 2 * rows * nlon,
            transcendentals=0,
        ),
        name="dft",
    )(x, table, wind, latrow, jnp.broadcast_to(waves.astype(F32)[:, None], (half, LANES)))


def split3_dot(w3, x):
    hi = x.astype(BF16)
    lo = (x - hi.astype(F32)).astype(BF16)
    return jnp.dot(w3, jnp.concatenate([hi, lo, hi], axis=0), preferred_element_type=F32)


def legendre_kernel(
    groups, levs, latd, nmodes, info, leg_ref, perm_ref, w1_ref, w2_ref, mr_ref, *rest
):
    own = rest[:groups]
    other = rest[groups]
    outs = rest[groups + 1 : 2 * groups + 1]
    give = rest[2 * groups + 1]
    acc = rest[2 * groups + 2]
    levd = own[0].shape[2]
    nlev = levs * levd
    t = pl.program_id(0)

    @pl.when(t == 0)
    def _():
        acc[...] = jnp.zeros_like(acc)

    for rel in range(groups):
        dz, dx = rel // levs, rel % levs
        lanes = slice(dz * LANES, dz * LANES + latd)
        for c in range(2):
            row = c * 2 * nlev + dx * levd
            acc[row : row + levd, lanes] = own[rel][0, c].astype(F32)
            row += nlev
            acc[row : row + levd, lanes] = other[rel, 0, c].astype(F32)
    data = acc[...].astype(BF16)
    leg = jnp.dot(perm_ref[...], leg_ref[0], preferred_element_type=F32).astype(BF16)
    spec = jnp.dot(data, leg, preferred_element_type=F32)
    k = lax.broadcasted_iota(jnp.int32, (1, nmodes), 1)
    wave, count, unknown = info[0, t], info[1, t], info[2, 0]
    n = (wave + k).astype(F32)
    h = n * (n + 1.0) / float(nmodes * (nmodes - 1))
    first = unknown == 0
    scale_own = jnp.where(first, 1.0, h)
    scale_other = jnp.where(first, h, 1.0)
    keep_own = jnp.where(first, 0.0, 1.0)
    keep_other = jnp.where(first, 1.0, 0.0)
    denom = 1.0 + h * mr_ref[...]
    spec = jnp.where(k < count, spec, 0.0)
    fresh = []
    for c in range(2):
        a = spec[c * 2 * nlev : c * 2 * nlev + nlev]
        b = spec[c * 2 * nlev + nlev : (c + 1) * 2 * nlev]
        src = split3_dot(w1_ref[...], jnp.concatenate([a * scale_own, b * scale_other], axis=0))
        q = src / denom
        new = split3_dot(w2_ref[...], q)
        fresh.append(new[:nlev] + keep_own * a)
        fresh.append(new[nlev:] + keep_other * b)
    fresh = jnp.concatenate(fresh, axis=0).astype(BF16)
    back = lax.dot_general(fresh, leg, (((1,), (1,)), ((), ())), preferred_element_type=F32)
    back = back * float(nmodes) ** (-0.5)
    for rel in range(groups):
        dz, dx = rel // levs, rel % levs
        lanes = slice(dz * LANES, dz * LANES + latd)
        for c in range(2):
            row = c * 2 * nlev + dx * levd
            outs[rel][0, c] = back[row : row + levd, lanes].astype(BF16)
            row += nlev
            give[rel, 0, c] = back[row : row + levd, lanes].astype(BF16)


def legendre_step(info, leg, perm, w1, w2, rates, own, other, levs, nmodes):
    groups = len(own)
    count, _, levd, latd = other.shape[1:]
    lanes, nlat = perm.shape
    nlev = levs * levd
    const = lambda t, s: (0, 0)
    piece = pl.BlockSpec((1, 2, levd, latd), lambda t, s: (t, 0, 0, 0))
    stack = pl.BlockSpec((groups, 1, 2, levd, latd), lambda t, s: (0, t, 0, 0, 0))
    flops = count * 2 * (2 * nlev * 2 * nmodes * lanes * 2 + nmodes * nlat * lanes)
    return pl.pallas_call(
        functools.partial(legendre_kernel, groups, levs, latd, nmodes),
        out_shape=[jax.ShapeDtypeStruct((2 * count, 2, levd, latd), BF16)] * groups
        + [jax.ShapeDtypeStruct((groups, count, 2, levd, latd), BF16)],
        grid_spec=pltpu.PrefetchScalarGridSpec(
            num_scalar_prefetch=1,
            grid=(count,),
            in_specs=[
                pl.BlockSpec((1, nlat, nmodes), lambda t, s: (s[3, 0] + t, 0, 0)),
                pl.BlockSpec((lanes, nlat), const),
                pl.BlockSpec(w1.shape, const),
                pl.BlockSpec(w2.shape, const),
                pl.BlockSpec(rates.shape, const),
            ]
            + [piece] * groups
            + [stack],
            out_specs=[piece] * groups + [stack],
            scratch_shapes=[pltpu.VMEM((4 * nlev, lanes), F32)],
        ),
        cost_estimate=pl.CostEstimate(
            flops=flops,
            bytes_accessed=count * 2 * (nmodes * nlat + 8 * nlev * lanes),
            transcendentals=0,
        ),
        name="legendre",
    )(info, leg, perm, w1, w2, rates, *own, other)


def gather_kernel(groups, *refs):
    ins, out = refs[:groups], refs[-1]
    for r in range(groups):
        out[r] = ins[r][...]


def gather_halves(blocks, after):
    groups = len(blocks)
    count, _, levd, latd = blocks[0].shape
    half = count // 2
    any_spec = pl.BlockSpec(memory_space=pl.ANY)
    return pl.pallas_call(
        functools.partial(gather_kernel, groups),
        out_shape=jax.ShapeDtypeStruct((groups, half, 2, levd, latd), BF16),
        grid=(1,),
        in_specs=[pl.BlockSpec((half, 2, levd, latd), lambda i: (1, 0, 0, 0))] * groups
        + [any_spec] * len(after),
        out_specs=pl.BlockSpec((groups, half, 2, levd, latd), lambda i: (0, 0, 0, 0, 0)),
        name="gather_halves",
    )(*blocks, *after)


def fill_kernel(groups, got, *refs):
    outs = refs[-groups:]
    for r in range(groups):
        outs[r][...] = got[r]


def fill_halves(blocks, got):
    groups, half, _, levd, latd = got.shape
    any_spec = pl.BlockSpec(memory_space=pl.ANY)
    return pl.pallas_call(
        functools.partial(fill_kernel, groups),
        out_shape=[jax.ShapeDtypeStruct(b.shape, b.dtype) for b in blocks],
        grid=(1,),
        in_specs=[pl.BlockSpec(got.shape, lambda i: (0, 0, 0, 0, 0))] + [any_spec] * groups,
        out_specs=[pl.BlockSpec((half, 2, levd, latd), lambda i: (1, 0, 0, 0))] * groups,
        input_output_aliases={r + 1: r for r in range(groups)},
        name="fill_halves",
    )(got, *blocks)


def inverse_kernel(spread, vb, latd, scale, add, t_ref, *rest):
    ins, rest = rest[: len(spread)], rest[len(spread) :]
    partial = rest[0] if add else None
    out, scr, lhs = rest[-3:]
    rows, nlon = t_ref.shape
    half = rows // 2
    for ref, (start, per) in zip(ins, spread):
        for c in range(2):
            at = (c * half + start) * vb
            scr[at : at + per * vb, :latd] = ref[:, c].astype(F32).reshape(per * vb, latd)
    for v in range(vb):
        col = scr[pl.ds(v, rows, stride=vb), :].astype(BF16)
        lhs[v * LANES : (v + 1) * LANES, :] = col.T
    step = 3 * LANES
    for j in range(0, nlon, step):
        cols = slice(j, j + step)
        grid = jnp.dot(lhs[...], t_ref[:, cols], preferred_element_type=F32) * scale
        for v in range(vb):
            piece = grid[v * LANES : v * LANES + latd]
            if partial is not None:
                piece = piece + partial[v, :, cols]
            out[v, :, cols] = piece.astype(out.dtype)


def inverse_dft(table, pieces, spread, partial, scale, out_dtype, after):
    levd, latd = pieces[0].shape[2:]
    rows, nlon = table.shape
    vb = 8
    grid_block = pl.BlockSpec((vb, latd, nlon), lambda i: (i, 0, 0))
    in_specs = [pl.BlockSpec((rows, nlon), lambda i: (0, 0))] + [
        pl.BlockSpec((p.shape[0], 2, vb, latd), lambda i: (0, 0, i, 0)) for p in pieces
    ]
    args = [table, *pieces]
    if partial is not None:
        in_specs.append(grid_block)
        args.append(partial)
    in_specs += [pl.BlockSpec(memory_space=pl.ANY)] * len(after)
    args += after
    return pl.pallas_call(
        functools.partial(inverse_kernel, spread, vb, latd, scale, partial is not None),
        out_shape=jax.ShapeDtypeStruct((levd, latd, nlon), out_dtype),
        grid=(levd // vb,),
        in_specs=in_specs,
        out_specs=grid_block,
        scratch_shapes=[
            pltpu.VMEM((rows * vb, LANES), F32),
            pltpu.VMEM((vb * LANES, rows), BF16),
        ],
        cost_estimate=pl.CostEstimate(
            flops=2 * rows * levd * latd * nlon,
            bytes_accessed=2 * levd * latd * (nlon + rows) + 2 * rows * nlon,
            transcendentals=0,
        ),
        name="inverse_dft",
    )(*args)


def local_fast(
    parts,
    grid_state,
    lat_order,
    slot_wave,
    truncation,
    zonal_wind,
    zonal_rate,
    quad_weight,
    legendre,
    vert_modes,
    vert_project,
    mode_rates,
    thermal_matrix,
    pressure_matrix,
):
    levd, latd, nlon = grid_state.shape[1:]
    slots = legendre.shape[0]
    nmodes = slot_wave.shape[0]
    nlat = lat_order.shape[0]
    nlev = vert_modes.shape[0]
    lats, levs = lax.axis_size("lat"), lax.axis_size("lev")
    groups = lats * levs
    z, x, f = lax.axis_index("lat"), lax.axis_index("lev"), lax.axis_index("fld")
    me = z * levs + x
    starts = [sum(parts[:i]) for i in range(len(parts))]

    waves = slot_wave.reshape(groups, 2, slots // 2)
    waves = xor_order(xor_order(waves, me, 0), f, 1)
    my_lats = lax.dynamic_slice_in_dim(lat_order, z * latd, latd)
    onehot = (my_lats[:, None] == jnp.arange(nlat, dtype=jnp.int32)[None, :]).astype(F32)
    per_lat = jnp.dot(
        onehot,
        jnp.stack([zonal_wind, zonal_rate, quad_weight * nlon ** (-0.5)], axis=1),
        precision=PRECISE,
    )
    wind = jnp.broadcast_to(per_lat[:, 0:1], (latd, LANES))
    latrow = jnp.pad(per_lat[:, 1:].T, ((0, 0), (0, LANES - latd)))

    first = f == 0
    mix = jnp.dot(vert_project, thermal_matrix, precision=PRECISE)
    drop = -jnp.dot(pressure_matrix, vert_modes, precision=PRECISE)
    by_col = lambda m: xor_order(m.reshape(nlev, levs, levd), x, 1).reshape(nlev, nlev)
    by_row = lambda m: xor_order(m.reshape(levs, levd, nlev), x, 0).reshape(nlev, nlev)
    w1 = by_col(jnp.where(first, vert_project, mix)), by_col(jnp.where(first, mix, vert_project))
    w1 = jnp.concatenate(w1, axis=1)
    w2 = by_row(jnp.where(first, vert_modes, drop)), by_row(jnp.where(first, drop, vert_modes))
    w2 = jnp.concatenate(w2, axis=0)

    def three(w):
        hi = lax.reduce_precision(w, 8, 7)
        lo = (w - hi).astype(BF16)
        hi = hi.astype(BF16)
        return jnp.concatenate([hi, hi, lo], axis=1)

    w1, w2 = three(w1), three(w2)
    rates = mode_rates[:, None]
    lat_rel = xor_order(lat_order.reshape(lats, latd), z, 0)
    lat_rel = jnp.pad(lat_rel, ((0, 0), (0, LANES - latd)), constant_values=-1).reshape(-1, 1)
    perm = (lat_rel == jnp.arange(nlat, dtype=jnp.int32)[None, :]).astype(BF16)
    my_waves = waves[0, 0]
    counts = pick_values(my_waves, truncation) - my_waves + 1

    lat_lev = ("lat", "lev")

    def exchange(blocks):
        return [
            b if r == 0 else lax.ppermute(b, lat_lev, [(i, i ^ r) for i in range(groups)])
            for r, b in enumerate(blocks)
        ]

    def swap(block):
        return lax.ppermute(block, "fld", [(0, 1), (1, 0)])

    tables, arrived = [], []
    for i, (at, part) in enumerate(zip(starts, parts)):
        w = waves[:, :, at : at + part].reshape(-1)
        tables.append(make_table(w, nlon))
        blocks = dft(grid_state[0], tables[i], wind, latrow, w, groups)
        arrived.append(exchange(blocks))
    legendre = jnp.swapaxes(legendre, 1, 2)
    returned = []
    after = [arrived[-1][0]]
    for i, (at, part) in enumerate(zip(starts, parts)):
        other = gather_halves(arrived[i], after)
        other = swap(other)
        info = jnp.stack(
            [
                my_waves[at : at + part],
                counts[at : at + part],
                jnp.full((part,), f, jnp.int32),
                jnp.full((part,), f * (slots // 2) + at, jnp.int32),
            ]
        )
        res = legendre_step(info, legendre, perm, w1, w2, rates, arrived[i], other, levs, nmodes)
        got = swap(res[groups])
        sent = fill_halves(res[:groups], got)
        after = [sent[0]]
        returned.append(exchange(sent))
    total = None
    for i, part in enumerate(parts):
        spread = tuple((r * 2 * part, 2 * part) for r in range(groups))
        last = i == len(parts) - 1
        total = inverse_dft(
            tables[i],
            returned[i],
            spread,
            total,
            float(nmodes) ** (-0.5),
            BF16 if last else F32,
            [] if last else after,
        )
    return total[None]


def power_of_two(n):
    return n & (n - 1) == 0


def solution(mesh):
    in_specs = (
        P(("member", "fld"), "lev", "lat", None),
        P(),
        P(),
        P(),
        P(),
        P(),
        P(),
        P(("lat", "lev"), None, None),
        P(),
        P(),
        P(),
        P(),
        P(),
    )
    out_specs = P(("member", "fld"), "lev", "lat", None)
    lats, levs = mesh.shape["lat"], mesh.shape["lev"]

    groups = lats * levs
    small = (
        mesh.shape["fld"] == 2 and power_of_two(lats) and power_of_two(levs) and 1 < groups <= 8
    )

    def local(grid_state, *rest):
        legendre = rest[6]
        levd, latd, nlon = grid_state.shape[1:]
        fits = (
            legendre.shape[0] % (2 * sum(SHARES)) == 0
            and levd % 8 == 0
            and latd % 8 == 0
            and latd <= LANES
            and nlon % (3 * LANES) == 0
        )
        if small and fits:
            unit = legendre.shape[0] // (2 * sum(SHARES))
            return local_fast([unit * n for n in SHARES], grid_state, *rest)
        return local_general(grid_state, *rest)

    return jax.shard_map(local, mesh=mesh, in_specs=in_specs, out_specs=out_specs, check_vma=False)
```

```python
import functools

import jax
import jax.numpy as jnp
from jax import lax
from jax.experimental import pallas as pl
from jax.experimental.pallas import tpu as pltpu
from jax.sharding import PartitionSpec as P


PRECISE = lax.Precision.HIGHEST
BF16 = jnp.bfloat16
F32 = jnp.float32


def dft_table(wavenums, nlon):
    columns = jnp.arange(nlon, dtype=jnp.int32)
    turns = columns[:, None] * wavenums[None, :] % nlon
    angles = turns.astype(jnp.float32) * (2.0 * jnp.pi / nlon)
    return jnp.stack([jnp.cos(angles), -jnp.sin(angles)], axis=1).astype(jnp.bfloat16)


def pick_values(idents, source_table):
    hits = idents[:, None] == jnp.arange(source_table.shape[0], dtype=jnp.int32)[None, :]
    return jnp.sum(jnp.where(hits, source_table[None, :], 0), axis=1)


def layer_eigen_basis(matrix, columns):
    return jnp.einsum("skcj,ij->skci", columns, matrix, precision=PRECISE)


def analyse(legendre, fourier_data):
    return jnp.einsum("skl,slx->skx", legendre, fourier_data, preferred_element_type=jnp.float32)


def synthesise(legendre, coeffs):
    return jnp.einsum("skl,skx->slx", legendre, coeffs, preferred_element_type=jnp.float32)


def local_general(
    grid_state,
    lat_order,
    slot_wave,
    truncation,
    zonal_wind,
    zonal_rate,
    quad_weight,
    legendre,
    vert_modes,
    vert_project,
    mode_rates,
    thermal_into_spread_matrix,
    pressure_balance_matrix,
):
    levd, latd, nlon = (grid_state.shape[1], grid_state.shape[2], grid_state.shape[3])
    slots = legendre.shape[0]
    nmodes = slot_wave.shape[0]
    nlat = lat_order.shape[0]
    nlev = vert_modes.shape[0]
    lat_count = lax.axis_size("lat")
    lev_count = lax.axis_size("lev")
    lat_index = lax.axis_index("lat")
    lev_index = lax.axis_index("lev")
    unknown_position = lax.axis_index("fld")
    my_lats = lax.dynamic_slice_in_dim(lat_order, lat_index * latd, latd)
    onehot = (my_lats[:, None] == jnp.arange(nlat, dtype=jnp.int32)[None, :]).astype(jnp.float32)
    per_lat = jnp.dot(
        onehot, jnp.stack([zonal_wind, zonal_rate, quad_weight], axis=1), precision=PRECISE
    )
    values = grid_state[0].astype(jnp.float32)
    flux = (values * (per_lat[None, :, 0][:, :, None] + values)).astype(jnp.bfloat16)
    count_rows = levd * latd
    stacked = jnp.concatenate(
        [grid_state[0].reshape(count_rows, nlon), flux.reshape(count_rows, nlon)], axis=0
    )
    table = dft_table(slot_wave, nlon).reshape(nlon, 2 * nmodes)
    spectra = lax.dot_general(
        table, stacked, (((0,), (1,)), ((), ())), preferred_element_type=jnp.float32
    ) * nlon ** (-0.5)
    spectra = spectra.reshape(2, nmodes, 2 * count_rows)
    plain = spectra[:, :, :count_rows]
    moved = spectra[:, :, count_rows:]
    rate_row = jnp.tile(per_lat[:, 1], levd)[None, :]
    weight_row = jnp.tile(per_lat[:, 2], levd)[None, :]
    wave_float = slot_wave.astype(jnp.float32)[:, None]
    factor = rate_row * wave_float
    real_part = (plain[0] + factor * moved[1]) * weight_row
    imag_part = (plain[1] - factor * moved[0]) * weight_row
    fourier = jnp.stack([real_part, imag_part], axis=0).astype(jnp.bfloat16)
    arrived = lax.all_to_all(fourier, ("lat", "lev"), split_axis=1, concat_axis=2, tiled=True)
    arrived = arrived.reshape(2, slots, lat_count, lev_count, levd, latd)
    arranged = jnp.transpose(arrived, (1, 2, 5, 0, 3, 4))
    arranged = arranged.reshape(slots, nlat, 2 * nlev)
    position = jnp.zeros((nlat,), jnp.int32).at[lat_order].set(jnp.arange(nlat, dtype=jnp.int32))
    ordered = jnp.take(arranged, position, axis=1)
    owner_index = lat_index * lev_count + lev_index
    my_waves = lax.dynamic_slice_in_dim(slot_wave, owner_index * slots, slots)
    limits = pick_values(my_waves, truncation)
    counts = limits - my_waves + 1
    degree = jnp.arange(nmodes, dtype=jnp.int32)
    valid = (degree[None, :] < counts[:, None])[:, :, None]
    own_spec = jnp.where(valid, analyse(legendre, ordered), jnp.float32(0.0))
    joined_harmonic_unknowns = lax.all_gather(own_spec, "fld", axis=2, tiled=True)
    joined_harmonic_unknowns = joined_harmonic_unknowns.reshape(slots, nmodes, 2, 2, nlev)
    outflow_rate_coeffs = joined_harmonic_unknowns[:, :, 0]
    thermal_coeffs = joined_harmonic_unknowns[:, :, 1]
    n_deg = (my_waves[:, None] + degree[None, :]).astype(jnp.float32)
    elliptic_inverse_scale = (n_deg * (n_deg + 1.0) / (nmodes * (nmodes - 1)))[:, :, None, None]
    outflow_rate_source = outflow_rate_coeffs + elliptic_inverse_scale * layer_eigen_basis(
        thermal_into_spread_matrix, thermal_coeffs
    )
    projected = layer_eigen_basis(vert_project, outflow_rate_source) / (
        1.0 + elliptic_inverse_scale * mode_rates
    )
    outflow_rate_next = layer_eigen_basis(vert_modes, projected)
    thermal_next = thermal_coeffs - layer_eigen_basis(pressure_balance_matrix, outflow_rate_next)
    own_new = (
        jnp.where(unknown_position == 0, outflow_rate_next, thermal_next)
        .astype(jnp.bfloat16)
        .reshape(slots, nmodes, 2 * nlev)
    )
    back = synthesise(legendre, own_new) * nmodes ** (-0.5)
    back = jnp.take(back, lat_order, axis=1).astype(jnp.bfloat16)
    shaped = back.reshape(slots, lat_count, latd, 2, lev_count, levd)
    outgoing = jnp.transpose(shaped, (3, 0, 1, 4, 5, 2)).reshape(
        2, slots, lat_count * lev_count * count_rows
    )
    returned = lax.all_to_all(outgoing, ("lat", "lev"), split_axis=2, concat_axis=1, tiled=True)
    leading = returned.reshape(2 * nmodes, count_rows)
    grid_out = lax.dot_general(
        leading, table, (((0,), (1,)), ((), ())), preferred_element_type=jnp.float32
    ) * nmodes ** (-0.5)
    return grid_out.astype(jnp.bfloat16).reshape(1, levd, latd, nlon)


LANES = 128
SHARES = (1, 1)


def xor_order(array, index, axis):
    size = array.shape[axis]
    bits = size.bit_length() - 1
    shape = array.shape[:axis] + (2,) * bits + array.shape[axis + 1 :]
    out = array.reshape(shape)
    for b in range(bits):
        ax = axis + bits - 1 - b
        out = jnp.where((index >> b) & 1 == 1, jnp.flip(out, ax), out)
    return out.reshape(array.shape)


def table_kernel(nblk, hi_c, hi_s, lo_c, lo_s, out):
    rows = hi_c.shape[0]
    cl, sl = lo_c[...], lo_s[...]
    for b in range(nblk):
        ch, sh = hi_c[:, b : b + 1], hi_s[:, b : b + 1]
        cols = slice(b * LANES, (b + 1) * LANES)
        out[:rows, cols] = (ch * cl - sh * sl).astype(BF16)
        out[rows:, cols] = (-(sh * cl + ch * sl)).astype(BF16)


def make_table(waves, nlon):
    nblk = nlon // LANES
    scale = 2.0 * jnp.pi / nlon
    step_lo = jnp.arange(LANES, dtype=jnp.int32)
    step_hi = jnp.arange(LANES, dtype=jnp.int32) * LANES
    lo = (waves[:, None] * step_lo[None, :] % nlon).astype(F32) * scale
    hi = (waves[:, None] * step_hi[None, :] % nlon).astype(F32) * scale
    rows = waves.shape[0]
    return pl.pallas_call(
        functools.partial(table_kernel, nblk),
        out_shape=jax.ShapeDtypeStruct((2 * rows, nlon), BF16),
        name="table",
    )(jnp.cos(hi), jnp.sin(hi), jnp.cos(lo), jnp.sin(lo))


def dft_kernel(groups, vb, latd, x_ref, t_ref, wind_ref, lat_ref, wave_ref, *rest):
    outs, (xf, scr) = rest[:groups], rest[groups:]
    rows = t_ref.shape[0]
    half = rows // 2
    per = half // groups
    nblk = x_ref.shape[2] // LANES

    @pl.when(pl.program_id(0) == 0)
    def _():
        xf[...] = jnp.zeros_like(xf)

    wind = jnp.concatenate([wind_ref[...]] * nblk, axis=1)
    rate = lat_ref[0:1, :]
    weight = lat_ref[1:2, :]

    def body(v, carry):
        xv = x_ref[v]
        x32 = xv.astype(F32)
        xf[0:latd, :] = xv
        xf[LANES : LANES + latd, :] = (x32 * (wind + x32)).astype(BF16)
        both = lax.dot_general(
            t_ref[...], xf[...], (((1,), (1,)), ((), ())), preferred_element_type=F32
        )
        plain, moved = both[:, :LANES], both[:, LANES:]
        factor = wave_ref[...] * rate
        real = (plain[:half] + factor * moved[half:]) * weight
        imag = (plain[half:] - factor * moved[:half]) * weight
        scr[pl.ds(v, half, stride=vb), :] = real
        scr[pl.ds(half * vb + v, half, stride=vb), :] = imag
        return carry

    lax.fori_loop(0, vb, body, 0, unroll=2)
    for g in range(groups):
        for c in range(2):
            start = (c * half + g * per) * vb
            piece = scr[start : start + per * vb, :].reshape(per, vb, LANES)
            outs[g][:, c] = piece[:, :, :latd].astype(BF16)


def dft(x, table, wind, latrow, waves, groups):
    levd, latd, nlon = x.shape
    rows = table.shape[0]
    half = rows // 2
    per = half // groups
    vb = 8
    const = lambda i: (0, 0)
    block = pl.BlockSpec((per, 2, vb, latd), lambda i: (0, 0, i, 0))
    return pl.pallas_call(
        functools.partial(dft_kernel, groups, vb, latd),
        out_shape=[jax.ShapeDtypeStruct((per, 2, levd, latd), BF16)] * groups,
        grid=(levd // vb,),
        in_specs=[
            pl.BlockSpec((vb, latd, nlon), lambda i: (i, 0, 0)),
            pl.BlockSpec((rows, nlon), const),
            pl.BlockSpec((latd, LANES), const),
            pl.BlockSpec((2, LANES), const),
            pl.BlockSpec((half, LANES), const),
        ],
        out_specs=[block] * groups,
        scratch_shapes=[
            pltpu.VMEM((2 * LANES, nlon), BF16),
            pltpu.VMEM((rows * vb, LANES), F32),
        ],
        cost_estimate=pl.CostEstimate(
            flops=4 * rows * levd * latd * nlon,
            bytes_accessed=2 * levd * latd * (nlon + rows) + 2 * rows * nlon,
            transcendentals=0,
        ),
        name="dft",
    )(x, table, wind, latrow, jnp.broadcast_to(waves.astype(F32)[:, None], (half, LANES)))


def split3_dot(w3, x):
    hi = x.astype(BF16)
    lo = (x - hi.astype(F32)).astype(BF16)
    return jnp.dot(w3, jnp.concatenate([hi, lo, hi], axis=0), preferred_element_type=F32)


def legendre_kernel(
    groups, levs, latd, nmodes, info, leg_ref, perm_ref, w1_ref, w2_ref, mr_ref, *rest
):
    own = rest[:groups]
    other = rest[groups]
    outs = rest[groups + 1 : 2 * groups + 1]
    give = rest[2 * groups + 1]
    acc = rest[2 * groups + 2]
    levd = own[0].shape[2]
    nlev = levs * levd
    count = leg_ref.shape[0]
    t = pl.program_id(0)

    @pl.when(t == 0)
    def _():
        acc[...] = jnp.zeros_like(acc)

    k = lax.broadcasted_iota(jnp.int32, (1, nmodes), 1)
    first = info[2, 0] == 0
    keep_own = jnp.where(first, 0.0, 1.0)
    keep_other = jnp.where(first, 1.0, 0.0)
    where = []
    for rel in range(groups):
        dz, dx = rel // levs, rel % levs
        for c in range(2):
            row = c * 2 * nlev + dx * levd
            where.append((rel, c, row, slice(dz * LANES, dz * LANES + latd)))
    for j in range(count):
        for rel, c, row, lanes in where:
            acc[j, row : row + levd, lanes] = own[rel][j, c].astype(F32)
            acc[j, row + nlev : row + nlev + levd, lanes] = other[rel, j, c].astype(F32)
    legs = [
        jnp.dot(perm_ref[...], leg_ref[j], preferred_element_type=F32).astype(BF16)
        for j in range(count)
    ]
    fresh = []
    for j in range(count):
        wave, terms = info[0, t * count + j], info[1, t * count + j]
        n = (wave + k).astype(F32)
        h = n * (n + 1.0) / float(nmodes * (nmodes - 1))
        scale_own = jnp.where(first, 1.0, h)
        scale_other = jnp.where(first, h, 1.0)
        denom = 1.0 + h * mr_ref[...]
        spec = jnp.dot(acc[j].astype(BF16), legs[j], preferred_element_type=F32)
        spec = jnp.where(k < terms, spec, 0.0)
        new = []
        for c in range(2):
            a = spec[c * 2 * nlev : c * 2 * nlev + nlev]
            b = spec[c * 2 * nlev + nlev : (c + 1) * 2 * nlev]
            src = jnp.concatenate([a * scale_own, b * scale_other], axis=0)
            q = split3_dot(w1_ref[...], src) / denom
            both = split3_dot(w2_ref[...], q)
            new.append(both[:nlev] + keep_own * a)
            new.append(both[nlev:] + keep_other * b)
        fresh.append(jnp.concatenate(new, axis=0).astype(BF16))
    for j in range(count):
        back = lax.dot_general(
            fresh[j], legs[j], (((1,), (1,)), ((), ())), preferred_element_type=F32
        )
        back = (back * float(nmodes) ** (-0.5)).astype(BF16)
        for rel, c, row, lanes in where:
            outs[rel][j, c] = back[row : row + levd, lanes]
            give[rel, j, c] = back[row + nlev : row + nlev + levd, lanes]


def legendre_step(info, leg, perm, w1, w2, rates, own, other, levs, nmodes):
    groups = len(own)
    count, _, levd, latd = other.shape[1:]
    lanes, nlat = perm.shape
    nlev = levs * levd
    const = lambda t, s: (0, 0)
    step = 2 if count % 2 == 0 else 1
    piece = pl.BlockSpec((step, 2, levd, latd), lambda t, s: (t, 0, 0, 0))
    stack = pl.BlockSpec((groups, step, 2, levd, latd), lambda t, s: (0, t, 0, 0, 0))
    flops = count * 2 * (2 * nlev * 2 * nmodes * lanes * 2 + nmodes * nlat * lanes)
    return pl.pallas_call(
        functools.partial(legendre_kernel, groups, levs, latd, nmodes),
        out_shape=[jax.ShapeDtypeStruct((2 * count, 2, levd, latd), BF16)] * groups
        + [jax.ShapeDtypeStruct((groups, count, 2, levd, latd), BF16)],
        grid_spec=pltpu.PrefetchScalarGridSpec(
            num_scalar_prefetch=1,
            grid=(count // step,),
            in_specs=[
                pl.BlockSpec((step, nlat, nmodes), lambda t, s: (s[3, 0] // step + t, 0, 0)),
                pl.BlockSpec((lanes, nlat), const),
                pl.BlockSpec(w1.shape, const),
                pl.BlockSpec(w2.shape, const),
                pl.BlockSpec(rates.shape, const),
            ]
            + [piece] * groups
            + [stack],
            out_specs=[piece] * groups + [stack],
            scratch_shapes=[pltpu.VMEM((step, 4 * nlev, lanes), F32)],
        ),
        cost_estimate=pl.CostEstimate(
            flops=flops,
            bytes_accessed=count * 2 * (nmodes * nlat + 8 * nlev * lanes),
            transcendentals=0,
        ),
        name="legendre",
    )(info, leg, perm, w1, w2, rates, *own, other)


def gather_kernel(groups, *refs):
    ins, out = refs[:groups], refs[-1]
    for r in range(groups):
        out[r] = ins[r][...]


def gather_halves(blocks, after):
    groups = len(blocks)
    count, _, levd, latd = blocks[0].shape
    half = count // 2
    any_spec = pl.BlockSpec(memory_space=pl.ANY)
    return pl.pallas_call(
        functools.partial(gather_kernel, groups),
        out_shape=jax.ShapeDtypeStruct((groups, half, 2, levd, latd), BF16),
        grid=(1,),
        in_specs=[pl.BlockSpec((half, 2, levd, latd), lambda i: (1, 0, 0, 0))] * groups
        + [any_spec] * len(after),
        out_specs=pl.BlockSpec((groups, half, 2, levd, latd), lambda i: (0, 0, 0, 0, 0)),
        name="gather_halves",
    )(*blocks, *after)


def fill_kernel(groups, got, *refs):
    outs = refs[-groups:]
    for r in range(groups):
        outs[r][...] = got[r]


def fill_halves(blocks, got):
    groups, half, _, levd, latd = got.shape
    any_spec = pl.BlockSpec(memory_space=pl.ANY)
    return pl.pallas_call(
        functools.partial(fill_kernel, groups),
        out_shape=[jax.ShapeDtypeStruct(b.shape, b.dtype) for b in blocks],
        grid=(1,),
        in_specs=[pl.BlockSpec(got.shape, lambda i: (0, 0, 0, 0, 0))] + [any_spec] * groups,
        out_specs=[pl.BlockSpec((half, 2, levd, latd), lambda i: (1, 0, 0, 0))] * groups,
        input_output_aliases={r + 1: r for r in range(groups)},
        name="fill_halves",
    )(got, *blocks)


def inverse_kernel(counts, vb, latd, scale, add, *refs):
    tabs, refs = refs[: len(counts)], refs[len(counts) :]
    pieces, refs = refs[: sum(counts)], refs[sum(counts) :]
    partial = refs[0] if add else None
    out, scr, lhs = refs[-3:]
    nlon = tabs[0].shape[1]
    base, depth = 0, 0
    for tab, number in zip(tabs, counts):
        rows = tab.shape[0]
        per = rows // (2 * number)
        for g in range(number):
            for c in range(2):
                at = (base + c * (rows // 2) + g * per) * vb
                part = pieces[depth + g][:, c].astype(F32)
                scr[at : at + per * vb, :latd] = part.reshape(per * vb, latd)
        base += rows
        depth += number
    for v in range(vb):
        col = scr[pl.ds(v, base, stride=vb), :].astype(BF16)
        lhs[v * LANES : (v + 1) * LANES, :] = col.T
    step = 3 * LANES
    for j in range(0, nlon, step):
        cols = slice(j, j + step)
        grid, base = None, 0
        for tab in tabs:
            rows = tab.shape[0]
            term = jnp.dot(
                lhs[:, base : base + rows], tab[:, cols], preferred_element_type=F32
            )
            grid = term if grid is None else grid + term
            base += rows
        grid = grid * scale
        for v in range(vb):
            piece = grid[v * LANES : v * LANES + latd]
            if partial is not None:
                piece = piece + partial[v, :, cols]
            out[v, :, cols] = piece.astype(out.dtype)


def inverse_dft(sets, partial, scale, out_dtype, after):
    tabs = [tab for tab, _ in sets]
    pieces = [p for _, group in sets for p in group]
    levd, latd = pieces[0].shape[2:]
    nlon = tabs[0].shape[1]
    rows = sum(tab.shape[0] for tab in tabs)
    vb = 8
    grid_block = pl.BlockSpec((vb, latd, nlon), lambda i: (i, 0, 0))
    in_specs = [pl.BlockSpec(tab.shape, lambda i: (0, 0)) for tab in tabs] + [
        pl.BlockSpec((p.shape[0], 2, vb, latd), lambda i: (0, 0, i, 0)) for p in pieces
    ]
    args = [*tabs, *pieces]
    if partial is not None:
        in_specs.append(grid_block)
        args.append(partial)
    in_specs += [pl.BlockSpec(memory_space=pl.ANY)] * len(after)
    args += after
    counts = tuple(len(group) for _, group in sets)
    return pl.pallas_call(
        functools.partial(inverse_kernel, counts, vb, latd, scale, partial is not None),
        out_shape=jax.ShapeDtypeStruct((levd, latd, nlon), out_dtype),
        grid=(levd // vb,),
        in_specs=in_specs,
        out_specs=grid_block,
        scratch_shapes=[
            pltpu.VMEM((rows * vb, LANES), F32),
            pltpu.VMEM((vb * LANES, rows), BF16),
        ],
        cost_estimate=pl.CostEstimate(
            flops=2 * rows * levd * latd * nlon,
            bytes_accessed=2 * levd * latd * (nlon + rows) + 2 * rows * nlon,
            transcendentals=0,
        ),
        name="inverse_dft",
    )(*args)


def local_fast(
    parts,
    grid_state,
    lat_order,
    slot_wave,
    truncation,
    zonal_wind,
    zonal_rate,
    quad_weight,
    legendre,
    vert_modes,
    vert_project,
    mode_rates,
    thermal_matrix,
    pressure_matrix,
):
    levd, latd, nlon = grid_state.shape[1:]
    slots = legendre.shape[0]
    nmodes = slot_wave.shape[0]
    nlat = lat_order.shape[0]
    nlev = vert_modes.shape[0]
    lats, levs = lax.axis_size("lat"), lax.axis_size("lev")
    groups = lats * levs
    z, x, f = lax.axis_index("lat"), lax.axis_index("lev"), lax.axis_index("fld")
    me = z * levs + x
    starts = [sum(parts[:i]) for i in range(len(parts))]

    waves = slot_wave.reshape(groups, 2, slots // 2)
    waves = xor_order(xor_order(waves, me, 0), f, 1)
    my_lats = lax.dynamic_slice_in_dim(lat_order, z * latd, latd)
    onehot = (my_lats[:, None] == jnp.arange(nlat, dtype=jnp.int32)[None, :]).astype(F32)
    per_lat = jnp.dot(
        onehot,
        jnp.stack([zonal_wind, zonal_rate, quad_weight * nlon ** (-0.5)], axis=1),
        precision=PRECISE,
    )
    wind = jnp.broadcast_to(per_lat[:, 0:1], (latd, LANES))
    latrow = jnp.pad(per_lat[:, 1:].T, ((0, 0), (0, LANES - latd)))

    first = f == 0
    mix = jnp.dot(vert_project, thermal_matrix, precision=PRECISE)
    drop = -jnp.dot(pressure_matrix, vert_modes, precision=PRECISE)
    by_col = lambda m: xor_order(m.reshape(nlev, levs, levd), x, 1).reshape(nlev, nlev)
    by_row = lambda m: xor_order(m.reshape(levs, levd, nlev), x, 0).reshape(nlev, nlev)
    w1 = by_col(jnp.where(first, vert_project, mix)), by_col(jnp.where(first, mix, vert_project))
    w1 = jnp.concatenate(w1, axis=1)
    w2 = by_row(jnp.where(first, vert_modes, drop)), by_row(jnp.where(first, drop, vert_modes))
    w2 = jnp.concatenate(w2, axis=0)

    def three(w):
        hi = lax.reduce_precision(w, 8, 7)
        lo = (w - hi).astype(BF16)
        hi = hi.astype(BF16)
        return jnp.concatenate([hi, hi, lo], axis=1)

    w1, w2 = three(w1), three(w2)
    rates = mode_rates[:, None]
    lat_rel = xor_order(lat_order.reshape(lats, latd), z, 0)
    lat_rel = jnp.pad(lat_rel, ((0, 0), (0, LANES - latd)), constant_values=-1).reshape(-1, 1)
    perm = (lat_rel == jnp.arange(nlat, dtype=jnp.int32)[None, :]).astype(BF16)
    my_waves = waves[0, 0]
    counts = pick_values(my_waves, truncation) - my_waves + 1

    lat_lev = ("lat", "lev")

    def exchange(blocks, order):
        out = list(blocks)
        for r in order:
            if r:
                pairs = [(i, i ^ r) for i in range(groups)]
                out[r] = lax.ppermute(blocks[r], lat_lev, pairs)
        return out

    def swap(block):
        return lax.ppermute(block, "fld", [(0, 1), (1, 0)])

    far, near = far_near(groups)
    tables, arrived = [], []
    for i, (at, part) in enumerate(zip(starts, parts)):
        blocks = [None] * groups
        tables.append({})
        for rels in (far, near) if i == 0 else (near, far):
            w = waves[rels[0] : rels[-1] + 1, :, at : at + part].reshape(-1)
            tables[i][rels] = make_table(w, nlon)
            got = dft(grid_state[0], tables[i][rels], wind, latrow, w, len(rels))
            blocks[rels[0] : rels[-1] + 1] = got
        arrived.append(exchange(blocks, far + near))
    legendre = jnp.swapaxes(legendre, 1, 2)
    returned = []
    after = [arrived[-1][0]]
    for i, (at, part) in enumerate(zip(starts, parts)):
        other = gather_halves(arrived[i], after)
        other = swap(other)
        info = jnp.stack(
            [
                my_waves[at : at + part],
                counts[at : at + part],
                jnp.full((part,), f, jnp.int32),
                jnp.full((part,), f * (slots // 2) + at, jnp.int32),
            ]
        )
        res = legendre_step(info, legendre, perm, w1, w2, rates, arrived[i], other, levs, nmodes)
        got = swap(res[groups])
        sent = fill_halves(res[:groups], got)
        after = [sent[0]]
        returned.append(exchange(sent, near + far))
    total = None
    last = len(parts) - 1
    scale = float(nmodes) ** (-0.5)
    one = lambda i, rels: (tables[i][rels], [returned[i][r] for r in rels])
    for i in range(last):
        total = inverse_dft([one(i, near), one(i, far)], total, scale, F32, after)
    total = inverse_dft([one(last, near)], total, scale, F32, [])
    total = inverse_dft([one(last, far)], total, scale, BF16, [])
    return total[None]


def far_near(groups):
    rels = tuple(range(groups))
    return rels[groups // 2 :], rels[: groups // 2]


def power_of_two(n):
    return n & (n - 1) == 0


def solution(mesh):
    in_specs = (
        P(("member", "fld"), "lev", "lat", None),
        P(),
        P(),
        P(),
        P(),
        P(),
        P(),
        P(("lat", "lev"), None, None),
        P(),
        P(),
        P(),
        P(),
        P(),
    )
    out_specs = P(("member", "fld"), "lev", "lat", None)
    lats, levs = mesh.shape["lat"], mesh.shape["lev"]

    groups = lats * levs
    small = (
        mesh.shape["fld"] == 2 and power_of_two(lats) and power_of_two(levs) and 1 < groups <= 8
    )

    def local(grid_state, *rest):
        legendre = rest[6]
        levd, latd, nlon = grid_state.shape[1:]
        fits = (
            legendre.shape[0] % (4 * sum(SHARES)) == 0
            and levd % 8 == 0
            and latd % 8 == 0
            and latd <= LANES
            and nlon % (3 * LANES) == 0
        )
        if small and fits:
            unit = legendre.shape[0] // (2 * sum(SHARES))
            return local_fast([unit * n for n in SHARES], grid_state, *rest)
        return local_general(grid_state, *rest)

    return jax.shard_map(local, mesh=mesh, in_specs=in_specs, out_specs=out_specs, check_vma=False)
```

```python
import functools

import jax
import jax.numpy as jnp
from jax import lax
from jax.experimental import pallas as pl
from jax.experimental.pallas import tpu as pltpu
from jax.sharding import PartitionSpec as P


PRECISE = lax.Precision.HIGHEST
BF16 = jnp.bfloat16
F32 = jnp.float32


def dft_table(wavenums, nlon):
    columns = jnp.arange(nlon, dtype=jnp.int32)
    turns = columns[:, None] * wavenums[None, :] % nlon
    angles = turns.astype(jnp.float32) * (2.0 * jnp.pi / nlon)
    return jnp.stack([jnp.cos(angles), -jnp.sin(angles)], axis=1).astype(jnp.bfloat16)


def pick_values(idents, source_table):
    hits = idents[:, None] == jnp.arange(source_table.shape[0], dtype=jnp.int32)[None, :]
    return jnp.sum(jnp.where(hits, source_table[None, :], 0), axis=1)


def layer_eigen_basis(matrix, columns):
    return jnp.einsum("skcj,ij->skci", columns, matrix, precision=PRECISE)


def analyse(legendre, fourier_data):
    return jnp.einsum("skl,slx->skx", legendre, fourier_data, preferred_element_type=jnp.float32)


def synthesise(legendre, coeffs):
    return jnp.einsum("skl,skx->slx", legendre, coeffs, preferred_element_type=jnp.float32)


def local_general(
    grid_state,
    lat_order,
    slot_wave,
    truncation,
    zonal_wind,
    zonal_rate,
    quad_weight,
    legendre,
    vert_modes,
    vert_project,
    mode_rates,
    thermal_into_spread_matrix,
    pressure_balance_matrix,
):
    levd, latd, nlon = (grid_state.shape[1], grid_state.shape[2], grid_state.shape[3])
    slots = legendre.shape[0]
    nmodes = slot_wave.shape[0]
    nlat = lat_order.shape[0]
    nlev = vert_modes.shape[0]
    lat_count = lax.axis_size("lat")
    lev_count = lax.axis_size("lev")
    lat_index = lax.axis_index("lat")
    lev_index = lax.axis_index("lev")
    unknown_position = lax.axis_index("fld")
    my_lats = lax.dynamic_slice_in_dim(lat_order, lat_index * latd, latd)
    onehot = (my_lats[:, None] == jnp.arange(nlat, dtype=jnp.int32)[None, :]).astype(jnp.float32)
    per_lat = jnp.dot(
        onehot, jnp.stack([zonal_wind, zonal_rate, quad_weight], axis=1), precision=PRECISE
    )
    values = grid_state[0].astype(jnp.float32)
    flux = (values * (per_lat[None, :, 0][:, :, None] + values)).astype(jnp.bfloat16)
    count_rows = levd * latd
    stacked = jnp.concatenate(
        [grid_state[0].reshape(count_rows, nlon), flux.reshape(count_rows, nlon)], axis=0
    )
    table = dft_table(slot_wave, nlon).reshape(nlon, 2 * nmodes)
    spectra = lax.dot_general(
        table, stacked, (((0,), (1,)), ((), ())), preferred_element_type=jnp.float32
    ) * nlon ** (-0.5)
    spectra = spectra.reshape(2, nmodes, 2 * count_rows)
    plain = spectra[:, :, :count_rows]
    moved = spectra[:, :, count_rows:]
    rate_row = jnp.tile(per_lat[:, 1], levd)[None, :]
    weight_row = jnp.tile(per_lat[:, 2], levd)[None, :]
    wave_float = slot_wave.astype(jnp.float32)[:, None]
    factor = rate_row * wave_float
    real_part = (plain[0] + factor * moved[1]) * weight_row
    imag_part = (plain[1] - factor * moved[0]) * weight_row
    fourier = jnp.stack([real_part, imag_part], axis=0).astype(jnp.bfloat16)
    arrived = lax.all_to_all(fourier, ("lat", "lev"), split_axis=1, concat_axis=2, tiled=True)
    arrived = arrived.reshape(2, slots, lat_count, lev_count, levd, latd)
    arranged = jnp.transpose(arrived, (1, 2, 5, 0, 3, 4))
    arranged = arranged.reshape(slots, nlat, 2 * nlev)
    position = jnp.zeros((nlat,), jnp.int32).at[lat_order].set(jnp.arange(nlat, dtype=jnp.int32))
    ordered = jnp.take(arranged, position, axis=1)
    owner_index = lat_index * lev_count + lev_index
    my_waves = lax.dynamic_slice_in_dim(slot_wave, owner_index * slots, slots)
    limits = pick_values(my_waves, truncation)
    counts = limits - my_waves + 1
    degree = jnp.arange(nmodes, dtype=jnp.int32)
    valid = (degree[None, :] < counts[:, None])[:, :, None]
    own_spec = jnp.where(valid, analyse(legendre, ordered), jnp.float32(0.0))
    joined_harmonic_unknowns = lax.all_gather(own_spec, "fld", axis=2, tiled=True)
    joined_harmonic_unknowns = joined_harmonic_unknowns.reshape(slots, nmodes, 2, 2, nlev)
    outflow_rate_coeffs = joined_harmonic_unknowns[:, :, 0]
    thermal_coeffs = joined_harmonic_unknowns[:, :, 1]
    n_deg = (my_waves[:, None] + degree[None, :]).astype(jnp.float32)
    elliptic_inverse_scale = (n_deg * (n_deg + 1.0) / (nmodes * (nmodes - 1)))[:, :, None, None]
    outflow_rate_source = outflow_rate_coeffs + elliptic_inverse_scale * layer_eigen_basis(
        thermal_into_spread_matrix, thermal_coeffs
    )
    projected = layer_eigen_basis(vert_project, outflow_rate_source) / (
        1.0 + elliptic_inverse_scale * mode_rates
    )
    outflow_rate_next = layer_eigen_basis(vert_modes, projected)
    thermal_next = thermal_coeffs - layer_eigen_basis(pressure_balance_matrix, outflow_rate_next)
    own_new = (
        jnp.where(unknown_position == 0, outflow_rate_next, thermal_next)
        .astype(jnp.bfloat16)
        .reshape(slots, nmodes, 2 * nlev)
    )
    back = synthesise(legendre, own_new) * nmodes ** (-0.5)
    back = jnp.take(back, lat_order, axis=1).astype(jnp.bfloat16)
    shaped = back.reshape(slots, lat_count, latd, 2, lev_count, levd)
    outgoing = jnp.transpose(shaped, (3, 0, 1, 4, 5, 2)).reshape(
        2, slots, lat_count * lev_count * count_rows
    )
    returned = lax.all_to_all(outgoing, ("lat", "lev"), split_axis=2, concat_axis=1, tiled=True)
    leading = returned.reshape(2 * nmodes, count_rows)
    grid_out = lax.dot_general(
        leading, table, (((0,), (1,)), ((), ())), preferred_element_type=jnp.float32
    ) * nmodes ** (-0.5)
    return grid_out.astype(jnp.bfloat16).reshape(1, levd, latd, nlon)


LANES = 128
UNROLL = 2
SHARES = (1, 1)


def xor_order(array, index, axis):
    size = array.shape[axis]
    bits = size.bit_length() - 1
    shape = array.shape[:axis] + (2,) * bits + array.shape[axis + 1 :]
    out = array.reshape(shape)
    for b in range(bits):
        ax = axis + bits - 1 - b
        out = jnp.where((index >> b) & 1 == 1, jnp.flip(out, ax), out)
    return out.reshape(array.shape)


def table_kernel(nblk, hi_c, hi_s, lo_c, lo_s, out):
    rows = hi_c.shape[0]
    cl, sl = lo_c[...], lo_s[...]
    for b in range(nblk):
        ch, sh = hi_c[:, b : b + 1], hi_s[:, b : b + 1]
        cols = slice(b * LANES, (b + 1) * LANES)
        out[:rows, cols] = (ch * cl - sh * sl).astype(BF16)
        out[rows:, cols] = (-(sh * cl + ch * sl)).astype(BF16)


def make_table(waves, nlon):
    nblk = nlon // LANES
    scale = 2.0 * jnp.pi / nlon
    step_lo = jnp.arange(LANES, dtype=jnp.int32)
    step_hi = jnp.arange(LANES, dtype=jnp.int32) * LANES
    lo = (waves[:, None] * step_lo[None, :] % nlon).astype(F32) * scale
    hi = (waves[:, None] * step_hi[None, :] % nlon).astype(F32) * scale
    rows = waves.shape[0]
    return pl.pallas_call(
        functools.partial(table_kernel, nblk),
        out_shape=jax.ShapeDtypeStruct((2 * rows, nlon), BF16),
        name="table",
    )(jnp.cos(hi), jnp.sin(hi), jnp.cos(lo), jnp.sin(lo))


def column_table_kernel(nlon, wave_ref, out):
    width = wave_ref.shape[1]
    nblk = nlon // LANES
    wave = wave_ref[...]

    def angles(rows, step):
        index = lax.broadcasted_iota(jnp.int32, (rows, width), 0) * step
        turns = index.astype(F32) * wave
        turns = turns - nlon * jnp.floor(turns * (1.0 / nlon))
        turns = jnp.where(turns < 0.0, turns + nlon, turns)
        turns = jnp.where(turns >= nlon, turns - nlon, turns)
        return turns * (2.0 * jnp.pi / nlon)

    lo = angles(LANES, 1)
    cl, sl = jnp.cos(lo), jnp.sin(lo)
    hi = angles(16, LANES)
    ch, sh = jnp.cos(hi), jnp.sin(hi)
    for b in range(nblk):
        c, s = ch[b : b + 1], sh[b : b + 1]
        rows = slice(b * LANES, (b + 1) * LANES)
        out[rows, :width] = (c * cl - s * sl).astype(BF16)
        out[rows, width:] = (-(s * cl + c * sl)).astype(BF16)


def make_column_table(wave_row, nlon):
    width = wave_row.shape[1]
    return pl.pallas_call(
        functools.partial(column_table_kernel, nlon),
        out_shape=jax.ShapeDtypeStruct((nlon, 2 * width), BF16),
        name="column_table",
    )(wave_row)


def dft_kernel(groups, vb, latd, slots, x_ref, t_ref, lat_ref, wave_ref, *rest):
    outs, (xf, scr) = rest[:groups], rest[groups:]
    width = t_ref.shape[1] // 2
    per = slots // groups

    @pl.when(pl.program_id(0) == 0)
    def _():
        xf[...] = jnp.zeros_like(xf)

    wind = lat_ref[:, 0:1]
    factor = lat_ref[:, 1:2] * wave_ref[...]
    weight = lat_ref[:, 2:3]
    pair = 2

    def body(p, carry):
        for u in range(pair):
            xv = x_ref[p * pair + u]
            x32 = xv.astype(F32)
            at = u * 2 * LANES
            xf[at : at + latd, :] = xv
            xf[at + LANES : at + LANES + latd, :] = (x32 * (wind + x32)).astype(BF16)
        both = jnp.dot(xf[...], t_ref[...], preferred_element_type=F32)
        for u in range(pair):
            v = p * pair + u
            at = u * 2 * LANES
            plain = both[at : at + latd]
            moved = both[at + LANES : at + LANES + latd]
            real = (plain[:, :width] + factor * moved[:, width:]) * weight
            imag = (plain[:, width:] - factor * moved[:, :width]) * weight
            pad = jnp.zeros((LANES - latd, width), F32)
            real = jnp.concatenate([real, pad], axis=0).T
            imag = jnp.concatenate([imag, pad], axis=0).T
            scr[pl.ds(v, slots, stride=vb), :] = real[:slots]
            scr[pl.ds(slots * vb + v, slots, stride=vb), :] = imag[:slots]
        return carry

    lax.fori_loop(0, vb // pair, body, 0, unroll=UNROLL)
    for g in range(groups):
        for c in range(2):
            start = (c * slots + g * per) * vb
            piece = scr[start : start + per * vb, :].reshape(per, vb, LANES)
            outs[g][:, c] = piece[:, :, :latd].astype(BF16)


def dft(x, table, per_lat, wave_row, slots, groups):
    levd, latd, nlon = x.shape
    per = slots // groups
    vb = 8
    const = lambda i: (0, 0)
    block = pl.BlockSpec((per, 2, vb, latd), lambda i: (0, 0, i, 0))
    return pl.pallas_call(
        functools.partial(dft_kernel, groups, vb, latd, slots),
        out_shape=[jax.ShapeDtypeStruct((per, 2, levd, latd), BF16)] * groups,
        grid=(levd // vb,),
        in_specs=[
            pl.BlockSpec((vb, latd, nlon), lambda i: (i, 0, 0)),
            pl.BlockSpec(table.shape, const),
            pl.BlockSpec(per_lat.shape, const),
            pl.BlockSpec(wave_row.shape, const),
        ],
        out_specs=[block] * groups,
        scratch_shapes=[
            pltpu.VMEM((4 * LANES, nlon), BF16),
            pltpu.VMEM((2 * slots * vb, LANES), F32),
        ],
        cost_estimate=pl.CostEstimate(
            flops=8 * slots * levd * latd * nlon,
            bytes_accessed=2 * levd * latd * (nlon + 2 * slots) + 4 * slots * nlon,
            transcendentals=0,
        ),
        name="dft",
    )(x, table, per_lat, wave_row)


def split3_dot(w3, x):
    hi = x.astype(BF16)
    lo = (x - hi.astype(F32)).astype(BF16)
    return jnp.dot(w3, jnp.concatenate([hi, lo, hi], axis=0), preferred_element_type=F32)


def legendre_kernel(
    groups, levs, latd, nmodes, info, leg_ref, perm_ref, w1_ref, w2_ref, mr_ref, *rest
):
    own = rest[:groups]
    other = rest[groups]
    outs = rest[groups + 1 : 2 * groups + 1]
    give = rest[2 * groups + 1]
    acc = rest[2 * groups + 2]
    levd = own[0].shape[2]
    nlev = levs * levd
    count = leg_ref.shape[0]
    t = pl.program_id(0)

    @pl.when(t == 0)
    def _():
        acc[...] = jnp.zeros_like(acc)

    k = lax.broadcasted_iota(jnp.int32, (1, nmodes), 1)
    first = info[2, 0] == 0
    keep_own = jnp.where(first, 0.0, 1.0)
    keep_other = jnp.where(first, 1.0, 0.0)
    where = []
    for rel in range(groups):
        dz, dx = rel // levs, rel % levs
        for c in range(2):
            row = c * 2 * nlev + dx * levd
            where.append((rel, c, row, slice(dz * LANES, dz * LANES + latd)))
    for j in range(count):
        for rel, c, row, lanes in where:
            acc[j, row : row + levd, lanes] = own[rel][j, c].astype(F32)
            acc[j, row + nlev : row + nlev + levd, lanes] = other[rel, j, c].astype(F32)
    legs = [
        jnp.dot(perm_ref[...], leg_ref[j], preferred_element_type=F32).astype(BF16)
        for j in range(count)
    ]
    fresh = []
    for j in range(count):
        wave, terms = info[0, t * count + j], info[1, t * count + j]
        n = (wave + k).astype(F32)
        h = n * (n + 1.0) / float(nmodes * (nmodes - 1))
        scale_own = jnp.where(first, 1.0, h)
        scale_other = jnp.where(first, h, 1.0)
        denom = 1.0 + h * mr_ref[...]
        spec = jnp.dot(acc[j].astype(BF16), legs[j], preferred_element_type=F32)
        spec = jnp.where(k < terms, spec, 0.0)
        new = []
        for c in range(2):
            a = spec[c * 2 * nlev : c * 2 * nlev + nlev]
            b = spec[c * 2 * nlev + nlev : (c + 1) * 2 * nlev]
            src = jnp.concatenate([a * scale_own, b * scale_other], axis=0)
            q = split3_dot(w1_ref[...], src) / denom
            both = split3_dot(w2_ref[...], q)
            new.append(both[:nlev] + keep_own * a)
            new.append(both[nlev:] + keep_other * b)
        fresh.append(jnp.concatenate(new, axis=0).astype(BF16))
    for j in range(count):
        back = lax.dot_general(
            fresh[j], legs[j], (((1,), (1,)), ((), ())), preferred_element_type=F32
        )
        back = (back * float(nmodes) ** (-0.5)).astype(BF16)
        for rel, c, row, lanes in where:
            outs[rel][j, c] = back[row : row + levd, lanes]
            give[rel, j, c] = back[row + nlev : row + nlev + levd, lanes]


def legendre_step(info, leg, perm, w1, w2, rates, own, other, levs, nmodes):
    groups = len(own)
    count, _, levd, latd = other.shape[1:]
    lanes, nlat = perm.shape
    nlev = levs * levd
    const = lambda t, s: (0, 0)
    step = 2 if count % 2 == 0 else 1
    piece = pl.BlockSpec((step, 2, levd, latd), lambda t, s: (t, 0, 0, 0))
    stack = pl.BlockSpec((groups, step, 2, levd, latd), lambda t, s: (0, t, 0, 0, 0))
    flops = count * 2 * (2 * nlev * 2 * nmodes * lanes * 2 + nmodes * nlat * lanes)
    return pl.pallas_call(
        functools.partial(legendre_kernel, groups, levs, latd, nmodes),
        out_shape=[jax.ShapeDtypeStruct((2 * count, 2, levd, latd), BF16)] * groups
        + [jax.ShapeDtypeStruct((groups, count, 2, levd, latd), BF16)],
        grid_spec=pltpu.PrefetchScalarGridSpec(
            num_scalar_prefetch=1,
            grid=(count // step,),
            in_specs=[
                pl.BlockSpec((step, nlat, nmodes), lambda t, s: (s[3, 0] // step + t, 0, 0)),
                pl.BlockSpec((lanes, nlat), const),
                pl.BlockSpec(w1.shape, const),
                pl.BlockSpec(w2.shape, const),
                pl.BlockSpec(rates.shape, const),
            ]
            + [piece] * groups
            + [stack],
            out_specs=[piece] * groups + [stack],
            scratch_shapes=[pltpu.VMEM((step, 4 * nlev, lanes), F32)],
        ),
        cost_estimate=pl.CostEstimate(
            flops=flops,
            bytes_accessed=count * 2 * (nmodes * nlat + 8 * nlev * lanes),
            transcendentals=0,
        ),
        name="legendre",
    )(info, leg, perm, w1, w2, rates, *own, other)


def gather_kernel(groups, *refs):
    ins, out = refs[:groups], refs[-1]
    for r in range(groups):
        out[r] = ins[r][...]


def gather_halves(blocks, after):
    groups = len(blocks)
    count, _, levd, latd = blocks[0].shape
    half = count // 2
    any_spec = pl.BlockSpec(memory_space=pl.ANY)
    return pl.pallas_call(
        functools.partial(gather_kernel, groups),
        out_shape=jax.ShapeDtypeStruct((groups, half, 2, levd, latd), BF16),
        grid=(1,),
        in_specs=[pl.BlockSpec((half, 2, levd, latd), lambda i: (1, 0, 0, 0))] * groups
        + [any_spec] * len(after),
        out_specs=pl.BlockSpec((groups, half, 2, levd, latd), lambda i: (0, 0, 0, 0, 0)),
        name="gather_halves",
    )(*blocks, *after)


def fill_kernel(groups, got, *refs):
    outs = refs[-groups:]
    for r in range(groups):
        outs[r][...] = got[r]


def fill_halves(blocks, got):
    groups, half, _, levd, latd = got.shape
    any_spec = pl.BlockSpec(memory_space=pl.ANY)
    return pl.pallas_call(
        functools.partial(fill_kernel, groups),
        out_shape=[jax.ShapeDtypeStruct(b.shape, b.dtype) for b in blocks],
        grid=(1,),
        in_specs=[pl.BlockSpec(got.shape, lambda i: (0, 0, 0, 0, 0))] + [any_spec] * groups,
        out_specs=[pl.BlockSpec((half, 2, levd, latd), lambda i: (1, 0, 0, 0))] * groups,
        input_output_aliases={r + 1: r for r in range(groups)},
        name="fill_halves",
    )(got, *blocks)


def inverse_kernel(counts, vb, latd, scale, add, *refs):
    tabs, refs = refs[: len(counts)], refs[len(counts) :]
    pieces, refs = refs[: sum(counts)], refs[sum(counts) :]
    partial = refs[0] if add else None
    out, scr, lhs = refs[-3:]
    nlon = tabs[0].shape[1]
    base, depth = 0, 0
    for tab, number in zip(tabs, counts):
        rows = tab.shape[0]
        per = rows // (2 * number)
        for g in range(number):
            for c in range(2):
                at = (base + c * (rows // 2) + g * per) * vb
                part = pieces[depth + g][:, c].astype(F32)
                scr[at : at + per * vb, :latd] = part.reshape(per * vb, latd)
        base += rows
        depth += number
    for v in range(vb):
        col = scr[pl.ds(v, base, stride=vb), :].astype(BF16)
        lhs[v * LANES : (v + 1) * LANES, :] = col.T
    step = 3 * LANES
    for j in range(0, nlon, step):
        cols = slice(j, j + step)
        grid, base = None, 0
        for tab in tabs:
            rows = tab.shape[0]
            term = jnp.dot(
                lhs[:, base : base + rows], tab[:, cols], preferred_element_type=F32
            )
            grid = term if grid is None else grid + term
            base += rows
        grid = grid * scale
        for v in range(vb):
            piece = grid[v * LANES : v * LANES + latd]
            if partial is not None:
                piece = piece + partial[v, :, cols]
            out[v, :, cols] = piece.astype(out.dtype)


def inverse_dft(sets, partial, scale, out_dtype, after):
    tabs = [tab for tab, _ in sets]
    pieces = [p for _, group in sets for p in group]
    levd, latd = pieces[0].shape[2:]
    nlon = tabs[0].shape[1]
    rows = sum(tab.shape[0] for tab in tabs)
    vb = 8
    grid_block = pl.BlockSpec((vb, latd, nlon), lambda i: (i, 0, 0))
    in_specs = [pl.BlockSpec(tab.shape, lambda i: (0, 0)) for tab in tabs] + [
        pl.BlockSpec((p.shape[0], 2, vb, latd), lambda i: (0, 0, i, 0)) for p in pieces
    ]
    args = [*tabs, *pieces]
    if partial is not None:
        in_specs.append(grid_block)
        args.append(partial)
    in_specs += [pl.BlockSpec(memory_space=pl.ANY)] * len(after)
    args += after
    counts = tuple(len(group) for _, group in sets)
    return pl.pallas_call(
        functools.partial(inverse_kernel, counts, vb, latd, scale, partial is not None),
        out_shape=jax.ShapeDtypeStruct((levd, latd, nlon), out_dtype),
        grid=(levd // vb,),
        in_specs=in_specs,
        out_specs=grid_block,
        scratch_shapes=[
            pltpu.VMEM((rows * vb, LANES), F32),
            pltpu.VMEM((vb * LANES, rows), BF16),
        ],
        cost_estimate=pl.CostEstimate(
            flops=2 * rows * levd * latd * nlon,
            bytes_accessed=2 * levd * latd * (nlon + rows) + 2 * rows * nlon,
            transcendentals=0,
        ),
        name="inverse_dft",
    )(*args)


def local_fast(
    parts,
    grid_state,
    lat_order,
    slot_wave,
    truncation,
    zonal_wind,
    zonal_rate,
    quad_weight,
    legendre,
    vert_modes,
    vert_project,
    mode_rates,
    thermal_matrix,
    pressure_matrix,
):
    levd, latd, nlon = grid_state.shape[1:]
    slots = legendre.shape[0]
    nmodes = slot_wave.shape[0]
    nlat = lat_order.shape[0]
    nlev = vert_modes.shape[0]
    lats, levs = lax.axis_size("lat"), lax.axis_size("lev")
    groups = lats * levs
    z, x, f = lax.axis_index("lat"), lax.axis_index("lev"), lax.axis_index("fld")
    me = z * levs + x
    starts = [sum(parts[:i]) for i in range(len(parts))]

    waves = slot_wave.reshape(groups, 2, slots // 2)
    waves = xor_order(xor_order(waves, me, 0), f, 1)
    my_lats = lax.dynamic_slice_in_dim(lat_order, z * latd, latd)
    hits = my_lats[:, None, None] == jnp.arange(nlat, dtype=jnp.int32)[None, None, :]
    zonal = jnp.stack([zonal_wind, zonal_rate, quad_weight * nlon ** (-0.5)], axis=0)
    per_lat = jnp.sum(jnp.where(hits, zonal[None], 0.0), axis=2)

    first = f == 0
    mix = jnp.dot(vert_project, thermal_matrix, precision=PRECISE)
    drop = -jnp.dot(pressure_matrix, vert_modes, precision=PRECISE)
    by_col = lambda m: xor_order(m.reshape(nlev, levs, levd), x, 1).reshape(nlev, nlev)
    by_row = lambda m: xor_order(m.reshape(levs, levd, nlev), x, 0).reshape(nlev, nlev)
    w1 = by_col(jnp.where(first, vert_project, mix)), by_col(jnp.where(first, mix, vert_project))
    w1 = jnp.concatenate(w1, axis=1)
    w2 = by_row(jnp.where(first, vert_modes, drop)), by_row(jnp.where(first, drop, vert_modes))
    w2 = jnp.concatenate(w2, axis=0)

    def three(w):
        hi = lax.reduce_precision(w, 8, 7)
        lo = (w - hi).astype(BF16)
        hi = hi.astype(BF16)
        return jnp.concatenate([hi, hi, lo], axis=1)

    w1, w2 = three(w1), three(w2)
    rates = mode_rates[:, None]
    lat_rel = xor_order(lat_order.reshape(lats, latd), z, 0)
    lat_rel = jnp.pad(lat_rel, ((0, 0), (0, LANES - latd)), constant_values=-1).reshape(-1, 1)
    perm = (lat_rel == jnp.arange(nlat, dtype=jnp.int32)[None, :]).astype(BF16)
    my_waves = waves[0, 0]
    counts = pick_values(my_waves, truncation) - my_waves + 1

    lat_lev = ("lat", "lev")

    def exchange(blocks, order):
        out = list(blocks)
        for r in order:
            if r:
                pairs = [(i, i ^ r) for i in range(groups)]
                out[r] = lax.ppermute(blocks[r], lat_lev, pairs)
        return out

    def swap(block):
        return lax.ppermute(block, "fld", [(0, 1), (1, 0)])

    far, near = far_near(groups)
    tables, arrived = [], []
    for at, part in zip(starts, parts):
        w = waves[:, :, at : at + part].reshape(-1)
        row = jnp.pad(w.astype(F32), (0, -w.shape[0] % LANES))[None, :]
        columns = make_column_table(row, nlon)
        blocks = dft(grid_state[0], columns, per_lat, row, w.shape[0], groups)
        arrived.append(exchange(blocks, far + near))
        tables.append(make_table(w, nlon))
    legendre = jnp.swapaxes(legendre, 1, 2)
    returned = []
    after = [arrived[-1][0]]
    for i, (at, part) in enumerate(zip(starts, parts)):
        other = gather_halves(arrived[i], after)
        other = swap(other)
        info = jnp.stack(
            [
                my_waves[at : at + part],
                counts[at : at + part],
                jnp.full((part,), f, jnp.int32),
                jnp.full((part,), f * (slots // 2) + at, jnp.int32),
            ]
        )
        res = legendre_step(info, legendre, perm, w1, w2, rates, arrived[i], other, levs, nmodes)
        got = swap(res[groups])
        sent = fill_halves(res[:groups], got)
        after = [sent[0]]
        returned.append(exchange(sent, near + far))
    total = None
    last = len(parts) - 1
    for i in range(len(parts)):
        total = inverse_dft(
            [(tables[i], returned[i])],
            total,
            float(nmodes) ** (-0.5),
            BF16 if i == last else F32,
            [] if i == last else after,
        )
    return total[None]


def far_near(groups):
    rels = tuple(range(groups))
    return rels[groups // 2 :], rels[: groups // 2]


def power_of_two(n):
    return n & (n - 1) == 0


def solution(mesh):
    in_specs = (
        P(("member", "fld"), "lev", "lat", None),
        P(),
        P(),
        P(),
        P(),
        P(),
        P(),
        P(("lat", "lev"), None, None),
        P(),
        P(),
        P(),
        P(),
        P(),
    )
    out_specs = P(("member", "fld"), "lev", "lat", None)
    lats, levs = mesh.shape["lat"], mesh.shape["lev"]

    groups = lats * levs
    small = (
        mesh.shape["fld"] == 2 and power_of_two(lats) and power_of_two(levs) and 1 < groups <= 8
    )

    def local(grid_state, *rest):
        legendre = rest[6]
        levd, latd, nlon = grid_state.shape[1:]
        fits = (
            legendre.shape[0] % (4 * sum(SHARES)) == 0
            and levd % 8 == 0
            and latd % 8 == 0
            and latd <= LANES
            and nlon % (3 * LANES) == 0
        )
        if small and fits:
            unit = legendre.shape[0] // (2 * sum(SHARES))
            return local_fast([unit * n for n in SHARES], grid_state, *rest)
        return local_general(grid_state, *rest)

    return jax.shard_map(local, mesh=mesh, in_specs=in_specs, out_specs=out_specs, check_vma=False)
```

```python
import functools

import jax
import jax.numpy as jnp
from jax import lax
from jax.experimental import pallas as pl
from jax.experimental.pallas import tpu as pltpu
from jax.sharding import PartitionSpec as P


PRECISE = lax.Precision.HIGHEST
BF16 = jnp.bfloat16
F32 = jnp.float32


def dft_table(wavenums, nlon):
    columns = jnp.arange(nlon, dtype=jnp.int32)
    turns = columns[:, None] * wavenums[None, :] % nlon
    angles = turns.astype(jnp.float32) * (2.0 * jnp.pi / nlon)
    return jnp.stack([jnp.cos(angles), -jnp.sin(angles)], axis=1).astype(jnp.bfloat16)


def pick_values(idents, source_table):
    hits = idents[:, None] == jnp.arange(source_table.shape[0], dtype=jnp.int32)[None, :]
    return jnp.sum(jnp.where(hits, source_table[None, :], 0), axis=1)


def layer_eigen_basis(matrix, columns):
    return jnp.einsum("skcj,ij->skci", columns, matrix, precision=PRECISE)


def analyse(legendre, fourier_data):
    return jnp.einsum("skl,slx->skx", legendre, fourier_data, preferred_element_type=jnp.float32)


def synthesise(legendre, coeffs):
    return jnp.einsum("skl,skx->slx", legendre, coeffs, preferred_element_type=jnp.float32)


def local_general(
    grid_state,
    lat_order,
    slot_wave,
    truncation,
    zonal_wind,
    zonal_rate,
    quad_weight,
    legendre,
    vert_modes,
    vert_project,
    mode_rates,
    thermal_into_spread_matrix,
    pressure_balance_matrix,
):
    levd, latd, nlon = (grid_state.shape[1], grid_state.shape[2], grid_state.shape[3])
    slots = legendre.shape[0]
    nmodes = slot_wave.shape[0]
    nlat = lat_order.shape[0]
    nlev = vert_modes.shape[0]
    lat_count = lax.axis_size("lat")
    lev_count = lax.axis_size("lev")
    lat_index = lax.axis_index("lat")
    lev_index = lax.axis_index("lev")
    unknown_position = lax.axis_index("fld")
    my_lats = lax.dynamic_slice_in_dim(lat_order, lat_index * latd, latd)
    onehot = (my_lats[:, None] == jnp.arange(nlat, dtype=jnp.int32)[None, :]).astype(jnp.float32)
    per_lat = jnp.dot(
        onehot, jnp.stack([zonal_wind, zonal_rate, quad_weight], axis=1), precision=PRECISE
    )
    values = grid_state[0].astype(jnp.float32)
    flux = (values * (per_lat[None, :, 0][:, :, None] + values)).astype(jnp.bfloat16)
    count_rows = levd * latd
    stacked = jnp.concatenate(
        [grid_state[0].reshape(count_rows, nlon), flux.reshape(count_rows, nlon)], axis=0
    )
    table = dft_table(slot_wave, nlon).reshape(nlon, 2 * nmodes)
    spectra = lax.dot_general(
        table, stacked, (((0,), (1,)), ((), ())), preferred_element_type=jnp.float32
    ) * nlon ** (-0.5)
    spectra = spectra.reshape(2, nmodes, 2 * count_rows)
    plain = spectra[:, :, :count_rows]
    moved = spectra[:, :, count_rows:]
    rate_row = jnp.tile(per_lat[:, 1], levd)[None, :]
    weight_row = jnp.tile(per_lat[:, 2], levd)[None, :]
    wave_float = slot_wave.astype(jnp.float32)[:, None]
    factor = rate_row * wave_float
    real_part = (plain[0] + factor * moved[1]) * weight_row
    imag_part = (plain[1] - factor * moved[0]) * weight_row
    fourier = jnp.stack([real_part, imag_part], axis=0).astype(jnp.bfloat16)
    arrived = lax.all_to_all(fourier, ("lat", "lev"), split_axis=1, concat_axis=2, tiled=True)
    arrived = arrived.reshape(2, slots, lat_count, lev_count, levd, latd)
    arranged = jnp.transpose(arrived, (1, 2, 5, 0, 3, 4))
    arranged = arranged.reshape(slots, nlat, 2 * nlev)
    position = jnp.zeros((nlat,), jnp.int32).at[lat_order].set(jnp.arange(nlat, dtype=jnp.int32))
    ordered = jnp.take(arranged, position, axis=1)
    owner_index = lat_index * lev_count + lev_index
    my_waves = lax.dynamic_slice_in_dim(slot_wave, owner_index * slots, slots)
    limits = pick_values(my_waves, truncation)
    counts = limits - my_waves + 1
    degree = jnp.arange(nmodes, dtype=jnp.int32)
    valid = (degree[None, :] < counts[:, None])[:, :, None]
    own_spec = jnp.where(valid, analyse(legendre, ordered), jnp.float32(0.0))
    joined_harmonic_unknowns = lax.all_gather(own_spec, "fld", axis=2, tiled=True)
    joined_harmonic_unknowns = joined_harmonic_unknowns.reshape(slots, nmodes, 2, 2, nlev)
    outflow_rate_coeffs = joined_harmonic_unknowns[:, :, 0]
    thermal_coeffs = joined_harmonic_unknowns[:, :, 1]
    n_deg = (my_waves[:, None] + degree[None, :]).astype(jnp.float32)
    elliptic_inverse_scale = (n_deg * (n_deg + 1.0) / (nmodes * (nmodes - 1)))[:, :, None, None]
    outflow_rate_source = outflow_rate_coeffs + elliptic_inverse_scale * layer_eigen_basis(
        thermal_into_spread_matrix, thermal_coeffs
    )
    projected = layer_eigen_basis(vert_project, outflow_rate_source) / (
        1.0 + elliptic_inverse_scale * mode_rates
    )
    outflow_rate_next = layer_eigen_basis(vert_modes, projected)
    thermal_next = thermal_coeffs - layer_eigen_basis(pressure_balance_matrix, outflow_rate_next)
    own_new = (
        jnp.where(unknown_position == 0, outflow_rate_next, thermal_next)
        .astype(jnp.bfloat16)
        .reshape(slots, nmodes, 2 * nlev)
    )
    back = synthesise(legendre, own_new) * nmodes ** (-0.5)
    back = jnp.take(back, lat_order, axis=1).astype(jnp.bfloat16)
    shaped = back.reshape(slots, lat_count, latd, 2, lev_count, levd)
    outgoing = jnp.transpose(shaped, (3, 0, 1, 4, 5, 2)).reshape(
        2, slots, lat_count * lev_count * count_rows
    )
    returned = lax.all_to_all(outgoing, ("lat", "lev"), split_axis=2, concat_axis=1, tiled=True)
    leading = returned.reshape(2 * nmodes, count_rows)
    grid_out = lax.dot_general(
        leading, table, (((0,), (1,)), ((), ())), preferred_element_type=jnp.float32
    ) * nmodes ** (-0.5)
    return grid_out.astype(jnp.bfloat16).reshape(1, levd, latd, nlon)


LANES = 128
SHARES = (1, 1)


def xor_order(array, index, axis):
    size = array.shape[axis]
    bits = size.bit_length() - 1
    shape = array.shape[:axis] + (2,) * bits + array.shape[axis + 1 :]
    out = array.reshape(shape)
    for b in range(bits):
        ax = axis + bits - 1 - b
        out = jnp.where((index >> b) & 1 == 1, jnp.flip(out, ax), out)
    return out.reshape(array.shape)


def table_kernel(nblk, hi_c, hi_s, lo_c, lo_s, out):
    rows = hi_c.shape[0]
    cl, sl = lo_c[...], lo_s[...]
    for b in range(nblk):
        ch, sh = hi_c[:, b : b + 1], hi_s[:, b : b + 1]
        cols = slice(b * LANES, (b + 1) * LANES)
        out[:rows, cols] = (ch * cl - sh * sl).astype(BF16)
        out[rows:, cols] = (-(sh * cl + ch * sl)).astype(BF16)


def make_table(waves, nlon):
    nblk = nlon // LANES
    scale = 2.0 * jnp.pi / nlon
    step_lo = jnp.arange(LANES, dtype=jnp.int32)
    step_hi = jnp.arange(LANES, dtype=jnp.int32) * LANES
    lo = (waves[:, None] * step_lo[None, :] % nlon).astype(F32) * scale
    hi = (waves[:, None] * step_hi[None, :] % nlon).astype(F32) * scale
    rows = waves.shape[0]
    return pl.pallas_call(
        functools.partial(table_kernel, nblk),
        out_shape=jax.ShapeDtypeStruct((2 * rows, nlon), BF16),
        name="table",
    )(jnp.cos(hi), jnp.sin(hi), jnp.cos(lo), jnp.sin(lo))


def column_table_kernel(nlon, wave_ref, cos_ref, sin_ref):
    width = wave_ref.shape[1]
    depth = cos_ref.shape[0]
    wave = wave_ref[...]

    def angles(rows, step):
        index = lax.broadcasted_iota(jnp.int32, (rows, width), 0) * step
        turns = index.astype(F32) * wave
        turns = turns - nlon * jnp.floor(turns * (1.0 / nlon))
        turns = jnp.where(turns < 0.0, turns + nlon, turns)
        turns = jnp.where(turns >= nlon, turns - nlon, turns)
        return turns * (2.0 * jnp.pi / nlon)

    lo = angles(LANES, 1)
    cl, sl = jnp.cos(lo), jnp.sin(lo)
    hi = angles(8 * -(-depth // (8 * LANES)), LANES)
    ch, sh = jnp.cos(hi), jnp.sin(hi)
    row = lax.broadcasted_iota(jnp.int32, (LANES, width), 0)
    for b in range(depth // LANES):
        c, s = ch[b : b + 1], sh[b : b + 1]
        at = row + b * LANES
        share = jnp.where((at == 0) | (at == nlon // 2), 0.5, 1.0)
        share = jnp.where(at > nlon // 2, 0.0, share)
        rows = slice(b * LANES, (b + 1) * LANES)
        cos_ref[rows, :] = (share * (c * cl - s * sl)).astype(BF16)
        sin_ref[rows, :] = (-share * (s * cl + c * sl)).astype(BF16)


def make_column_tables(wave_row, nlon):
    width = wave_row.shape[1]
    depth = (nlon // 2 // LANES + 1) * LANES
    return pl.pallas_call(
        functools.partial(column_table_kernel, nlon),
        out_shape=[jax.ShapeDtypeStruct((depth, width), BF16)] * 2,
        name="column_table",
    )(wave_row)


def dft_kernel(groups, vb, latd, slots, x_ref, cos_ref, sin_ref, lat_ref, wave_ref, *rest):
    outs, (sums, difs, scr) = rest[:groups], rest[groups:]
    width = cos_ref.shape[1]
    depth = cos_ref.shape[0]
    per = slots // groups
    nblk = x_ref.shape[2] // LANES
    pair = 2

    @pl.when(pl.program_id(0) == 0)
    def _():
        sums[...] = jnp.zeros_like(sums)
        difs[...] = jnp.zeros_like(difs)

    wind = lat_ref[:, 0:1]
    factor = lat_ref[:, 1:2] * wave_ref[...]
    weight = lat_ref[:, 2:3]
    lane = lax.broadcasted_iota(jnp.int32, (latd, LANES), 1)
    mirror = (LANES - lane) % LANES
    first = lane == 0
    wind = jnp.broadcast_to(wind, (latd, LANES))

    def moved_of(x):
        return (x * (wind + x)).astype(BF16).astype(F32)

    def fold(p):
        for u in range(pair):
            at = u * 2 * LANES
            xs = [
                x_ref[p * pair + u, :, b * LANES : (b + 1) * LANES].astype(F32)
                for b in range(nblk)
            ]
            for b in range(depth // LANES):
                cols = slice(b * LANES, (b + 1) * LANES)
                x = xs[b]
                turned = jnp.take_along_axis(xs[nblk - 1 - b], mirror, axis=1)
                y = jnp.where(first, xs[(nblk - b) % nblk], turned)
                f, g = moved_of(x), moved_of(y)
                sums[p % 2, at : at + latd, cols] = (x + y).astype(BF16)
                difs[p % 2, at : at + latd, cols] = (x - y).astype(BF16)
                sums[p % 2, at + LANES : at + LANES + latd, cols] = (f + g).astype(BF16)
                difs[p % 2, at + LANES : at + LANES + latd, cols] = (f - g).astype(BF16)

    fold(0)
    for p in range(vb // pair):
        if p + 1 < vb // pair:
            fold(p + 1)
        even = jnp.dot(sums[p % 2], cos_ref[...], preferred_element_type=F32)
        odd = jnp.dot(difs[p % 2], sin_ref[...], preferred_element_type=F32)
        for u in range(pair):
            v = p * pair + u
            plain = slice(u * 2 * LANES, u * 2 * LANES + latd)
            moved = slice(u * 2 * LANES + LANES, u * 2 * LANES + LANES + latd)
            real = (even[plain] + factor * odd[moved]) * weight
            imag = (odd[plain] - factor * even[moved]) * weight
            pad = jnp.zeros((LANES - latd, width), F32)
            real = jnp.concatenate([real, pad], axis=0).T
            imag = jnp.concatenate([imag, pad], axis=0).T
            scr[pl.ds(v, slots, stride=vb), :] = real[:slots]
            scr[pl.ds(slots * vb + v, slots, stride=vb), :] = imag[:slots]
    for g in range(groups):
        for c in range(2):
            start = (c * slots + g * per) * vb
            piece = scr[start : start + per * vb, :].reshape(per, vb, LANES)
            outs[g][:, c] = piece[:, :, :latd].astype(BF16)


def dft(x, tables, per_lat, wave_row, slots, groups):
    levd, latd, nlon = x.shape
    per = slots // groups
    vb = 8
    const = lambda i: (0, 0)
    block = pl.BlockSpec((per, 2, vb, latd), lambda i: (0, 0, i, 0))
    shape = tables[0].shape
    return pl.pallas_call(
        functools.partial(dft_kernel, groups, vb, latd, slots),
        out_shape=[jax.ShapeDtypeStruct((per, 2, levd, latd), BF16)] * groups,
        grid=(levd // vb,),
        in_specs=[
            pl.BlockSpec((vb, latd, nlon), lambda i: (i, 0, 0)),
            pl.BlockSpec(shape, const),
            pl.BlockSpec(shape, const),
            pl.BlockSpec(per_lat.shape, const),
            pl.BlockSpec(wave_row.shape, const),
        ],
        out_specs=[block] * groups,
        scratch_shapes=[
            pltpu.VMEM((2, 4 * LANES, shape[0]), BF16),
            pltpu.VMEM((2, 4 * LANES, shape[0]), BF16),
            pltpu.VMEM((2 * slots * vb, LANES), F32),
        ],
        cost_estimate=pl.CostEstimate(
            flops=4 * slots * levd * latd * nlon,
            bytes_accessed=2 * levd * latd * (nlon + 2 * slots) + 4 * slots * nlon,
            transcendentals=0,
        ),
        name="dft",
    )(x, *tables, per_lat, wave_row)


def split3_dot(w3, x):
    hi = x.astype(BF16)
    lo = (x - hi.astype(F32)).astype(BF16)
    return jnp.dot(w3, jnp.concatenate([hi, lo, hi], axis=0), preferred_element_type=F32)


def legendre_kernel(
    groups, levs, latd, nmodes, info, leg_ref, perm_ref, w1_ref, w2_ref, mr_ref, *rest
):
    own = rest[:groups]
    other = rest[groups]
    outs = rest[groups + 1 : 2 * groups + 1]
    give = rest[2 * groups + 1]
    acc = rest[2 * groups + 2]
    levd = own[0].shape[2]
    nlev = levs * levd
    count = leg_ref.shape[0]
    t = pl.program_id(0)

    @pl.when(t == 0)
    def _():
        acc[...] = jnp.zeros_like(acc)

    k = lax.broadcasted_iota(jnp.int32, (1, nmodes), 1)
    first = info[2, 0] == 0
    keep_own = jnp.where(first, 0.0, 1.0)
    keep_other = jnp.where(first, 1.0, 0.0)
    where = []
    for rel in range(groups):
        dz, dx = rel // levs, rel % levs
        for c in range(2):
            row = c * 2 * nlev + dx * levd
            where.append((rel, c, row, slice(dz * LANES, dz * LANES + latd)))
    for j in range(count):
        for rel, c, row, lanes in where:
            acc[j, row : row + levd, lanes] = own[rel][j, c].astype(F32)
            acc[j, row + nlev : row + nlev + levd, lanes] = other[rel, j, c].astype(F32)
    legs = [
        jnp.dot(perm_ref[...], leg_ref[j], preferred_element_type=F32).astype(BF16)
        for j in range(count)
    ]
    fresh = []
    for j in range(count):
        wave, terms = info[0, t * count + j], info[1, t * count + j]
        n = (wave + k).astype(F32)
        h = n * (n + 1.0) / float(nmodes * (nmodes - 1))
        scale_own = jnp.where(first, 1.0, h)
        scale_other = jnp.where(first, h, 1.0)
        denom = 1.0 + h * mr_ref[...]
        spec = jnp.dot(acc[j].astype(BF16), legs[j], preferred_element_type=F32)
        spec = jnp.where(k < terms, spec, 0.0)
        new = []
        for c in range(2):
            a = spec[c * 2 * nlev : c * 2 * nlev + nlev]
            b = spec[c * 2 * nlev + nlev : (c + 1) * 2 * nlev]
            src = jnp.concatenate([a * scale_own, b * scale_other], axis=0)
            q = split3_dot(w1_ref[...], src) / denom
            both = split3_dot(w2_ref[...], q)
            new.append(both[:nlev] + keep_own * a)
            new.append(both[nlev:] + keep_other * b)
        fresh.append(jnp.concatenate(new, axis=0).astype(BF16))
    for j in range(count):
        back = lax.dot_general(
            fresh[j], legs[j], (((1,), (1,)), ((), ())), preferred_element_type=F32
        )
        back = (back * float(nmodes) ** (-0.5)).astype(BF16)
        for rel, c, row, lanes in where:
            outs[rel][j, c] = back[row : row + levd, lanes]
            give[rel, j, c] = back[row + nlev : row + nlev + levd, lanes]


def legendre_step(info, leg, perm, w1, w2, rates, own, other, levs, nmodes):
    groups = len(own)
    count, _, levd, latd = other.shape[1:]
    lanes, nlat = perm.shape
    nlev = levs * levd
    const = lambda t, s: (0, 0)
    step = 2 if count % 2 == 0 else 1
    piece = pl.BlockSpec((step, 2, levd, latd), lambda t, s: (t, 0, 0, 0))
    stack = pl.BlockSpec((groups, step, 2, levd, latd), lambda t, s: (0, t, 0, 0, 0))
    flops = count * 2 * (2 * nlev * 2 * nmodes * lanes * 2 + nmodes * nlat * lanes)
    return pl.pallas_call(
        functools.partial(legendre_kernel, groups, levs, latd, nmodes),
        out_shape=[jax.ShapeDtypeStruct((2 * count, 2, levd, latd), BF16)] * groups
        + [jax.ShapeDtypeStruct((groups, count, 2, levd, latd), BF16)],
        grid_spec=pltpu.PrefetchScalarGridSpec(
            num_scalar_prefetch=1,
            grid=(count // step,),
            in_specs=[
                pl.BlockSpec((step, nlat, nmodes), lambda t, s: (s[3, 0] // step + t, 0, 0)),
                pl.BlockSpec((lanes, nlat), const),
                pl.BlockSpec(w1.shape, const),
                pl.BlockSpec(w2.shape, const),
                pl.BlockSpec(rates.shape, const),
            ]
            + [piece] * groups
            + [stack],
            out_specs=[piece] * groups + [stack],
            scratch_shapes=[pltpu.VMEM((step, 4 * nlev, lanes), F32)],
        ),
        cost_estimate=pl.CostEstimate(
            flops=flops,
            bytes_accessed=count * 2 * (nmodes * nlat + 8 * nlev * lanes),
            transcendentals=0,
        ),
        name="legendre",
    )(info, leg, perm, w1, w2, rates, *own, other)


def gather_kernel(groups, *refs):
    ins, out = refs[:groups], refs[-1]
    for r in range(groups):
        out[r] = ins[r][...]


def gather_halves(blocks, after):
    groups = len(blocks)
    count, _, levd, latd = blocks[0].shape
    half = count // 2
    any_spec = pl.BlockSpec(memory_space=pl.ANY)
    return pl.pallas_call(
        functools.partial(gather_kernel, groups),
        out_shape=jax.ShapeDtypeStruct((groups, half, 2, levd, latd), BF16),
        grid=(1,),
        in_specs=[pl.BlockSpec((half, 2, levd, latd), lambda i: (1, 0, 0, 0))] * groups
        + [any_spec] * len(after),
        out_specs=pl.BlockSpec((groups, half, 2, levd, latd), lambda i: (0, 0, 0, 0, 0)),
        name="gather_halves",
    )(*blocks, *after)


def fill_kernel(groups, got, *refs):
    outs = refs[-groups:]
    for r in range(groups):
        outs[r][...] = got[r]


def fill_halves(blocks, got):
    groups, half, _, levd, latd = got.shape
    any_spec = pl.BlockSpec(memory_space=pl.ANY)
    return pl.pallas_call(
        functools.partial(fill_kernel, groups),
        out_shape=[jax.ShapeDtypeStruct(b.shape, b.dtype) for b in blocks],
        grid=(1,),
        in_specs=[pl.BlockSpec(got.shape, lambda i: (0, 0, 0, 0, 0))] + [any_spec] * groups,
        out_specs=[pl.BlockSpec((half, 2, levd, latd), lambda i: (1, 0, 0, 0))] * groups,
        input_output_aliases={r + 1: r for r in range(groups)},
        name="fill_halves",
    )(got, *blocks)


def inverse_kernel(counts, vb, latd, scale, add, *refs):
    tabs, refs = refs[: len(counts)], refs[len(counts) :]
    pieces, refs = refs[: sum(counts)], refs[sum(counts) :]
    partial = refs[0] if add else None
    out, scr, lhs = refs[-3:]
    nlon = tabs[0].shape[1]
    base, depth = 0, 0
    for tab, number in zip(tabs, counts):
        rows = tab.shape[0]
        per = rows // (2 * number)
        for g in range(number):
            for c in range(2):
                at = (base + c * (rows // 2) + g * per) * vb
                part = pieces[depth + g][:, c].astype(F32)
                scr[at : at + per * vb, :latd] = part.reshape(per * vb, latd)
        base += rows
        depth += number
    for v in range(vb):
        col = scr[pl.ds(v, base, stride=vb), :].astype(BF16)
        lhs[v * LANES : (v + 1) * LANES, :] = col.T
    step = 3 * LANES
    for j in range(0, nlon, step):
        cols = slice(j, j + step)
        grid, base = None, 0
        for tab in tabs:
            rows = tab.shape[0]
            term = jnp.dot(
                lhs[:, base : base + rows], tab[:, cols], preferred_element_type=F32
            )
            grid = term if grid is None else grid + term
            base += rows
        grid = grid * scale
        for v in range(vb):
            piece = grid[v * LANES : v * LANES + latd]
            if partial is not None:
                piece = piece + partial[v, :, cols]
            out[v, :, cols] = piece.astype(out.dtype)


def inverse_dft(sets, partial, scale, out_dtype, after):
    tabs = [tab for tab, _ in sets]
    pieces = [p for _, group in sets for p in group]
    levd, latd = pieces[0].shape[2:]
    nlon = tabs[0].shape[1]
    rows = sum(tab.shape[0] for tab in tabs)
    vb = 8
    grid_block = pl.BlockSpec((vb, latd, nlon), lambda i: (i, 0, 0))
    in_specs = [pl.BlockSpec(tab.shape, lambda i: (0, 0)) for tab in tabs] + [
        pl.BlockSpec((p.shape[0], 2, vb, latd), lambda i: (0, 0, i, 0)) for p in pieces
    ]
    args = [*tabs, *pieces]
    if partial is not None:
        in_specs.append(grid_block)
        args.append(partial)
    in_specs += [pl.BlockSpec(memory_space=pl.ANY)] * len(after)
    args += after
    counts = tuple(len(group) for _, group in sets)
    return pl.pallas_call(
        functools.partial(inverse_kernel, counts, vb, latd, scale, partial is not None),
        out_shape=jax.ShapeDtypeStruct((levd, latd, nlon), out_dtype),
        grid=(levd // vb,),
        in_specs=in_specs,
        out_specs=grid_block,
        scratch_shapes=[
            pltpu.VMEM((rows * vb, LANES), F32),
            pltpu.VMEM((vb * LANES, rows), BF16),
        ],
        cost_estimate=pl.CostEstimate(
            flops=2 * rows * levd * latd * nlon,
            bytes_accessed=2 * levd * latd * (nlon + rows) + 2 * rows * nlon,
            transcendentals=0,
        ),
        name="inverse_dft",
    )(*args)


def local_fast(
    parts,
    grid_state,
    lat_order,
    slot_wave,
    truncation,
    zonal_wind,
    zonal_rate,
    quad_weight,
    legendre,
    vert_modes,
    vert_project,
    mode_rates,
    thermal_matrix,
    pressure_matrix,
):
    levd, latd, nlon = grid_state.shape[1:]
    slots = legendre.shape[0]
    nmodes = slot_wave.shape[0]
    nlat = lat_order.shape[0]
    nlev = vert_modes.shape[0]
    lats, levs = lax.axis_size("lat"), lax.axis_size("lev")
    groups = lats * levs
    z, x, f = lax.axis_index("lat"), lax.axis_index("lev"), lax.axis_index("fld")
    me = z * levs + x
    starts = [sum(parts[:i]) for i in range(len(parts))]

    waves = slot_wave.reshape(groups, 2, slots // 2)
    waves = xor_order(xor_order(waves, me, 0), f, 1)
    my_lats = lax.dynamic_slice_in_dim(lat_order, z * latd, latd)
    hits = my_lats[:, None, None] == jnp.arange(nlat, dtype=jnp.int32)[None, None, :]
    zonal = jnp.stack([zonal_wind, zonal_rate, quad_weight * nlon ** (-0.5)], axis=0)
    per_lat = jnp.sum(jnp.where(hits, zonal[None], 0.0), axis=2)

    first = f == 0
    mix = jnp.dot(vert_project, thermal_matrix, precision=PRECISE)
    drop = -jnp.dot(pressure_matrix, vert_modes, precision=PRECISE)
    by_col = lambda m: xor_order(m.reshape(nlev, levs, levd), x, 1).reshape(nlev, nlev)
    by_row = lambda m: xor_order(m.reshape(levs, levd, nlev), x, 0).reshape(nlev, nlev)
    w1 = by_col(jnp.where(first, vert_project, mix)), by_col(jnp.where(first, mix, vert_project))
    w1 = jnp.concatenate(w1, axis=1)
    w2 = by_row(jnp.where(first, vert_modes, drop)), by_row(jnp.where(first, drop, vert_modes))
    w2 = jnp.concatenate(w2, axis=0)

    def three(w):
        hi = lax.reduce_precision(w, 8, 7)
        lo = (w - hi).astype(BF16)
        hi = hi.astype(BF16)
        return jnp.concatenate([hi, hi, lo], axis=1)

    w1, w2 = three(w1), three(w2)
    rates = mode_rates[:, None]
    lat_rel = xor_order(lat_order.reshape(lats, latd), z, 0)
    lat_rel = jnp.pad(lat_rel, ((0, 0), (0, LANES - latd)), constant_values=-1).reshape(-1, 1)
    perm = (lat_rel == jnp.arange(nlat, dtype=jnp.int32)[None, :]).astype(BF16)
    my_waves = waves[0, 0]
    counts = pick_values(my_waves, truncation) - my_waves + 1

    lat_lev = ("lat", "lev")

    def exchange(blocks, order):
        out = list(blocks)
        for r in order:
            if r:
                pairs = [(i, i ^ r) for i in range(groups)]
                out[r] = lax.ppermute(blocks[r], lat_lev, pairs)
        return out

    def swap(block):
        return lax.ppermute(block, "fld", [(0, 1), (1, 0)])

    far, near = far_near(groups)
    tables, arrived = [], []
    for at, part in zip(starts, parts):
        w = waves[:, :, at : at + part].reshape(-1)
        row = jnp.pad(w.astype(F32), (0, -w.shape[0] % LANES))[None, :]
        columns = make_column_tables(row, nlon)
        blocks = dft(grid_state[0], columns, per_lat, row, w.shape[0], groups)
        arrived.append(exchange(blocks, far + near))
        tables.append(make_table(w, nlon))
    legendre = jnp.swapaxes(legendre, 1, 2)
    returned = []
    after = [arrived[-1][0]]
    for i, (at, part) in enumerate(zip(starts, parts)):
        other = gather_halves(arrived[i], after)
        other = swap(other)
        info = jnp.stack(
            [
                my_waves[at : at + part],
                counts[at : at + part],
                jnp.full((part,), f, jnp.int32),
                jnp.full((part,), f * (slots // 2) + at, jnp.int32),
            ]
        )
        res = legendre_step(info, legendre, perm, w1, w2, rates, arrived[i], other, levs, nmodes)
        got = swap(res[groups])
        sent = fill_halves(res[:groups], got)
        after = [sent[0]]
        returned.append(exchange(sent, near + far))
    total = None
    last = len(parts) - 1
    for i in range(len(parts)):
        total = inverse_dft(
            [(tables[i], returned[i])],
            total,
            float(nmodes) ** (-0.5),
            BF16 if i == last else F32,
            [] if i == last else after,
        )
    return total[None]


def far_near(groups):
    rels = tuple(range(groups))
    return rels[groups // 2 :], rels[: groups // 2]


def power_of_two(n):
    return n & (n - 1) == 0


def solution(mesh):
    in_specs = (
        P(("member", "fld"), "lev", "lat", None),
        P(),
        P(),
        P(),
        P(),
        P(),
        P(),
        P(("lat", "lev"), None, None),
        P(),
        P(),
        P(),
        P(),
        P(),
    )
    out_specs = P(("member", "fld"), "lev", "lat", None)
    lats, levs = mesh.shape["lat"], mesh.shape["lev"]

    groups = lats * levs
    small = (
        mesh.shape["fld"] == 2 and power_of_two(lats) and power_of_two(levs) and 1 < groups <= 8
    )

    def local(grid_state, *rest):
        legendre = rest[6]
        levd, latd, nlon = grid_state.shape[1:]
        fits = (
            legendre.shape[0] % (4 * sum(SHARES)) == 0
            and levd % 8 == 0
            and latd % 8 == 0
            and latd <= LANES
            and nlon % (3 * LANES) == 0
            and nlon % 2 == 0
        )
        if small and fits:
            unit = legendre.shape[0] // (2 * sum(SHARES))
            return local_fast([unit * n for n in SHARES], grid_state, *rest)
        return local_general(grid_state, *rest)

    return jax.shard_map(local, mesh=mesh, in_specs=in_specs, out_specs=out_specs, check_vma=False)
```

```python
import functools

import jax
import jax.numpy as jnp
from jax import lax
from jax.experimental import pallas as pl
from jax.experimental.pallas import tpu as pltpu
from jax.sharding import PartitionSpec as P


PRECISE = lax.Precision.HIGHEST
BF16 = jnp.bfloat16
F32 = jnp.float32


def dft_table(wavenums, nlon):
    columns = jnp.arange(nlon, dtype=jnp.int32)
    turns = columns[:, None] * wavenums[None, :] % nlon
    angles = turns.astype(jnp.float32) * (2.0 * jnp.pi / nlon)
    return jnp.stack([jnp.cos(angles), -jnp.sin(angles)], axis=1).astype(jnp.bfloat16)


def pick_values(idents, source_table):
    hits = idents[:, None] == jnp.arange(source_table.shape[0], dtype=jnp.int32)[None, :]
    return jnp.sum(jnp.where(hits, source_table[None, :], 0), axis=1)


def layer_eigen_basis(matrix, columns):
    return jnp.einsum("skcj,ij->skci", columns, matrix, precision=PRECISE)


def analyse(legendre, fourier_data):
    return jnp.einsum("skl,slx->skx", legendre, fourier_data, preferred_element_type=jnp.float32)


def synthesise(legendre, coeffs):
    return jnp.einsum("skl,skx->slx", legendre, coeffs, preferred_element_type=jnp.float32)


def local_general(
    grid_state,
    lat_order,
    slot_wave,
    truncation,
    zonal_wind,
    zonal_rate,
    quad_weight,
    legendre,
    vert_modes,
    vert_project,
    mode_rates,
    thermal_into_spread_matrix,
    pressure_balance_matrix,
):
    levd, latd, nlon = (grid_state.shape[1], grid_state.shape[2], grid_state.shape[3])
    slots = legendre.shape[0]
    nmodes = slot_wave.shape[0]
    nlat = lat_order.shape[0]
    nlev = vert_modes.shape[0]
    lat_count = lax.axis_size("lat")
    lev_count = lax.axis_size("lev")
    lat_index = lax.axis_index("lat")
    lev_index = lax.axis_index("lev")
    unknown_position = lax.axis_index("fld")
    my_lats = lax.dynamic_slice_in_dim(lat_order, lat_index * latd, latd)
    onehot = (my_lats[:, None] == jnp.arange(nlat, dtype=jnp.int32)[None, :]).astype(jnp.float32)
    per_lat = jnp.dot(
        onehot, jnp.stack([zonal_wind, zonal_rate, quad_weight], axis=1), precision=PRECISE
    )
    values = grid_state[0].astype(jnp.float32)
    flux = (values * (per_lat[None, :, 0][:, :, None] + values)).astype(jnp.bfloat16)
    count_rows = levd * latd
    stacked = jnp.concatenate(
        [grid_state[0].reshape(count_rows, nlon), flux.reshape(count_rows, nlon)], axis=0
    )
    table = dft_table(slot_wave, nlon).reshape(nlon, 2 * nmodes)
    spectra = lax.dot_general(
        table, stacked, (((0,), (1,)), ((), ())), preferred_element_type=jnp.float32
    ) * nlon ** (-0.5)
    spectra = spectra.reshape(2, nmodes, 2 * count_rows)
    plain = spectra[:, :, :count_rows]
    moved = spectra[:, :, count_rows:]
    rate_row = jnp.tile(per_lat[:, 1], levd)[None, :]
    weight_row = jnp.tile(per_lat[:, 2], levd)[None, :]
    wave_float = slot_wave.astype(jnp.float32)[:, None]
    factor = rate_row * wave_float
    real_part = (plain[0] + factor * moved[1]) * weight_row
    imag_part = (plain[1] - factor * moved[0]) * weight_row
    fourier = jnp.stack([real_part, imag_part], axis=0).astype(jnp.bfloat16)
    arrived = lax.all_to_all(fourier, ("lat", "lev"), split_axis=1, concat_axis=2, tiled=True)
    arrived = arrived.reshape(2, slots, lat_count, lev_count, levd, latd)
    arranged = jnp.transpose(arrived, (1, 2, 5, 0, 3, 4))
    arranged = arranged.reshape(slots, nlat, 2 * nlev)
    position = jnp.zeros((nlat,), jnp.int32).at[lat_order].set(jnp.arange(nlat, dtype=jnp.int32))
    ordered = jnp.take(arranged, position, axis=1)
    owner_index = lat_index * lev_count + lev_index
    my_waves = lax.dynamic_slice_in_dim(slot_wave, owner_index * slots, slots)
    limits = pick_values(my_waves, truncation)
    counts = limits - my_waves + 1
    degree = jnp.arange(nmodes, dtype=jnp.int32)
    valid = (degree[None, :] < counts[:, None])[:, :, None]
    own_spec = jnp.where(valid, analyse(legendre, ordered), jnp.float32(0.0))
    joined_harmonic_unknowns = lax.all_gather(own_spec, "fld", axis=2, tiled=True)
    joined_harmonic_unknowns = joined_harmonic_unknowns.reshape(slots, nmodes, 2, 2, nlev)
    outflow_rate_coeffs = joined_harmonic_unknowns[:, :, 0]
    thermal_coeffs = joined_harmonic_unknowns[:, :, 1]
    n_deg = (my_waves[:, None] + degree[None, :]).astype(jnp.float32)
    elliptic_inverse_scale = (n_deg * (n_deg + 1.0) / (nmodes * (nmodes - 1)))[:, :, None, None]
    outflow_rate_source = outflow_rate_coeffs + elliptic_inverse_scale * layer_eigen_basis(
        thermal_into_spread_matrix, thermal_coeffs
    )
    projected = layer_eigen_basis(vert_project, outflow_rate_source) / (
        1.0 + elliptic_inverse_scale * mode_rates
    )
    outflow_rate_next = layer_eigen_basis(vert_modes, projected)
    thermal_next = thermal_coeffs - layer_eigen_basis(pressure_balance_matrix, outflow_rate_next)
    own_new = (
        jnp.where(unknown_position == 0, outflow_rate_next, thermal_next)
        .astype(jnp.bfloat16)
        .reshape(slots, nmodes, 2 * nlev)
    )
    back = synthesise(legendre, own_new) * nmodes ** (-0.5)
    back = jnp.take(back, lat_order, axis=1).astype(jnp.bfloat16)
    shaped = back.reshape(slots, lat_count, latd, 2, lev_count, levd)
    outgoing = jnp.transpose(shaped, (3, 0, 1, 4, 5, 2)).reshape(
        2, slots, lat_count * lev_count * count_rows
    )
    returned = lax.all_to_all(outgoing, ("lat", "lev"), split_axis=2, concat_axis=1, tiled=True)
    leading = returned.reshape(2 * nmodes, count_rows)
    grid_out = lax.dot_general(
        leading, table, (((0,), (1,)), ((), ())), preferred_element_type=jnp.float32
    ) * nmodes ** (-0.5)
    return grid_out.astype(jnp.bfloat16).reshape(1, levd, latd, nlon)


LANES = 128
LEVELS = 8
SHARES = (1, 1, 1)


def xor_order(array, index, axis):
    size = array.shape[axis]
    bits = size.bit_length() - 1
    shape = array.shape[:axis] + (2,) * bits + array.shape[axis + 1 :]
    out = array.reshape(shape)
    for b in range(bits):
        ax = axis + bits - 1 - b
        out = jnp.where((index >> b) & 1 == 1, jnp.flip(out, ax), out)
    return out.reshape(array.shape)


def packed_rows():
    return 2 * LEVELS - 1


def spare_lanes(row, last, latd):
    index, values = row
    share = LANES - latd
    lane = lax.broadcasted_iota(jnp.int32, values.shape, 1)
    turned = pltpu.roll(last, (latd - share * index) % LANES, 1)
    return jnp.where(lane < latd, values, turned)


def last_row(rows, latd):
    share = LANES - latd
    lane = lax.broadcasted_iota(jnp.int32, rows[0].shape, 1)
    out = jnp.zeros_like(rows[0])
    for i, row in enumerate(rows):
        turned = pltpu.roll(row, (share * i - latd) % LANES, 1)
        out = jnp.where((lane >= share * i) & (lane < share * (i + 1)), turned, out)
    return out


def table_kernel(nlon, wave_ref, out):
    rows = wave_ref.shape[0]
    nblk = nlon // LANES
    wave = wave_ref[...]
    lane = lax.broadcasted_iota(jnp.int32, (rows, LANES), 1)

    def sincos(step):
        turns = (lane * step).astype(F32) * wave
        turns = turns - nlon * jnp.floor(turns * (1.0 / nlon))
        turns = jnp.where(turns < 0.0, turns + nlon, turns)
        turns = jnp.where(turns >= nlon, turns - nlon, turns)
        angle = turns * (2.0 * jnp.pi / nlon)
        return jnp.cos(angle), jnp.sin(angle)

    cl, sl = sincos(1)
    ch, sh = sincos(LANES)
    for b in range(nblk):
        c, s = ch[:, b : b + 1], sh[:, b : b + 1]
        cols = slice(b * LANES, (b + 1) * LANES)
        out[:rows, cols] = (c * cl - s * sl).astype(BF16)
        out[rows:, cols] = (-(s * cl + c * sl)).astype(BF16)


def make_table(wave_lanes, nlon):
    return pl.pallas_call(
        functools.partial(table_kernel, nlon),
        out_shape=jax.ShapeDtypeStruct((2 * wave_lanes.shape[0], nlon), BF16),
        name="table",
    )(wave_lanes)


def dft_kernel(groups, latd, x_ref, t_ref, lat_ref, wave_ref, *rest):
    outs, (xf,) = rest[:groups], rest[groups:]
    rows = t_ref.shape[0]
    half = rows // 2
    per = half // groups
    nblk = x_ref.shape[2] // LANES

    @pl.when(pl.program_id(0) == 0)
    def _():
        xf[...] = jnp.zeros_like(xf)

    wind = jnp.broadcast_to(lat_ref[...].T[:latd, 0:1], (latd, LANES))
    wind = jnp.concatenate([wind] * nblk, axis=1)
    weight = lat_ref[2:3, :]
    factor = wave_ref[...] * lat_ref[1:2, :]

    def load(v):
        xv = x_ref[v]
        x32 = xv.astype(F32)
        xf[v % 2, 0:latd, :] = xv
        xf[v % 2, LANES : LANES + latd, :] = (x32 * (wind + x32)).astype(BF16)

    last = None
    load(LEVELS - 1)
    order = [LEVELS - 1, *range(LEVELS - 1)]
    for at, v in enumerate(order):
        if at + 1 < LEVELS:
            load(order[at + 1])
        both = lax.dot_general(
            t_ref[...], xf[v % 2], (((1,), (1,)), ((), ())), preferred_element_type=F32
        )
        plain, moved = both[:, :LANES], both[:, LANES:]
        real = (plain[:half] + factor * moved[half:]) * weight
        imag = (plain[half:] - factor * moved[:half]) * weight
        parts = [(v, real)]
        if last is None:
            last = imag
        else:
            parts.append((LEVELS + v, imag))
        for index, values in parts:
            full = spare_lanes((index, values), last, latd).astype(BF16)
            for g in range(groups):
                outs[g][index] = full[g * per : (g + 1) * per]


def dft(x, table, lat_rows, wave_lanes, groups):
    levd, latd, nlon = x.shape
    rows = table.shape[0]
    half = rows // 2
    per = half // groups
    packed = packed_rows()
    const = lambda i: (0, 0)
    block = pl.BlockSpec((packed, per, LANES), lambda i: (i, 0, 0))
    return pl.pallas_call(
        functools.partial(dft_kernel, groups, latd),
        out_shape=[jax.ShapeDtypeStruct((levd // LEVELS * packed, per, LANES), BF16)] * groups,
        grid=(levd // LEVELS,),
        in_specs=[
            pl.BlockSpec((LEVELS, latd, nlon), lambda i: (i, 0, 0)),
            pl.BlockSpec((rows, nlon), const),
            pl.BlockSpec(lat_rows.shape, const),
            pl.BlockSpec((half, LANES), const),
        ],
        out_specs=[block] * groups,
        scratch_shapes=[pltpu.VMEM((2, 2 * LANES, nlon), BF16)],
        cost_estimate=pl.CostEstimate(
            flops=4 * rows * levd * latd * nlon,
            bytes_accessed=2 * levd * latd * (nlon + rows) + 2 * rows * nlon,
            transcendentals=0,
        ),
        name="dft",
    )(x, table, lat_rows, wave_lanes)


def split3_dot(w3, x):
    hi = x.astype(BF16)
    lo = (x - hi.astype(F32)).astype(BF16)
    return jnp.dot(w3, jnp.concatenate([hi, lo, hi], axis=0), preferred_element_type=F32)


def legendre_kernel(
    groups, levs, levd, latd, nmodes, info, leg_ref, perm_ref, w1_ref, w2_ref, mr_ref, *rest
):
    own = rest[:groups]
    other = rest[groups]
    outs = rest[groups + 1 : 2 * groups + 1]
    give = rest[2 * groups + 1]
    data, fresh_data = rest[2 * groups + 2 :]
    slots = other.shape[2]
    lats = groups // levs
    nlev = levs * levd
    total = 4 * nlev
    count = leg_ref.shape[0]
    packed = packed_rows()
    t = pl.program_id(0)

    def each_group(move):
        def body(group, carry):
            for rel in range(groups):
                dz, dx = rel // levs, rel % levs
                for field in range(2):
                    base = field * nlev + dx * levd + group * LEVELS
                    rows = [
                        base + (i // LEVELS) * 2 * nlev + i % LEVELS for i in range(packed + 1)
                    ]
                    move(rel, field, dz, group * packed, rows)
            return carry

        lax.fori_loop(0, levd // LEVELS, body, 0)

    def unpack(rel, field, dz, at, rows):
        values = []
        for i in range(packed):
            value = own[rel][at + i, :slots] if field == 0 else other[rel, at + i]
            values.append(value.astype(F32))
        values.append(last_row(values, latd))
        for row, value in zip(rows, values):
            data[dz, pl.ds(row, slots, stride=total), :] = value

    def pack(rel, field, dz, at, rows):
        last = fresh_data[dz, pl.ds(rows[-1], slots, stride=total), :]
        for i in range(packed):
            value = fresh_data[dz, pl.ds(rows[i], slots, stride=total), :]
            full = spare_lanes((i, value), last, latd).astype(BF16)
            if field == 0:
                outs[rel][at + i] = full
            else:
                give[rel, at + i] = full

    @pl.when(t == 0)
    def _():
        each_group(unpack)

    k = lax.broadcasted_iota(jnp.int32, (1, nmodes), 1)
    first = info[2, 0] == 0
    keep_own = jnp.where(first, 0.0, 1.0)
    keep_other = jnp.where(first, 1.0, 0.0)
    legs = [
        jnp.dot(perm_ref[...], leg_ref[j], preferred_element_type=F32).astype(BF16)
        for j in range(count)
    ]
    fresh = []
    for j in range(count):
        slot = t * count + j
        wave, terms = info[0, slot], info[1, slot]
        n = (wave + k).astype(F32)
        h = n * (n + 1.0) / float(nmodes * (nmodes - 1))
        scale_own = jnp.where(first, 1.0, h)
        scale_other = jnp.where(first, h, 1.0)
        denom = 1.0 + h * mr_ref[...]
        here = pl.ds(pl.multiple_of(slot * total, total), total)
        lined = jnp.concatenate([data[dz, here, :].astype(BF16) for dz in range(lats)], axis=1)
        spec = jnp.dot(lined, legs[j], preferred_element_type=F32)
        spec = jnp.where(k < terms, spec, 0.0)
        new = []
        for c in range(2):
            a = spec[c * 2 * nlev : c * 2 * nlev + nlev]
            b = spec[c * 2 * nlev + nlev : (c + 1) * 2 * nlev]
            src = jnp.concatenate([a * scale_own, b * scale_other], axis=0)
            q = split3_dot(w1_ref[...], src) / denom
            both = split3_dot(w2_ref[...], q)
            new.append(both[:nlev] + keep_own * a)
            new.append(both[nlev:] + keep_other * b)
        fresh.append(jnp.concatenate(new, axis=0).astype(BF16))
    for j in range(count):
        back = lax.dot_general(
            fresh[j], legs[j], (((1,), (1,)), ((), ())), preferred_element_type=F32
        )
        here = pl.ds(pl.multiple_of((t * count + j) * total, total), total)
        back = back * float(nmodes) ** (-0.5)
        for dz in range(lats):
            fresh_data[dz, here, :] = back[:, dz * LANES : (dz + 1) * LANES]

    @pl.when(t == pl.num_programs(0) - 1)
    def _():
        each_group(pack)


def legendre_step(info, leg, perm, w1, w2, rates, own, other, levs, levd, latd):
    groups, packed, count, _ = other.shape
    nmodes = leg.shape[2]
    lanes, nlat = perm.shape
    nlev = levs * levd
    const = lambda t, s: (0, 0)
    step = 2 if count % 2 == 0 else 1
    piece = pl.BlockSpec((packed, count, LANES), lambda t, s: (0, 0, 0))
    stack = pl.BlockSpec((groups, packed, count, LANES), lambda t, s: (0, 0, 0, 0))
    flops = count * 2 * (2 * nlev * 2 * nmodes * lanes * 2 + nmodes * nlat * lanes)
    return pl.pallas_call(
        functools.partial(legendre_kernel, groups, levs, levd, latd, nmodes),
        out_shape=[jax.ShapeDtypeStruct((packed, 2 * count, LANES), BF16)] * groups
        + [jax.ShapeDtypeStruct(other.shape, BF16)],
        grid_spec=pltpu.PrefetchScalarGridSpec(
            num_scalar_prefetch=1,
            grid=(count // step,),
            in_specs=[
                pl.BlockSpec((step, nlat, nmodes), lambda t, s: (s[3, 0] // step + t, 0, 0)),
                pl.BlockSpec((lanes, nlat), const),
                pl.BlockSpec(w1.shape, const),
                pl.BlockSpec(w2.shape, const),
                pl.BlockSpec(rates.shape, const),
            ]
            + [piece] * groups
            + [stack],
            out_specs=[piece] * groups + [stack],
            scratch_shapes=[pltpu.VMEM((groups // levs, count * 4 * nlev, LANES), F32)] * 2,
        ),
        cost_estimate=pl.CostEstimate(
            flops=flops,
            bytes_accessed=count * 2 * (nmodes * nlat + 8 * nlev * lanes),
            transcendentals=0,
        ),
        name="legendre",
    )(info, leg, perm, w1, w2, rates, *own, other)


def gather_kernel(groups, *refs):
    ins, out = refs[:groups], refs[-1]
    for r in range(groups):
        out[r] = ins[r][...]


def gather_halves(blocks):
    groups = len(blocks)
    packed, count, _ = blocks[0].shape
    half = count // 2
    return pl.pallas_call(
        functools.partial(gather_kernel, groups),
        out_shape=jax.ShapeDtypeStruct((groups, packed, half, LANES), BF16),
        grid=(1,),
        in_specs=[pl.BlockSpec((packed, half, LANES), lambda i: (0, 1, 0))] * groups,
        out_specs=pl.BlockSpec((groups, packed, half, LANES), lambda i: (0, 0, 0, 0)),
        name="gather_halves",
    )(*blocks)


def fill_kernel(groups, got, *refs):
    outs = refs[-groups:]
    for r in range(groups):
        outs[r][...] = got[r]


def fill_halves(blocks, got):
    groups, packed, half, _ = got.shape
    any_spec = pl.BlockSpec(memory_space=pl.ANY)
    return pl.pallas_call(
        functools.partial(fill_kernel, groups),
        out_shape=[jax.ShapeDtypeStruct(b.shape, b.dtype) for b in blocks],
        grid=(1,),
        in_specs=[pl.BlockSpec(got.shape, lambda i: (0, 0, 0, 0))] + [any_spec] * groups,
        out_specs=[pl.BlockSpec((packed, half, LANES), lambda i: (0, 1, 0))] * groups,
        input_output_aliases={r + 1: r for r in range(groups)},
        name="fill_halves",
    )(got, *blocks)


def inverse_kernel(counts, latd, scale, add, *refs):
    tabs, refs = refs[: len(counts)], refs[len(counts) :]
    pieces, refs = refs[: sum(counts)], refs[sum(counts) :]
    partial = refs[0] if add else None
    out, lhs = refs[-2:]
    nlon = tabs[0].shape[1]
    packed = packed_rows()
    base, depth = 0, 0
    for tab, number in zip(tabs, counts):
        half = tab.shape[0] // 2
        group = pieces[depth : depth + number]
        for i in range(packed):
            v, c = i % LEVELS, i // LEVELS
            rows = jnp.concatenate([ref[i] for ref in group], axis=0)
            at = base + c * half
            lhs[v * LANES : (v + 1) * LANES, at : at + half] = rows.T
        rows = [
            jnp.concatenate([ref[i].astype(F32) for ref in group], axis=0) for i in range(packed)
        ]
        v = LEVELS - 1
        lhs[v * LANES : (v + 1) * LANES, base + half : base + 2 * half] = (
            last_row(rows, latd).astype(BF16).T
        )
        base += 2 * half
        depth += number
    step = 3 * LANES
    for j in range(0, nlon, step):
        cols = slice(j, j + step)
        grid, base = None, 0
        for tab in tabs:
            rows = tab.shape[0]
            term = jnp.dot(
                lhs[:, base : base + rows], tab[:, cols], preferred_element_type=F32
            )
            grid = term if grid is None else grid + term
            base += rows
        grid = grid * scale
        for v in range(LEVELS):
            piece = grid[v * LANES : v * LANES + latd]
            if partial is not None:
                piece = piece + partial[v, :, cols]
            out[v, :, cols] = piece.astype(out.dtype)


def inverse_dft(sets, shape, partial, scale, out_dtype):
    tabs = [tab for tab, _ in sets]
    pieces = [p for _, group in sets for p in group]
    levd, latd, nlon = shape
    rows = sum(tab.shape[0] for tab in tabs)
    packed = packed_rows()
    grid_block = pl.BlockSpec((LEVELS, latd, nlon), lambda i: (i, 0, 0))
    in_specs = [pl.BlockSpec(tab.shape, lambda i: (0, 0)) for tab in tabs] + [
        pl.BlockSpec((packed, p.shape[1], LANES), lambda i: (i, 0, 0)) for p in pieces
    ]
    args = [*tabs, *pieces]
    if partial is not None:
        in_specs.append(grid_block)
        args.append(partial)
    counts = tuple(len(group) for _, group in sets)
    return pl.pallas_call(
        functools.partial(inverse_kernel, counts, latd, scale, partial is not None),
        out_shape=jax.ShapeDtypeStruct((levd, latd, nlon), out_dtype),
        grid=(levd // LEVELS,),
        in_specs=in_specs,
        out_specs=grid_block,
        scratch_shapes=[pltpu.VMEM((LEVELS * LANES, rows), BF16)],
        cost_estimate=pl.CostEstimate(
            flops=2 * rows * levd * latd * nlon,
            bytes_accessed=2 * levd * latd * (nlon + rows) + 2 * rows * nlon,
            transcendentals=0,
        ),
        name="inverse_dft",
    )(*args)


def local_fast(
    parts,
    grid_state,
    lat_order,
    slot_wave,
    truncation,
    zonal_wind,
    zonal_rate,
    quad_weight,
    legendre,
    vert_modes,
    vert_project,
    mode_rates,
    thermal_matrix,
    pressure_matrix,
):
    levd, latd, nlon = grid_state.shape[1:]
    slots = legendre.shape[0]
    nmodes = slot_wave.shape[0]
    nlat = lat_order.shape[0]
    nlev = vert_modes.shape[0]
    lats, levs = lax.axis_size("lat"), lax.axis_size("lev")
    groups = lats * levs
    z, x, f = lax.axis_index("lat"), lax.axis_index("lev"), lax.axis_index("fld")
    me = z * levs + x
    starts = [sum(parts[:i]) for i in range(len(parts))]

    waves = slot_wave.reshape(groups, 2, slots // 2)
    waves = xor_order(xor_order(waves, me, 0), f, 1)
    lat_rel = xor_order(lat_order.reshape(lats, latd), z, 0)
    lat_rel = jnp.pad(lat_rel, ((0, 0), (0, LANES - latd)), constant_values=-1)
    hits = lat_rel[0][None, :, None] == jnp.arange(nlat, dtype=jnp.int32)[None, None, :]
    zonal = jnp.stack([zonal_wind, zonal_rate, quad_weight * nlon ** (-0.5)], axis=0)
    lat_rows = jnp.sum(jnp.where(hits, zonal[:, None, :], 0.0), axis=2)
    lat_rows = jnp.pad(lat_rows, ((0, 5), (0, 0)))

    first = f == 0
    mix = jnp.dot(vert_project, thermal_matrix, precision=PRECISE)
    drop = -jnp.dot(pressure_matrix, vert_modes, precision=PRECISE)
    by_col = lambda m: xor_order(m.reshape(nlev, levs, levd), x, 1).reshape(nlev, nlev)
    by_row = lambda m: xor_order(m.reshape(levs, levd, nlev), x, 0).reshape(nlev, nlev)
    w1 = by_col(jnp.where(first, vert_project, mix)), by_col(jnp.where(first, mix, vert_project))
    w1 = jnp.concatenate(w1, axis=1)
    w2 = by_row(jnp.where(first, vert_modes, drop)), by_row(jnp.where(first, drop, vert_modes))
    w2 = jnp.concatenate(w2, axis=0)

    def three(w):
        hi = lax.reduce_precision(w, 8, 7)
        lo = (w - hi).astype(BF16)
        hi = hi.astype(BF16)
        return jnp.concatenate([hi, hi, lo], axis=1)

    w1, w2 = three(w1), three(w2)
    rates = mode_rates[:, None]
    perm = (lat_rel.reshape(-1, 1) == jnp.arange(nlat, dtype=jnp.int32)[None, :]).astype(BF16)
    my_waves = waves[0, 0]
    counts = pick_values(my_waves, truncation) - my_waves + 1

    lat_lev = ("lat", "lev")

    def exchange(blocks, order):
        out = list(blocks)
        for r in order:
            if r:
                pairs = [(i, i ^ r) for i in range(groups)]
                out[r] = lax.ppermute(blocks[r], lat_lev, pairs)
        return out

    def swap(block):
        return lax.ppermute(block, "fld", [(0, 1), (1, 0)])

    far, near = far_near(groups)
    tables, arrived = [], []
    for i, (at, part) in enumerate(zip(starts, parts)):
        w = waves[:, :, at : at + part].reshape(-1)
        lanes = jnp.broadcast_to(w.astype(F32)[:, None], (w.shape[0], LANES))
        tables.append(make_table(lanes, nlon))
        blocks = dft(grid_state[0], tables[i], lat_rows, lanes, groups)
        arrived.append(exchange(blocks, far + near))
    legendre = jnp.swapaxes(legendre, 1, 2)
    returned = []
    for i, (at, part) in enumerate(zip(starts, parts)):
        other = gather_halves(arrived[i])
        other = swap(other)
        info = jnp.stack(
            [
                my_waves[at : at + part],
                counts[at : at + part],
                jnp.full((part,), f, jnp.int32),
                jnp.full((part,), f * (slots // 2) + at, jnp.int32),
            ]
        )
        res = legendre_step(
            info, legendre, perm, w1, w2, rates, arrived[i], other, levs, levd, latd
        )
        got = swap(res[groups])
        sent = fill_halves(res[:groups], got)
        returned.append(exchange(sent, near + far))
    sets = list(zip(tables, returned))
    scale = float(nmodes) ** (-0.5)
    shape = (levd, latd, nlon)
    total = inverse_dft(sets[:-1], shape, None, scale, F32)
    total = inverse_dft(sets[-1:], shape, total, scale, BF16)
    return total[None]


def far_near(groups):
    rels = tuple(range(groups))
    return rels[groups // 2 :], rels[: groups // 2]


def power_of_two(n):
    return n & (n - 1) == 0


def solution(mesh):
    in_specs = (
        P(("member", "fld"), "lev", "lat", None),
        P(),
        P(),
        P(),
        P(),
        P(),
        P(),
        P(("lat", "lev"), None, None),
        P(),
        P(),
        P(),
        P(),
        P(),
    )
    out_specs = P(("member", "fld"), "lev", "lat", None)
    lats, levs = mesh.shape["lat"], mesh.shape["lev"]

    groups = lats * levs
    small = (
        mesh.shape["fld"] == 2 and power_of_two(lats) and power_of_two(levs) and 1 < groups <= 8
    )

    def local(grid_state, *rest):
        legendre = rest[6]
        levd, latd, nlon = grid_state.shape[1:]
        share = LANES - latd
        fits = (
            legendre.shape[0] % (2 * 8 * sum(SHARES)) == 0
            and levd % LEVELS == 0
            and latd % 8 == 0
            and share > 0
            and share * (2 * LEVELS - 1) == latd
            and nlon % (3 * LANES) == 0
        )
        if small and fits:
            unit = legendre.shape[0] // (2 * sum(SHARES))
            return local_fast([unit * n for n in SHARES], grid_state, *rest)
        return local_general(grid_state, *rest)

    return jax.shard_map(local, mesh=mesh, in_specs=in_specs, out_specs=out_specs, check_vma=False)
```

```python
import functools

import jax
import jax.numpy as jnp
from jax import lax
from jax.experimental import pallas as pl
from jax.experimental.pallas import tpu as pltpu
from jax.sharding import PartitionSpec as P


PRECISE = lax.Precision.HIGHEST
BF16 = jnp.bfloat16
F32 = jnp.float32


def dft_table(wavenums, nlon):
    columns = jnp.arange(nlon, dtype=jnp.int32)
    turns = columns[:, None] * wavenums[None, :] % nlon
    angles = turns.astype(jnp.float32) * (2.0 * jnp.pi / nlon)
    return jnp.stack([jnp.cos(angles), -jnp.sin(angles)], axis=1).astype(jnp.bfloat16)


def pick_values(idents, source_table):
    hits = idents[:, None] == jnp.arange(source_table.shape[0], dtype=jnp.int32)[None, :]
    return jnp.sum(jnp.where(hits, source_table[None, :], 0), axis=1)


def layer_eigen_basis(matrix, columns):
    return jnp.einsum("skcj,ij->skci", columns, matrix, precision=PRECISE)


def analyse(legendre, fourier_data):
    return jnp.einsum("skl,slx->skx", legendre, fourier_data, preferred_element_type=jnp.float32)


def synthesise(legendre, coeffs):
    return jnp.einsum("skl,skx->slx", legendre, coeffs, preferred_element_type=jnp.float32)


def local_general(
    grid_state,
    lat_order,
    slot_wave,
    truncation,
    zonal_wind,
    zonal_rate,
    quad_weight,
    legendre,
    vert_modes,
    vert_project,
    mode_rates,
    thermal_into_spread_matrix,
    pressure_balance_matrix,
):
    levd, latd, nlon = (grid_state.shape[1], grid_state.shape[2], grid_state.shape[3])
    slots = legendre.shape[0]
    nmodes = slot_wave.shape[0]
    nlat = lat_order.shape[0]
    nlev = vert_modes.shape[0]
    lat_count = lax.axis_size("lat")
    lev_count = lax.axis_size("lev")
    lat_index = lax.axis_index("lat")
    lev_index = lax.axis_index("lev")
    unknown_position = lax.axis_index("fld")
    my_lats = lax.dynamic_slice_in_dim(lat_order, lat_index * latd, latd)
    onehot = (my_lats[:, None] == jnp.arange(nlat, dtype=jnp.int32)[None, :]).astype(jnp.float32)
    per_lat = jnp.dot(
        onehot, jnp.stack([zonal_wind, zonal_rate, quad_weight], axis=1), precision=PRECISE
    )
    values = grid_state[0].astype(jnp.float32)
    flux = (values * (per_lat[None, :, 0][:, :, None] + values)).astype(jnp.bfloat16)
    count_rows = levd * latd
    stacked = jnp.concatenate(
        [grid_state[0].reshape(count_rows, nlon), flux.reshape(count_rows, nlon)], axis=0
    )
    table = dft_table(slot_wave, nlon).reshape(nlon, 2 * nmodes)
    spectra = lax.dot_general(
        table, stacked, (((0,), (1,)), ((), ())), preferred_element_type=jnp.float32
    ) * nlon ** (-0.5)
    spectra = spectra.reshape(2, nmodes, 2 * count_rows)
    plain = spectra[:, :, :count_rows]
    moved = spectra[:, :, count_rows:]
    rate_row = jnp.tile(per_lat[:, 1], levd)[None, :]
    weight_row = jnp.tile(per_lat[:, 2], levd)[None, :]
    wave_float = slot_wave.astype(jnp.float32)[:, None]
    factor = rate_row * wave_float
    real_part = (plain[0] + factor * moved[1]) * weight_row
    imag_part = (plain[1] - factor * moved[0]) * weight_row
    fourier = jnp.stack([real_part, imag_part], axis=0).astype(jnp.bfloat16)
    arrived = lax.all_to_all(fourier, ("lat", "lev"), split_axis=1, concat_axis=2, tiled=True)
    arrived = arrived.reshape(2, slots, lat_count, lev_count, levd, latd)
    arranged = jnp.transpose(arrived, (1, 2, 5, 0, 3, 4))
    arranged = arranged.reshape(slots, nlat, 2 * nlev)
    position = jnp.zeros((nlat,), jnp.int32).at[lat_order].set(jnp.arange(nlat, dtype=jnp.int32))
    ordered = jnp.take(arranged, position, axis=1)
    owner_index = lat_index * lev_count + lev_index
    my_waves = lax.dynamic_slice_in_dim(slot_wave, owner_index * slots, slots)
    limits = pick_values(my_waves, truncation)
    counts = limits - my_waves + 1
    degree = jnp.arange(nmodes, dtype=jnp.int32)
    valid = (degree[None, :] < counts[:, None])[:, :, None]
    own_spec = jnp.where(valid, analyse(legendre, ordered), jnp.float32(0.0))
    joined_harmonic_unknowns = lax.all_gather(own_spec, "fld", axis=2, tiled=True)
    joined_harmonic_unknowns = joined_harmonic_unknowns.reshape(slots, nmodes, 2, 2, nlev)
    outflow_rate_coeffs = joined_harmonic_unknowns[:, :, 0]
    thermal_coeffs = joined_harmonic_unknowns[:, :, 1]
    n_deg = (my_waves[:, None] + degree[None, :]).astype(jnp.float32)
    elliptic_inverse_scale = (n_deg * (n_deg + 1.0) / (nmodes * (nmodes - 1)))[:, :, None, None]
    outflow_rate_source = outflow_rate_coeffs + elliptic_inverse_scale * layer_eigen_basis(
        thermal_into_spread_matrix, thermal_coeffs
    )
    projected = layer_eigen_basis(vert_project, outflow_rate_source) / (
        1.0 + elliptic_inverse_scale * mode_rates
    )
    outflow_rate_next = layer_eigen_basis(vert_modes, projected)
    thermal_next = thermal_coeffs - layer_eigen_basis(pressure_balance_matrix, outflow_rate_next)
    own_new = (
        jnp.where(unknown_position == 0, outflow_rate_next, thermal_next)
        .astype(jnp.bfloat16)
        .reshape(slots, nmodes, 2 * nlev)
    )
    back = synthesise(legendre, own_new) * nmodes ** (-0.5)
    back = jnp.take(back, lat_order, axis=1).astype(jnp.bfloat16)
    shaped = back.reshape(slots, lat_count, latd, 2, lev_count, levd)
    outgoing = jnp.transpose(shaped, (3, 0, 1, 4, 5, 2)).reshape(
        2, slots, lat_count * lev_count * count_rows
    )
    returned = lax.all_to_all(outgoing, ("lat", "lev"), split_axis=2, concat_axis=1, tiled=True)
    leading = returned.reshape(2 * nmodes, count_rows)
    grid_out = lax.dot_general(
        leading, table, (((0,), (1,)), ((), ())), preferred_element_type=jnp.float32
    ) * nmodes ** (-0.5)
    return grid_out.astype(jnp.bfloat16).reshape(1, levd, latd, nlon)


LANES = 128
LEVELS = 8
SHARES = (1, 1)


def xor_order(array, index, axis):
    size = array.shape[axis]
    bits = size.bit_length() - 1
    shape = array.shape[:axis] + (2,) * bits + array.shape[axis + 1 :]
    out = array.reshape(shape)
    for b in range(bits):
        ax = axis + bits - 1 - b
        out = jnp.where((index >> b) & 1 == 1, jnp.flip(out, ax), out)
    return out.reshape(array.shape)


def packed_rows():
    return 2 * LEVELS - 1


def spare_lanes(row, last, latd):
    index, values = row
    share = LANES - latd
    lane = lax.broadcasted_iota(jnp.int32, values.shape, 1)
    turned = pltpu.roll(last, (latd - share * index) % LANES, 1)
    return jnp.where(lane < latd, values, turned)


def last_row(rows, latd):
    share = LANES - latd
    lane = lax.broadcasted_iota(jnp.int32, rows[0].shape, 1)
    out = jnp.zeros_like(rows[0])
    for i, row in enumerate(rows):
        turned = pltpu.roll(row, (share * i - latd) % LANES, 1)
        out = jnp.where((lane >= share * i) & (lane < share * (i + 1)), turned, out)
    return out


def table_kernel(nlon, wave_ref, out):
    rows = wave_ref.shape[0]
    nblk = nlon // LANES
    wave = wave_ref[...]
    lane = lax.broadcasted_iota(jnp.int32, (rows, LANES), 1)

    def sincos(step):
        turns = (lane * step).astype(F32) * wave
        turns = turns - nlon * jnp.floor(turns * (1.0 / nlon))
        turns = jnp.where(turns < 0.0, turns + nlon, turns)
        turns = jnp.where(turns >= nlon, turns - nlon, turns)
        angle = turns * (2.0 * jnp.pi / nlon)
        return jnp.cos(angle), jnp.sin(angle)

    cl, sl = sincos(1)
    ch, sh = sincos(LANES)
    for b in range(nblk):
        c, s = ch[:, b : b + 1], sh[:, b : b + 1]
        cols = slice(b * LANES, (b + 1) * LANES)
        out[:rows, cols] = (c * cl - s * sl).astype(BF16)
        out[rows:, cols] = (-(s * cl + c * sl)).astype(BF16)


def make_table(wave_lanes, nlon):
    return pl.pallas_call(
        functools.partial(table_kernel, nlon),
        out_shape=jax.ShapeDtypeStruct((2 * wave_lanes.shape[0], nlon), BF16),
        name="table",
    )(wave_lanes)


def dft_kernel(groups, latd, x_ref, t_ref, lat_ref, wave_ref, *rest):
    outs, (xf,) = rest[:groups], rest[groups:]
    rows = t_ref.shape[0]
    half = rows // 2
    per = half // groups
    nblk = x_ref.shape[2] // LANES

    @pl.when(pl.program_id(0) == 0)
    def _():
        xf[...] = jnp.zeros_like(xf)

    wind = jnp.broadcast_to(lat_ref[...].T[:latd, 0:1], (latd, LANES))
    wind = jnp.concatenate([wind] * nblk, axis=1)
    weight = lat_ref[2:3, :]
    factor = wave_ref[...] * lat_ref[1:2, :]

    def load(v):
        xv = x_ref[v]
        x32 = xv.astype(F32)
        xf[v % 2, 0:latd, :] = xv
        xf[v % 2, LANES : LANES + latd, :] = (x32 * (wind + x32)).astype(BF16)

    last = None
    load(LEVELS - 1)
    order = [LEVELS - 1, *range(LEVELS - 1)]
    for at, v in enumerate(order):
        if at + 1 < LEVELS:
            load(order[at + 1])
        both = lax.dot_general(
            t_ref[...], xf[v % 2], (((1,), (1,)), ((), ())), preferred_element_type=F32
        )
        plain, moved = both[:, :LANES], both[:, LANES:]
        real = (plain[:half] + factor * moved[half:]) * weight
        imag = (plain[half:] - factor * moved[:half]) * weight
        parts = [(v, real)]
        if last is None:
            last = imag
        else:
            parts.append((LEVELS + v, imag))
        for index, values in parts:
            full = spare_lanes((index, values), last, latd)
            for g in range(groups):
                outs[g][index] = full[g * per : (g + 1) * per].astype(BF16)


def dft(x, table, lat_rows, wave_lanes, groups):
    levd, latd, nlon = x.shape
    rows = table.shape[0]
    half = rows // 2
    per = half // groups
    packed = packed_rows()
    const = lambda i: (0, 0)
    block = pl.BlockSpec((packed, per, LANES), lambda i: (i, 0, 0))
    return pl.pallas_call(
        functools.partial(dft_kernel, groups, latd),
        out_shape=[jax.ShapeDtypeStruct((levd // LEVELS * packed, per, LANES), BF16)] * groups,
        grid=(levd // LEVELS,),
        in_specs=[
            pl.BlockSpec((LEVELS, latd, nlon), lambda i: (i, 0, 0)),
            pl.BlockSpec((rows, nlon), const),
            pl.BlockSpec(lat_rows.shape, const),
            pl.BlockSpec((half, LANES), const),
        ],
        out_specs=[block] * groups,
        scratch_shapes=[pltpu.VMEM((2, 2 * LANES, nlon), BF16)],
        cost_estimate=pl.CostEstimate(
            flops=4 * rows * levd * latd * nlon,
            bytes_accessed=2 * levd * latd * (nlon + rows) + 2 * rows * nlon,
            transcendentals=0,
        ),
        name="dft",
    )(x, table, lat_rows, wave_lanes)


def split3_dot(w3, x):
    hi = x.astype(BF16)
    lo = (x - hi.astype(F32)).astype(BF16)
    return jnp.dot(w3, jnp.concatenate([hi, lo, hi], axis=0), preferred_element_type=F32)


def legendre_kernel(
    groups, levs, levd, latd, nmodes, info, leg_ref, perm_ref, w1_ref, w2_ref, mr_ref, *rest
):
    own = rest[:groups]
    other = rest[groups]
    outs = rest[groups + 1 : 2 * groups + 1]
    give = rest[2 * groups + 1]
    data, fresh_data = rest[2 * groups + 2 :]
    slots = outs[0].shape[1]
    lats = groups // levs
    nlev = levs * levd
    total = 4 * nlev
    count = leg_ref.shape[0]
    packed = packed_rows()
    t = pl.program_id(0)

    def each_group(move):
        def body(group, carry):
            for rel in range(groups):
                dz, dx = rel // levs, rel % levs
                for field in range(2):
                    base = field * nlev + dx * levd + group * LEVELS
                    rows = [
                        base + (i // LEVELS) * 2 * nlev + i % LEVELS for i in range(packed + 1)
                    ]
                    move(rel, field, dz, group * packed, rows)
            return carry

        lax.fori_loop(0, levd // LEVELS, body, 0)

    def unpack(rel, field, dz, at, rows):
        values = []
        for i in range(packed):
            value = own[rel][at + i] if field == 0 else other[rel, at + i]
            values.append(value.astype(F32)[:slots])
        values.append(last_row(values, latd))
        for row, value in zip(rows, values):
            data[dz, pl.ds(row, slots, stride=total), :] = value

    def pack(rel, field, dz, at, rows):
        last = fresh_data[dz, pl.ds(rows[-1], slots, stride=total), :]
        for i in range(packed):
            value = fresh_data[dz, pl.ds(rows[i], slots, stride=total), :]
            full = spare_lanes((i, value), last, latd).astype(BF16)
            if field == 0:
                outs[rel][at + i] = full
            else:
                give[rel, at + i, :slots] = full

    @pl.when(t == 0)
    def _():
        each_group(unpack)

    k = lax.broadcasted_iota(jnp.int32, (1, nmodes), 1)
    first = info[2, 0] == 0
    keep_own = jnp.where(first, 0.0, 1.0)
    keep_other = jnp.where(first, 1.0, 0.0)
    legs = [
        jnp.dot(perm_ref[...], leg_ref[j], preferred_element_type=F32).astype(BF16)
        for j in range(count)
    ]
    fresh = []
    for j in range(count):
        slot = t * count + j
        wave, terms = info[0, slot], info[1, slot]
        n = (wave + k).astype(F32)
        h = n * (n + 1.0) / float(nmodes * (nmodes - 1))
        scale_own = jnp.where(first, 1.0, h)
        scale_other = jnp.where(first, h, 1.0)
        denom = 1.0 + h * mr_ref[...]
        here = pl.ds(pl.multiple_of(slot * total, total), total)
        lined = jnp.concatenate([data[dz, here, :].astype(BF16) for dz in range(lats)], axis=1)
        spec = jnp.dot(lined, legs[j], preferred_element_type=F32)
        spec = jnp.where(k < terms, spec, 0.0)
        new = []
        for c in range(2):
            a = spec[c * 2 * nlev : c * 2 * nlev + nlev]
            b = spec[c * 2 * nlev + nlev : (c + 1) * 2 * nlev]
            src = jnp.concatenate([a * scale_own, b * scale_other], axis=0)
            q = split3_dot(w1_ref[...], src) / denom
            both = split3_dot(w2_ref[...], q)
            new.append(both[:nlev] + keep_own * a)
            new.append(both[nlev:] + keep_other * b)
        fresh.append(jnp.concatenate(new, axis=0).astype(BF16))
    for j in range(count):
        back = lax.dot_general(
            fresh[j], legs[j], (((1,), (1,)), ((), ())), preferred_element_type=F32
        )
        here = pl.ds(pl.multiple_of((t * count + j) * total, total), total)
        back = back * float(nmodes) ** (-0.5)
        for dz in range(lats):
            fresh_data[dz, here, :] = back[:, dz * LANES : (dz + 1) * LANES]

    @pl.when(t == pl.num_programs(0) - 1)
    def _():
        each_group(pack)


def legendre_step(info, leg, perm, w1, w2, rates, own, other, levs, levd, latd):
    groups, packed, rows, _ = other.shape
    count = own[0].shape[1] // 2
    nmodes = leg.shape[2]
    lanes, nlat = perm.shape
    nlev = levs * levd
    const = lambda t, s: (0, 0)
    step = 2 if count % 2 == 0 else 1
    piece = pl.BlockSpec((packed, 2 * count, LANES), lambda t, s: (0, 0, 0))
    half = pl.BlockSpec((packed, count, LANES), lambda t, s: (0, 0, 0))
    stack = pl.BlockSpec((groups, packed, rows, LANES), lambda t, s: (0, 0, 0, 0))
    flops = count * 2 * (2 * nlev * 2 * nmodes * lanes * 2 + nmodes * nlat * lanes)
    return pl.pallas_call(
        functools.partial(legendre_kernel, groups, levs, levd, latd, nmodes),
        out_shape=[jax.ShapeDtypeStruct((packed, count, LANES), BF16)] * groups
        + [jax.ShapeDtypeStruct(other.shape, BF16)],
        grid_spec=pltpu.PrefetchScalarGridSpec(
            num_scalar_prefetch=1,
            grid=(count // step,),
            in_specs=[
                pl.BlockSpec((step, nlat, nmodes), lambda t, s: (s[3, 0] // step + t, 0, 0)),
                pl.BlockSpec((lanes, nlat), const),
                pl.BlockSpec(w1.shape, const),
                pl.BlockSpec(w2.shape, const),
                pl.BlockSpec(rates.shape, const),
            ]
            + [piece] * groups
            + [stack],
            out_specs=[half] * groups + [stack],
            scratch_shapes=[pltpu.VMEM((groups // levs, count * 4 * nlev, LANES), F32)] * 2,
        ),
        cost_estimate=pl.CostEstimate(
            flops=flops,
            bytes_accessed=count * 2 * (nmodes * nlat + 8 * nlev * lanes),
            transcendentals=0,
        ),
        name="legendre",
    )(info, leg, perm, w1, w2, rates, *own, other)


def gather_kernel(groups, *refs):
    ins, out = refs[:groups], refs[-1]
    half = ins[0].shape[1] // 2
    for r in range(groups):
        out[r, :, :half] = ins[r][...].astype(F32)[:, half:].astype(BF16)


def padded(rows):
    return -(-rows // 8) * 8


def gather_halves(blocks):
    groups = len(blocks)
    packed, count, _ = blocks[0].shape
    half = padded(count // 2)
    group = packed_rows()
    return pl.pallas_call(
        functools.partial(gather_kernel, groups),
        out_shape=jax.ShapeDtypeStruct((groups, packed, half, LANES), BF16),
        grid=(packed // group,),
        in_specs=[pl.BlockSpec((group, count, LANES), lambda i: (i, 0, 0))] * groups,
        out_specs=pl.BlockSpec((groups, group, half, LANES), lambda i: (0, i, 0, 0)),
        name="gather_halves",
    )(*blocks)


def fill_kernel(groups, got, *refs):
    ins, outs = refs[:groups], refs[groups:]
    half = ins[0].shape[1]
    for r in range(groups):
        both = [ins[r][...].astype(F32), got[r].astype(F32)[:, :half]]
        outs[r][...] = jnp.concatenate(both, axis=1).astype(BF16)


def fill_halves(blocks, got):
    groups, packed, rows, _ = got.shape
    half = blocks[0].shape[1]
    group = packed_rows()
    return pl.pallas_call(
        functools.partial(fill_kernel, groups),
        out_shape=[jax.ShapeDtypeStruct((packed, 2 * half, LANES), BF16)] * groups,
        grid=(packed // group,),
        in_specs=[pl.BlockSpec((groups, group, rows, LANES), lambda i: (0, i, 0, 0))]
        + [pl.BlockSpec((group, half, LANES), lambda i: (i, 0, 0))] * groups,
        out_specs=[pl.BlockSpec((group, 2 * half, LANES), lambda i: (i, 0, 0))] * groups,
        name="fill_halves",
    )(got, *blocks)


def inverse_kernel(counts, latd, scale, add, *refs):
    tabs, refs = refs[: len(counts)], refs[len(counts) :]
    pieces, refs = refs[: sum(counts)], refs[sum(counts) :]
    partial = refs[0] if add else None
    out, lhs = refs[-2:]
    nlon = tabs[0].shape[1]
    packed = packed_rows()
    base, depth = 0, 0
    for tab, number in zip(tabs, counts):
        half = tab.shape[0] // 2
        group = pieces[depth : depth + number]
        rows = [
            jnp.concatenate([ref[i].astype(F32) for ref in group], axis=0) for i in range(packed)
        ]
        rows.append(last_row(rows, latd))
        for i, row in enumerate(rows):
            v, at = i % LEVELS, base + i // LEVELS * half
            lhs[v * LANES : (v + 1) * LANES, at : at + half] = row.astype(BF16).T
        base += 2 * half
        depth += number
    step = 3 * LANES
    for j in range(0, nlon, step):
        cols = slice(j, j + step)
        grid, base = None, 0
        for tab in tabs:
            rows = tab.shape[0]
            term = jnp.dot(
                lhs[:, base : base + rows], tab[:, cols], preferred_element_type=F32
            )
            grid = term if grid is None else grid + term
            base += rows
        grid = grid * scale
        for v in range(LEVELS):
            piece = grid[v * LANES : v * LANES + latd]
            if partial is not None:
                piece = piece + partial[v, :, cols]
            out[v, :, cols] = piece.astype(out.dtype)


def inverse_dft(sets, shape, partial, scale, out_dtype):
    tabs = [tab for tab, _ in sets]
    pieces = [p for _, group in sets for p in group]
    levd, latd, nlon = shape
    rows = sum(tab.shape[0] for tab in tabs)
    packed = packed_rows()
    grid_block = pl.BlockSpec((LEVELS, latd, nlon), lambda i: (i, 0, 0))
    in_specs = [pl.BlockSpec(tab.shape, lambda i: (0, 0)) for tab in tabs] + [
        pl.BlockSpec((packed, p.shape[1], LANES), lambda i: (i, 0, 0)) for p in pieces
    ]
    args = [*tabs, *pieces]
    if partial is not None:
        in_specs.append(grid_block)
        args.append(partial)
    counts = tuple(len(group) for _, group in sets)
    return pl.pallas_call(
        functools.partial(inverse_kernel, counts, latd, scale, partial is not None),
        out_shape=jax.ShapeDtypeStruct((levd, latd, nlon), out_dtype),
        grid=(levd // LEVELS,),
        in_specs=in_specs,
        out_specs=grid_block,
        scratch_shapes=[pltpu.VMEM((LEVELS * LANES, rows), BF16)],
        cost_estimate=pl.CostEstimate(
            flops=2 * rows * levd * latd * nlon,
            bytes_accessed=2 * levd * latd * (nlon + rows) + 2 * rows * nlon,
            transcendentals=0,
        ),
        name="inverse_dft",
    )(*args)


def local_fast(
    parts,
    grid_state,
    lat_order,
    slot_wave,
    truncation,
    zonal_wind,
    zonal_rate,
    quad_weight,
    legendre,
    vert_modes,
    vert_project,
    mode_rates,
    thermal_matrix,
    pressure_matrix,
):
    levd, latd, nlon = grid_state.shape[1:]
    slots = legendre.shape[0]
    nmodes = slot_wave.shape[0]
    nlat = lat_order.shape[0]
    nlev = vert_modes.shape[0]
    lats, levs = lax.axis_size("lat"), lax.axis_size("lev")
    groups = lats * levs
    z, x, f = lax.axis_index("lat"), lax.axis_index("lev"), lax.axis_index("fld")
    me = z * levs + x
    starts = [sum(parts[:i]) for i in range(len(parts))]

    waves = slot_wave.reshape(groups, 2, slots // 2)
    waves = xor_order(xor_order(waves, me, 0), f, 1)
    lat_rel = xor_order(lat_order.reshape(lats, latd), z, 0)
    lat_rel = jnp.pad(lat_rel, ((0, 0), (0, LANES - latd)), constant_values=-1)
    hits = lat_rel[0][None, :, None] == jnp.arange(nlat, dtype=jnp.int32)[None, None, :]
    zonal = jnp.stack([zonal_wind, zonal_rate, quad_weight * nlon ** (-0.5)], axis=0)
    lat_rows = jnp.sum(jnp.where(hits, zonal[:, None, :], 0.0), axis=2)
    lat_rows = jnp.pad(lat_rows, ((0, 5), (0, 0)))

    first = f == 0
    mix = jnp.dot(vert_project, thermal_matrix, precision=PRECISE)
    drop = -jnp.dot(pressure_matrix, vert_modes, precision=PRECISE)
    by_col = lambda m: xor_order(m.reshape(nlev, levs, levd), x, 1).reshape(nlev, nlev)
    by_row = lambda m: xor_order(m.reshape(levs, levd, nlev), x, 0).reshape(nlev, nlev)
    w1 = by_col(jnp.where(first, vert_project, mix)), by_col(jnp.where(first, mix, vert_project))
    w1 = jnp.concatenate(w1, axis=1)
    w2 = by_row(jnp.where(first, vert_modes, drop)), by_row(jnp.where(first, drop, vert_modes))
    w2 = jnp.concatenate(w2, axis=0)

    def three(w):
        hi = lax.reduce_precision(w, 8, 7)
        lo = (w - hi).astype(BF16)
        hi = hi.astype(BF16)
        return jnp.concatenate([hi, hi, lo], axis=1)

    w1, w2 = three(w1), three(w2)
    rates = mode_rates[:, None]
    perm = (lat_rel.reshape(-1, 1) == jnp.arange(nlat, dtype=jnp.int32)[None, :]).astype(BF16)
    my_waves = waves[0, 0]
    counts = pick_values(my_waves, truncation) - my_waves + 1

    lat_lev = ("lat", "lev")

    def exchange(blocks, order):
        out = list(blocks)
        for r in order:
            if r:
                pairs = [(i, i ^ r) for i in range(groups)]
                out[r] = lax.ppermute(blocks[r], lat_lev, pairs)
        return out

    def swap(block):
        return lax.ppermute(block, "fld", [(0, 1), (1, 0)])

    far, near = far_near(groups)
    tables, arrived = [], []
    for i, (at, part) in enumerate(zip(starts, parts)):
        w = waves[:, :, at : at + part].reshape(-1)
        lanes = jnp.broadcast_to(w.astype(F32)[:, None], (w.shape[0], LANES))
        tables.append(make_table(lanes, nlon))
        blocks = dft(grid_state[0], tables[i], lat_rows, lanes, groups)
        arrived.append(exchange(blocks, far + near))
    legendre = jnp.swapaxes(legendre, 1, 2)
    returned = []
    for i, (at, part) in enumerate(zip(starts, parts)):
        other = gather_halves(arrived[i])
        other = swap(other)
        info = jnp.stack(
            [
                my_waves[at : at + part],
                counts[at : at + part],
                jnp.full((part,), f, jnp.int32),
                jnp.full((part,), f * (slots // 2) + at, jnp.int32),
            ]
        )
        res = legendre_step(
            info, legendre, perm, w1, w2, rates, arrived[i], other, levs, levd, latd
        )
        got = swap(res[groups])
        sent = fill_halves(res[:groups], got)
        returned.append(exchange(sent, near + far))
    sets = list(zip(tables, returned))
    scale = float(nmodes) ** (-0.5)
    shape = (levd, latd, nlon)
    total = inverse_dft(sets[:-1], shape, None, scale, F32)
    total = inverse_dft(sets[-1:], shape, total, scale, BF16)
    return total[None]


def far_near(groups):
    rels = tuple(range(groups))
    return rels[groups // 2 :], rels[: groups // 2]


def power_of_two(n):
    return n & (n - 1) == 0


def solution(mesh):
    in_specs = (
        P(("member", "fld"), "lev", "lat", None),
        P(),
        P(),
        P(),
        P(),
        P(),
        P(),
        P(("lat", "lev"), None, None),
        P(),
        P(),
        P(),
        P(),
        P(),
    )
    out_specs = P(("member", "fld"), "lev", "lat", None)
    lats, levs = mesh.shape["lat"], mesh.shape["lev"]

    groups = lats * levs
    small = (
        mesh.shape["fld"] == 2 and power_of_two(lats) and power_of_two(levs) and 1 < groups <= 8
    )

    def local(grid_state, *rest):
        legendre = rest[6]
        levd, latd, nlon = grid_state.shape[1:]
        share = LANES - latd
        fits = (
            legendre.shape[0] % (4 * sum(SHARES)) == 0
            and levd % LEVELS == 0
            and latd % 8 == 0
            and share > 0
            and share * (2 * LEVELS - 1) == latd
            and nlon % (3 * LANES) == 0
        )
        if small and fits:
            unit = legendre.shape[0] // (2 * sum(SHARES))
            return local_fast([unit * n for n in SHARES], grid_state, *rest)
        return local_general(grid_state, *rest)

    return jax.shard_map(local, mesh=mesh, in_specs=in_specs, out_specs=out_specs, check_vma=False)
```

```python
import functools

import jax
import jax.numpy as jnp
from jax import lax
from jax.experimental import pallas as pl
from jax.experimental.pallas import tpu as pltpu
from jax.sharding import PartitionSpec as P


PRECISE = lax.Precision.HIGHEST
BF16 = jnp.bfloat16
F32 = jnp.float32


def dft_table(wavenums, nlon):
    columns = jnp.arange(nlon, dtype=jnp.int32)
    turns = columns[:, None] * wavenums[None, :] % nlon
    angles = turns.astype(jnp.float32) * (2.0 * jnp.pi / nlon)
    return jnp.stack([jnp.cos(angles), -jnp.sin(angles)], axis=1).astype(jnp.bfloat16)


def pick_values(idents, source_table):
    hits = idents[:, None] == jnp.arange(source_table.shape[0], dtype=jnp.int32)[None, :]
    return jnp.sum(jnp.where(hits, source_table[None, :], 0), axis=1)


def layer_eigen_basis(matrix, columns):
    return jnp.einsum("skcj,ij->skci", columns, matrix, precision=PRECISE)


def analyse(legendre, fourier_data):
    return jnp.einsum("skl,slx->skx", legendre, fourier_data, preferred_element_type=jnp.float32)


def synthesise(legendre, coeffs):
    return jnp.einsum("skl,skx->slx", legendre, coeffs, preferred_element_type=jnp.float32)


def local_general(
    grid_state,
    lat_order,
    slot_wave,
    truncation,
    zonal_wind,
    zonal_rate,
    quad_weight,
    legendre,
    vert_modes,
    vert_project,
    mode_rates,
    thermal_into_spread_matrix,
    pressure_balance_matrix,
):
    levd, latd, nlon = (grid_state.shape[1], grid_state.shape[2], grid_state.shape[3])
    slots = legendre.shape[0]
    nmodes = slot_wave.shape[0]
    nlat = lat_order.shape[0]
    nlev = vert_modes.shape[0]
    lat_count = lax.axis_size("lat")
    lev_count = lax.axis_size("lev")
    lat_index = lax.axis_index("lat")
    lev_index = lax.axis_index("lev")
    unknown_position = lax.axis_index("fld")
    my_lats = lax.dynamic_slice_in_dim(lat_order, lat_index * latd, latd)
    onehot = (my_lats[:, None] == jnp.arange(nlat, dtype=jnp.int32)[None, :]).astype(jnp.float32)
    per_lat = jnp.dot(
        onehot, jnp.stack([zonal_wind, zonal_rate, quad_weight], axis=1), precision=PRECISE
    )
    values = grid_state[0].astype(jnp.float32)
    flux = (values * (per_lat[None, :, 0][:, :, None] + values)).astype(jnp.bfloat16)
    count_rows = levd * latd
    stacked = jnp.concatenate(
        [grid_state[0].reshape(count_rows, nlon), flux.reshape(count_rows, nlon)], axis=0
    )
    table = dft_table(slot_wave, nlon).reshape(nlon, 2 * nmodes)
    spectra = lax.dot_general(
        table, stacked, (((0,), (1,)), ((), ())), preferred_element_type=jnp.float32
    ) * nlon ** (-0.5)
    spectra = spectra.reshape(2, nmodes, 2 * count_rows)
    plain = spectra[:, :, :count_rows]
    moved = spectra[:, :, count_rows:]
    rate_row = jnp.tile(per_lat[:, 1], levd)[None, :]
    weight_row = jnp.tile(per_lat[:, 2], levd)[None, :]
    wave_float = slot_wave.astype(jnp.float32)[:, None]
    factor = rate_row * wave_float
    real_part = (plain[0] + factor * moved[1]) * weight_row
    imag_part = (plain[1] - factor * moved[0]) * weight_row
    fourier = jnp.stack([real_part, imag_part], axis=0).astype(jnp.bfloat16)
    arrived = lax.all_to_all(fourier, ("lat", "lev"), split_axis=1, concat_axis=2, tiled=True)
    arrived = arrived.reshape(2, slots, lat_count, lev_count, levd, latd)
    arranged = jnp.transpose(arrived, (1, 2, 5, 0, 3, 4))
    arranged = arranged.reshape(slots, nlat, 2 * nlev)
    position = jnp.zeros((nlat,), jnp.int32).at[lat_order].set(jnp.arange(nlat, dtype=jnp.int32))
    ordered = jnp.take(arranged, position, axis=1)
    owner_index = lat_index * lev_count + lev_index
    my_waves = lax.dynamic_slice_in_dim(slot_wave, owner_index * slots, slots)
    limits = pick_values(my_waves, truncation)
    counts = limits - my_waves + 1
    degree = jnp.arange(nmodes, dtype=jnp.int32)
    valid = (degree[None, :] < counts[:, None])[:, :, None]
    own_spec = jnp.where(valid, analyse(legendre, ordered), jnp.float32(0.0))
    joined_harmonic_unknowns = lax.all_gather(own_spec, "fld", axis=2, tiled=True)
    joined_harmonic_unknowns = joined_harmonic_unknowns.reshape(slots, nmodes, 2, 2, nlev)
    outflow_rate_coeffs = joined_harmonic_unknowns[:, :, 0]
    thermal_coeffs = joined_harmonic_unknowns[:, :, 1]
    n_deg = (my_waves[:, None] + degree[None, :]).astype(jnp.float32)
    elliptic_inverse_scale = (n_deg * (n_deg + 1.0) / (nmodes * (nmodes - 1)))[:, :, None, None]
    outflow_rate_source = outflow_rate_coeffs + elliptic_inverse_scale * layer_eigen_basis(
        thermal_into_spread_matrix, thermal_coeffs
    )
    projected = layer_eigen_basis(vert_project, outflow_rate_source) / (
        1.0 + elliptic_inverse_scale * mode_rates
    )
    outflow_rate_next = layer_eigen_basis(vert_modes, projected)
    thermal_next = thermal_coeffs - layer_eigen_basis(pressure_balance_matrix, outflow_rate_next)
    own_new = (
        jnp.where(unknown_position == 0, outflow_rate_next, thermal_next)
        .astype(jnp.bfloat16)
        .reshape(slots, nmodes, 2 * nlev)
    )
    back = synthesise(legendre, own_new) * nmodes ** (-0.5)
    back = jnp.take(back, lat_order, axis=1).astype(jnp.bfloat16)
    shaped = back.reshape(slots, lat_count, latd, 2, lev_count, levd)
    outgoing = jnp.transpose(shaped, (3, 0, 1, 4, 5, 2)).reshape(
        2, slots, lat_count * lev_count * count_rows
    )
    returned = lax.all_to_all(outgoing, ("lat", "lev"), split_axis=2, concat_axis=1, tiled=True)
    leading = returned.reshape(2 * nmodes, count_rows)
    grid_out = lax.dot_general(
        leading, table, (((0,), (1,)), ((), ())), preferred_element_type=jnp.float32
    ) * nmodes ** (-0.5)
    return grid_out.astype(jnp.bfloat16).reshape(1, levd, latd, nlon)


LANES = 128
LEVELS = 8
SHARES = (1, 1)


def xor_order(array, index, axis):
    size = array.shape[axis]
    bits = size.bit_length() - 1
    shape = array.shape[:axis] + (2,) * bits + array.shape[axis + 1 :]
    out = array.reshape(shape)
    for b in range(bits):
        ax = axis + bits - 1 - b
        out = jnp.where((index >> b) & 1 == 1, jnp.flip(out, ax), out)
    return out.reshape(array.shape)


def packed_rows():
    return 2 * LEVELS - 1


def spare_lanes(row, last, latd):
    index, values = row
    share = LANES - latd
    lane = lax.broadcasted_iota(jnp.int32, values.shape, 1)
    turned = pltpu.roll(last, (latd - share * index) % LANES, 1)
    return jnp.where(lane < latd, values, turned)


def last_row(rows, latd):
    share = LANES - latd
    lane = lax.broadcasted_iota(jnp.int32, rows[0].shape, 1)
    out = pltpu.roll(rows[0], LANES - latd, 1)
    for i, row in enumerate(rows[1:], 1):
        turned = pltpu.roll(row, (share * i - latd) % LANES, 1)
        out = jnp.where(lane >= share * i, turned, out)
    return out


def table_kernel(nlon, wave_ref, out):
    rows = wave_ref.shape[0]
    nblk = nlon // LANES
    wave = wave_ref[...]
    lane = lax.broadcasted_iota(jnp.int32, (rows, LANES), 1)

    def sincos(step):
        turns = (lane * step).astype(F32) * wave
        turns = turns - nlon * jnp.floor(turns * (1.0 / nlon))
        turns = jnp.where(turns < 0.0, turns + nlon, turns)
        turns = jnp.where(turns >= nlon, turns - nlon, turns)
        angle = turns * (2.0 * jnp.pi / nlon)
        return jnp.cos(angle), jnp.sin(angle)

    cl, sl = sincos(1)
    ch, sh = sincos(LANES)
    for b in range(nblk):
        c, s = ch[:, b : b + 1], sh[:, b : b + 1]
        cols = slice(b * LANES, (b + 1) * LANES)
        out[:rows, cols] = (c * cl - s * sl).astype(BF16)
        out[rows:, cols] = (-(s * cl + c * sl)).astype(BF16)


def make_table(wave_lanes, nlon):
    return pl.pallas_call(
        functools.partial(table_kernel, nlon),
        out_shape=jax.ShapeDtypeStruct((2 * wave_lanes.shape[0], nlon), BF16),
        name="table",
    )(wave_lanes)


def dft_kernel(groups, latd, x_ref, t_ref, lat_ref, wave_ref, *rest):
    outs, (xf,) = rest[:groups], rest[groups:]
    rows = t_ref.shape[0]
    half = rows // 2
    per = half // groups
    nblk = x_ref.shape[2] // LANES

    @pl.when(pl.program_id(0) == 0)
    def _():
        xf[...] = jnp.zeros_like(xf)

    wind = jnp.broadcast_to(lat_ref[...].T[:latd, 0:1], (latd, LANES))
    wind = jnp.concatenate([wind] * nblk, axis=1)
    weight = lat_ref[2:3, :]
    factor = wave_ref[...] * lat_ref[1:2, :]

    def load(v):
        xv = x_ref[v]
        x32 = xv.astype(F32)
        xf[v % 2, 0:latd, :] = xv
        xf[v % 2, LANES : LANES + latd, :] = (x32 * (wind + x32)).astype(BF16)

    last = None
    load(LEVELS - 1)
    order = [LEVELS - 1, *range(LEVELS - 1)]
    for at, v in enumerate(order):
        if at + 1 < LEVELS:
            load(order[at + 1])
        both = lax.dot_general(
            t_ref[...], xf[v % 2], (((1,), (1,)), ((), ())), preferred_element_type=F32
        )
        plain, moved = both[:, :LANES], both[:, LANES:]
        real = (plain[:half] + factor * moved[half:]) * weight
        imag = (plain[half:] - factor * moved[:half]) * weight
        parts = [(v, real)]
        if last is None:
            last = imag
        else:
            parts.append((LEVELS + v, imag))
        for index, values in parts:
            full = spare_lanes((index, values), last, latd)
            for g in range(groups):
                outs[g][index] = full[g * per : (g + 1) * per].astype(BF16)


def dft(x, table, lat_rows, wave_lanes, groups):
    levd, latd, nlon = x.shape
    rows = table.shape[0]
    half = rows // 2
    per = half // groups
    packed = packed_rows()
    const = lambda i: (0, 0)
    block = pl.BlockSpec((packed, per, LANES), lambda i: (i, 0, 0))
    return pl.pallas_call(
        functools.partial(dft_kernel, groups, latd),
        out_shape=[jax.ShapeDtypeStruct((levd // LEVELS * packed, per, LANES), BF16)] * groups,
        grid=(levd // LEVELS,),
        in_specs=[
            pl.BlockSpec((LEVELS, latd, nlon), lambda i: (i, 0, 0)),
            pl.BlockSpec((rows, nlon), const),
            pl.BlockSpec(lat_rows.shape, const),
            pl.BlockSpec((half, LANES), const),
        ],
        out_specs=[block] * groups,
        scratch_shapes=[pltpu.VMEM((2, 2 * LANES, nlon), BF16)],
        cost_estimate=pl.CostEstimate(
            flops=4 * rows * levd * latd * nlon,
            bytes_accessed=2 * levd * latd * (nlon + rows) + 2 * rows * nlon,
            transcendentals=0,
        ),
        name="dft",
    )(x, table, lat_rows, wave_lanes)


def split3_dot(w3, x):
    hi = x.astype(BF16)
    lo = (x - hi.astype(F32)).astype(BF16)
    return jnp.dot(w3, jnp.concatenate([hi, lo, hi], axis=0), preferred_element_type=F32)


def permute_kernel(info, leg_ref, perm_ref, out):
    for j in range(leg_ref.shape[0]):
        out[j] = jnp.dot(perm_ref[...], leg_ref[j], preferred_element_type=F32).astype(BF16)


def permute_legendre(first_slot, leg, perm, count):
    _, nlat, nmodes = leg.shape
    lanes = perm.shape[0]
    step = 2 if count % 2 == 0 else 1
    return pl.pallas_call(
        permute_kernel,
        out_shape=jax.ShapeDtypeStruct((count, lanes, nmodes), BF16),
        grid_spec=pltpu.PrefetchScalarGridSpec(
            num_scalar_prefetch=1,
            grid=(count // step,),
            in_specs=[
                pl.BlockSpec((step, nlat, nmodes), lambda t, s: (s[0] // step + t, 0, 0)),
                pl.BlockSpec((lanes, nlat), lambda t, s: (0, 0)),
            ],
            out_specs=pl.BlockSpec((step, lanes, nmodes), lambda t, s: (t, 0, 0)),
        ),
        cost_estimate=pl.CostEstimate(
            flops=2 * count * lanes * nlat * nmodes,
            bytes_accessed=2 * count * (lanes + nlat) * nmodes,
            transcendentals=0,
        ),
        name="permute_legendre",
    )(first_slot, leg, perm)


def legendre_kernel(
    groups, levs, levd, latd, nmodes, info, leg_ref, w1_ref, w2_ref, mr_ref, *rest
):
    own = rest[:groups]
    other = rest[groups]
    outs = rest[groups + 1 : 2 * groups + 1]
    give = rest[2 * groups + 1]
    data, fresh_data = rest[2 * groups + 2 :]
    slots = outs[0].shape[1]
    lats = groups // levs
    nlev = levs * levd
    total = 4 * nlev
    count = leg_ref.shape[0]
    packed = packed_rows()
    t = pl.program_id(0)

    def each_group(move):
        def body(group, carry):
            for rel in range(groups):
                dz, dx = rel // levs, rel % levs
                for field in range(2):
                    base = field * nlev + dx * levd + group * LEVELS
                    rows = [
                        base + (i // LEVELS) * 2 * nlev + i % LEVELS for i in range(packed + 1)
                    ]
                    move(rel, field, dz, group * packed, rows)
            return carry

        lax.fori_loop(0, levd // LEVELS, body, 0)

    def unpack(rel, field, dz, at, rows):
        values = []
        for i in range(packed):
            value = own[rel][at + i] if field == 0 else other[rel, at + i]
            values.append(value.astype(F32)[:slots])
        values.append(last_row(values, latd))
        for row, value in zip(rows, values):
            data[dz, pl.ds(row, slots, stride=total), :] = value

    def pack(rel, field, dz, at, rows):
        last = fresh_data[dz, pl.ds(rows[-1], slots, stride=total), :]
        for i in range(packed):
            value = fresh_data[dz, pl.ds(rows[i], slots, stride=total), :]
            full = spare_lanes((i, value), last, latd).astype(BF16)
            if field == 0:
                outs[rel][at + i] = full
            else:
                give[rel, at + i, :slots] = full

    @pl.when(t == 0)
    def _():
        each_group(unpack)

    k = lax.broadcasted_iota(jnp.int32, (1, nmodes), 1)
    first = info[2, 0] == 0
    keep_own = jnp.where(first, 0.0, 1.0)
    keep_other = jnp.where(first, 1.0, 0.0)
    legs = [leg_ref[j] for j in range(count)]
    fresh = []
    for j in range(count):
        slot = t * count + j
        wave, terms = info[0, slot], info[1, slot]
        n = (wave + k).astype(F32)
        h = n * (n + 1.0) / float(nmodes * (nmodes - 1))
        scale_own = jnp.where(first, 1.0, h)
        scale_other = jnp.where(first, h, 1.0)
        denom = 1.0 + h * mr_ref[...]
        here = pl.ds(pl.multiple_of(slot * total, total), total)
        lined = jnp.concatenate([data[dz, here, :].astype(BF16) for dz in range(lats)], axis=1)
        spec = jnp.dot(lined, legs[j], preferred_element_type=F32)
        spec = jnp.where(k < terms, spec, 0.0)
        new = []
        for c in range(2):
            a = spec[c * 2 * nlev : c * 2 * nlev + nlev]
            b = spec[c * 2 * nlev + nlev : (c + 1) * 2 * nlev]
            src = jnp.concatenate([a * scale_own, b * scale_other], axis=0)
            q = split3_dot(w1_ref[...], src) / denom
            both = split3_dot(w2_ref[...], q)
            new.append(both[:nlev] + keep_own * a)
            new.append(both[nlev:] + keep_other * b)
        fresh.append(jnp.concatenate(new, axis=0).astype(BF16))
    for j in range(count):
        back = lax.dot_general(
            fresh[j], legs[j], (((1,), (1,)), ((), ())), preferred_element_type=F32
        )
        here = pl.ds(pl.multiple_of((t * count + j) * total, total), total)
        back = back * float(nmodes) ** (-0.5)
        for dz in range(lats):
            fresh_data[dz, here, :] = back[:, dz * LANES : (dz + 1) * LANES]

    @pl.when(t == pl.num_programs(0) - 1)
    def _():
        each_group(pack)


def legendre_step(info, leg, at, w1, w2, rates, own, other, levs, levd, latd):
    groups, packed, rows, _ = other.shape
    count = own[0].shape[1] // 2
    lanes, nmodes = leg.shape[1:]
    nlev = levs * levd
    const = lambda t, s: (0, 0)
    step = 2 if count % 2 == 0 else 1
    piece = pl.BlockSpec((packed, 2 * count, LANES), lambda t, s: (0, 0, 0))
    half = pl.BlockSpec((packed, count, LANES), lambda t, s: (0, 0, 0))
    stack = pl.BlockSpec((groups, packed, rows, LANES), lambda t, s: (0, 0, 0, 0))
    flops = count * 2 * 2 * nlev * 2 * nmodes * lanes * 2
    return pl.pallas_call(
        functools.partial(legendre_kernel, groups, levs, levd, latd, nmodes),
        out_shape=[jax.ShapeDtypeStruct((packed, count, LANES), BF16)] * groups
        + [jax.ShapeDtypeStruct(other.shape, BF16)],
        grid_spec=pltpu.PrefetchScalarGridSpec(
            num_scalar_prefetch=1,
            grid=(count // step,),
            in_specs=[
                pl.BlockSpec((step, lanes, nmodes), lambda t, s: (at // step + t, 0, 0)),
                pl.BlockSpec(w1.shape, const),
                pl.BlockSpec(w2.shape, const),
                pl.BlockSpec(rates.shape, const),
            ]
            + [piece] * groups
            + [pl.BlockSpec(memory_space=pltpu.VMEM)],
            out_specs=[half] * groups + [stack],
            scratch_shapes=[pltpu.VMEM((groups // levs, count * 4 * nlev, LANES), F32)] * 2,
        ),
        cost_estimate=pl.CostEstimate(
            flops=flops,
            bytes_accessed=count * 2 * (nmodes * lanes + 8 * nlev * lanes),
            transcendentals=0,
        ),
        name="legendre",
    )(info, leg, w1, w2, rates, *own, other)


def gather_kernel(groups, *refs):
    ins, out = refs[:groups], refs[-1]
    half = ins[0].shape[1] // 2
    for r in range(groups):
        out[r, :, :half] = ins[r][...].astype(F32)[:, half:].astype(BF16)


def padded(rows):
    return -(-rows // 8) * 8


def gather_halves(blocks):
    groups = len(blocks)
    packed, count, _ = blocks[0].shape
    half = padded(count // 2)
    group = packed_rows()
    return pl.pallas_call(
        functools.partial(gather_kernel, groups),
        out_shape=jax.ShapeDtypeStruct((groups, packed, half, LANES), BF16),
        grid=(packed // group,),
        in_specs=[pl.BlockSpec((group, count, LANES), lambda i: (i, 0, 0))] * groups,
        out_specs=pl.BlockSpec((groups, group, half, LANES), lambda i: (0, i, 0, 0)),
        name="gather_halves",
    )(*blocks)


def fill_kernel(groups, got, *refs):
    ins, outs = refs[:groups], refs[groups:]
    rows, half = ins[0].shape[:2]
    here = pl.ds(pl.program_id(0) * rows, rows)
    for r in range(groups):
        both = [ins[r][...].astype(F32), got[r, here].astype(F32)[:, :half]]
        outs[r][...] = jnp.concatenate(both, axis=1).astype(BF16)


def fill_halves(blocks, got):
    groups, packed, _, _ = got.shape
    half = blocks[0].shape[1]
    group = packed_rows()
    return pl.pallas_call(
        functools.partial(fill_kernel, groups),
        out_shape=[jax.ShapeDtypeStruct((packed, 2 * half, LANES), BF16)] * groups,
        grid=(packed // group,),
        in_specs=[pl.BlockSpec(memory_space=pltpu.VMEM)]
        + [pl.BlockSpec((group, half, LANES), lambda i: (i, 0, 0))] * groups,
        out_specs=[pl.BlockSpec((group, 2 * half, LANES), lambda i: (i, 0, 0))] * groups,
        name="fill_halves",
    )(got, *blocks)


def inverse_kernel(counts, latd, scale, add, *refs):
    tabs, refs = refs[: len(counts)], refs[len(counts) :]
    pieces, refs = refs[: sum(counts)], refs[sum(counts) :]
    partial = refs[0] if add else None
    out, lhs = refs[-2:]
    nlon = tabs[0].shape[1]
    packed = packed_rows()
    base, depth = 0, 0
    for tab, number in zip(tabs, counts):
        half = tab.shape[0] // 2
        group = pieces[depth : depth + number]
        rows = [
            jnp.concatenate([ref[i].astype(F32) for ref in group], axis=0) for i in range(packed)
        ]
        rows.append(last_row(rows, latd))
        for i, row in enumerate(rows):
            v, at = i % LEVELS, base + i // LEVELS * half
            lhs[v * LANES : (v + 1) * LANES, at : at + half] = row.astype(BF16).T
        base += 2 * half
        depth += number
    step = 3 * LANES
    for j in range(0, nlon, step):
        cols = slice(j, j + step)
        grid, base = None, 0
        for tab in tabs:
            rows = tab.shape[0]
            term = jnp.dot(
                lhs[:, base : base + rows], tab[:, cols], preferred_element_type=F32
            )
            grid = term if grid is None else grid + term
            base += rows
        grid = grid * scale
        for v in range(LEVELS):
            piece = grid[v * LANES : v * LANES + latd]
            if partial is not None:
                piece = piece + partial[v, :, cols]
            out[v, :, cols] = piece.astype(out.dtype)


def inverse_dft(sets, shape, partial, scale, out_dtype):
    tabs = [tab for tab, _ in sets]
    pieces = [p for _, group in sets for p in group]
    levd, latd, nlon = shape
    rows = sum(tab.shape[0] for tab in tabs)
    packed = packed_rows()
    grid_block = pl.BlockSpec((LEVELS, latd, nlon), lambda i: (i, 0, 0))
    in_specs = [pl.BlockSpec(tab.shape, lambda i: (0, 0)) for tab in tabs] + [
        pl.BlockSpec((packed, p.shape[1], LANES), lambda i: (i, 0, 0)) for p in pieces
    ]
    args = [*tabs, *pieces]
    if partial is not None:
        in_specs.append(grid_block)
        args.append(partial)
    counts = tuple(len(group) for _, group in sets)
    return pl.pallas_call(
        functools.partial(inverse_kernel, counts, latd, scale, partial is not None),
        out_shape=jax.ShapeDtypeStruct((levd, latd, nlon), out_dtype),
        grid=(levd // LEVELS,),
        in_specs=in_specs,
        out_specs=grid_block,
        scratch_shapes=[pltpu.VMEM((LEVELS * LANES, rows), BF16)],
        cost_estimate=pl.CostEstimate(
            flops=2 * rows * levd * latd * nlon,
            bytes_accessed=2 * levd * latd * (nlon + rows) + 2 * rows * nlon,
            transcendentals=0,
        ),
        name="inverse_dft",
    )(*args)


def local_fast(
    parts,
    grid_state,
    lat_order,
    slot_wave,
    truncation,
    zonal_wind,
    zonal_rate,
    quad_weight,
    legendre,
    vert_modes,
    vert_project,
    mode_rates,
    thermal_matrix,
    pressure_matrix,
):
    levd, latd, nlon = grid_state.shape[1:]
    slots = legendre.shape[0]
    nmodes = slot_wave.shape[0]
    nlat = lat_order.shape[0]
    nlev = vert_modes.shape[0]
    lats, levs = lax.axis_size("lat"), lax.axis_size("lev")
    groups = lats * levs
    z, x, f = lax.axis_index("lat"), lax.axis_index("lev"), lax.axis_index("fld")
    me = z * levs + x
    starts = [sum(parts[:i]) for i in range(len(parts))]

    waves = slot_wave.reshape(groups, 2, slots // 2)
    waves = xor_order(xor_order(waves, me, 0), f, 1)
    lat_rel = xor_order(lat_order.reshape(lats, latd), z, 0)
    lat_rel = jnp.pad(lat_rel, ((0, 0), (0, LANES - latd)), constant_values=-1)
    hits = lat_rel[0][None, :, None] == jnp.arange(nlat, dtype=jnp.int32)[None, None, :]
    zonal = jnp.stack([zonal_wind, zonal_rate, quad_weight * nlon ** (-0.5)], axis=0)
    lat_rows = jnp.sum(jnp.where(hits, zonal[:, None, :], 0.0), axis=2)
    lat_rows = jnp.pad(lat_rows, ((0, 5), (0, 0)))

    first = f == 0
    mix = jnp.dot(vert_project, thermal_matrix, precision=PRECISE)
    drop = -jnp.dot(pressure_matrix, vert_modes, precision=PRECISE)
    by_col = lambda m: xor_order(m.reshape(nlev, levs, levd), x, 1).reshape(nlev, nlev)
    by_row = lambda m: xor_order(m.reshape(levs, levd, nlev), x, 0).reshape(nlev, nlev)
    w1 = by_col(jnp.where(first, vert_project, mix)), by_col(jnp.where(first, mix, vert_project))
    w1 = jnp.concatenate(w1, axis=1)
    w2 = by_row(jnp.where(first, vert_modes, drop)), by_row(jnp.where(first, drop, vert_modes))
    w2 = jnp.concatenate(w2, axis=0)

    def three(w):
        hi = lax.reduce_precision(w, 8, 7)
        lo = (w - hi).astype(BF16)
        hi = hi.astype(BF16)
        return jnp.concatenate([hi, hi, lo], axis=1)

    w1, w2 = three(w1), three(w2)
    rates = mode_rates[:, None]
    perm = (lat_rel.reshape(-1, 1) == jnp.arange(nlat, dtype=jnp.int32)[None, :]).astype(BF16)
    my_waves = waves[0, 0]
    counts = pick_values(my_waves, truncation) - my_waves + 1

    lat_lev = ("lat", "lev")

    def exchange(blocks, order):
        out = list(blocks)
        for r in order:
            if r:
                pairs = [(i, i ^ r) for i in range(groups)]
                out[r] = lax.ppermute(blocks[r], lat_lev, pairs)
        return out

    def swap(block):
        return lax.ppermute(block, "fld", [(0, 1), (1, 0)])

    far, near = far_near(groups)
    tables, arrived = [], []
    for i, (at, part) in enumerate(zip(starts, parts)):
        w = waves[:, :, at : at + part].reshape(-1)
        lanes = jnp.broadcast_to(w.astype(F32)[:, None], (w.shape[0], LANES))
        tables.append(make_table(lanes, nlon))
        blocks = dft(grid_state[0], tables[i], lat_rows, lanes, groups)
        arrived.append(exchange(blocks, far + near))
    first_slot = jnp.full((1,), f * (slots // 2), jnp.int32)
    leg = permute_legendre(first_slot, jnp.swapaxes(legendre, 1, 2), perm, slots // 2)
    returned = []
    for i, (at, part) in enumerate(zip(starts, parts)):
        other = gather_halves(arrived[i])
        other = swap(other)
        info = jnp.stack(
            [
                my_waves[at : at + part],
                counts[at : at + part],
                jnp.full((part,), f, jnp.int32),
            ]
        )
        res = legendre_step(
            info, leg, at, w1, w2, rates, arrived[i], other, levs, levd, latd
        )
        got = swap(res[groups])
        sent = fill_halves(res[:groups], got)
        returned.append(exchange(sent, near + far))
    sets = list(zip(tables, returned))
    scale = float(nmodes) ** (-0.5)
    shape = (levd, latd, nlon)
    total = inverse_dft(sets[:-1], shape, None, scale, F32)
    total = inverse_dft(sets[-1:], shape, total, scale, BF16)
    return total[None]


def far_near(groups):
    rels = tuple(range(groups))
    return rels[groups // 2 :], rels[: groups // 2]


def power_of_two(n):
    return n & (n - 1) == 0


def solution(mesh):
    in_specs = (
        P(("member", "fld"), "lev", "lat", None),
        P(),
        P(),
        P(),
        P(),
        P(),
        P(),
        P(("lat", "lev"), None, None),
        P(),
        P(),
        P(),
        P(),
        P(),
    )
    out_specs = P(("member", "fld"), "lev", "lat", None)
    lats, levs = mesh.shape["lat"], mesh.shape["lev"]

    groups = lats * levs
    small = (
        mesh.shape["fld"] == 2 and power_of_two(lats) and power_of_two(levs) and 1 < groups <= 8
    )

    def local(grid_state, *rest):
        legendre = rest[6]
        levd, latd, nlon = grid_state.shape[1:]
        share = LANES - latd
        fits = (
            legendre.shape[0] % (4 * sum(SHARES)) == 0
            and levd % LEVELS == 0
            and latd % 8 == 0
            and share > 0
            and share * (2 * LEVELS - 1) == latd
            and nlon % (3 * LANES) == 0
        )
        if small and fits:
            unit = legendre.shape[0] // (2 * sum(SHARES))
            return local_fast([unit * n for n in SHARES], grid_state, *rest)
        return local_general(grid_state, *rest)

    return jax.shard_map(local, mesh=mesh, in_specs=in_specs, out_specs=out_specs, check_vma=False)
```

```python
import functools

import jax
import jax.numpy as jnp
from jax import lax
from jax.experimental import pallas as pl
from jax.experimental.pallas import tpu as pltpu
from jax.sharding import PartitionSpec as P


PRECISE = lax.Precision.HIGHEST
BF16 = jnp.bfloat16
F32 = jnp.float32


def dft_table(wavenums, nlon):
    columns = jnp.arange(nlon, dtype=jnp.int32)
    turns = columns[:, None] * wavenums[None, :] % nlon
    angles = turns.astype(jnp.float32) * (2.0 * jnp.pi / nlon)
    return jnp.stack([jnp.cos(angles), -jnp.sin(angles)], axis=1).astype(jnp.bfloat16)


def pick_values(idents, source_table):
    hits = idents[:, None] == jnp.arange(source_table.shape[0], dtype=jnp.int32)[None, :]
    return jnp.sum(jnp.where(hits, source_table[None, :], 0), axis=1)


def layer_eigen_basis(matrix, columns):
    return jnp.einsum("skcj,ij->skci", columns, matrix, precision=PRECISE)


def analyse(legendre, fourier_data):
    return jnp.einsum("skl,slx->skx", legendre, fourier_data, preferred_element_type=jnp.float32)


def synthesise(legendre, coeffs):
    return jnp.einsum("skl,skx->slx", legendre, coeffs, preferred_element_type=jnp.float32)


def local_general(
    grid_state,
    lat_order,
    slot_wave,
    truncation,
    zonal_wind,
    zonal_rate,
    quad_weight,
    legendre,
    vert_modes,
    vert_project,
    mode_rates,
    thermal_into_spread_matrix,
    pressure_balance_matrix,
):
    levd, latd, nlon = (grid_state.shape[1], grid_state.shape[2], grid_state.shape[3])
    slots = legendre.shape[0]
    nmodes = slot_wave.shape[0]
    nlat = lat_order.shape[0]
    nlev = vert_modes.shape[0]
    lat_count = lax.axis_size("lat")
    lev_count = lax.axis_size("lev")
    lat_index = lax.axis_index("lat")
    lev_index = lax.axis_index("lev")
    unknown_position = lax.axis_index("fld")
    my_lats = lax.dynamic_slice_in_dim(lat_order, lat_index * latd, latd)
    onehot = (my_lats[:, None] == jnp.arange(nlat, dtype=jnp.int32)[None, :]).astype(jnp.float32)
    per_lat = jnp.dot(
        onehot, jnp.stack([zonal_wind, zonal_rate, quad_weight], axis=1), precision=PRECISE
    )
    values = grid_state[0].astype(jnp.float32)
    flux = (values * (per_lat[None, :, 0][:, :, None] + values)).astype(jnp.bfloat16)
    count_rows = levd * latd
    stacked = jnp.concatenate(
        [grid_state[0].reshape(count_rows, nlon), flux.reshape(count_rows, nlon)], axis=0
    )
    table = dft_table(slot_wave, nlon).reshape(nlon, 2 * nmodes)
    spectra = lax.dot_general(
        table, stacked, (((0,), (1,)), ((), ())), preferred_element_type=jnp.float32
    ) * nlon ** (-0.5)
    spectra = spectra.reshape(2, nmodes, 2 * count_rows)
    plain = spectra[:, :, :count_rows]
    moved = spectra[:, :, count_rows:]
    rate_row = jnp.tile(per_lat[:, 1], levd)[None, :]
    weight_row = jnp.tile(per_lat[:, 2], levd)[None, :]
    wave_float = slot_wave.astype(jnp.float32)[:, None]
    factor = rate_row * wave_float
    real_part = (plain[0] + factor * moved[1]) * weight_row
    imag_part = (plain[1] - factor * moved[0]) * weight_row
    fourier = jnp.stack([real_part, imag_part], axis=0).astype(jnp.bfloat16)
    arrived = lax.all_to_all(fourier, ("lat", "lev"), split_axis=1, concat_axis=2, tiled=True)
    arrived = arrived.reshape(2, slots, lat_count, lev_count, levd, latd)
    arranged = jnp.transpose(arrived, (1, 2, 5, 0, 3, 4))
    arranged = arranged.reshape(slots, nlat, 2 * nlev)
    position = jnp.zeros((nlat,), jnp.int32).at[lat_order].set(jnp.arange(nlat, dtype=jnp.int32))
    ordered = jnp.take(arranged, position, axis=1)
    owner_index = lat_index * lev_count + lev_index
    my_waves = lax.dynamic_slice_in_dim(slot_wave, owner_index * slots, slots)
    limits = pick_values(my_waves, truncation)
    counts = limits - my_waves + 1
    degree = jnp.arange(nmodes, dtype=jnp.int32)
    valid = (degree[None, :] < counts[:, None])[:, :, None]
    own_spec = jnp.where(valid, analyse(legendre, ordered), jnp.float32(0.0))
    joined_harmonic_unknowns = lax.all_gather(own_spec, "fld", axis=2, tiled=True)
    joined_harmonic_unknowns = joined_harmonic_unknowns.reshape(slots, nmodes, 2, 2, nlev)
    outflow_rate_coeffs = joined_harmonic_unknowns[:, :, 0]
    thermal_coeffs = joined_harmonic_unknowns[:, :, 1]
    n_deg = (my_waves[:, None] + degree[None, :]).astype(jnp.float32)
    elliptic_inverse_scale = (n_deg * (n_deg + 1.0) / (nmodes * (nmodes - 1)))[:, :, None, None]
    outflow_rate_source = outflow_rate_coeffs + elliptic_inverse_scale * layer_eigen_basis(
        thermal_into_spread_matrix, thermal_coeffs
    )
    projected = layer_eigen_basis(vert_project, outflow_rate_source) / (
        1.0 + elliptic_inverse_scale * mode_rates
    )
    outflow_rate_next = layer_eigen_basis(vert_modes, projected)
    thermal_next = thermal_coeffs - layer_eigen_basis(pressure_balance_matrix, outflow_rate_next)
    own_new = (
        jnp.where(unknown_position == 0, outflow_rate_next, thermal_next)
        .astype(jnp.bfloat16)
        .reshape(slots, nmodes, 2 * nlev)
    )
    back = synthesise(legendre, own_new) * nmodes ** (-0.5)
    back = jnp.take(back, lat_order, axis=1).astype(jnp.bfloat16)
    shaped = back.reshape(slots, lat_count, latd, 2, lev_count, levd)
    outgoing = jnp.transpose(shaped, (3, 0, 1, 4, 5, 2)).reshape(
        2, slots, lat_count * lev_count * count_rows
    )
    returned = lax.all_to_all(outgoing, ("lat", "lev"), split_axis=2, concat_axis=1, tiled=True)
    leading = returned.reshape(2 * nmodes, count_rows)
    grid_out = lax.dot_general(
        leading, table, (((0,), (1,)), ((), ())), preferred_element_type=jnp.float32
    ) * nmodes ** (-0.5)
    return grid_out.astype(jnp.bfloat16).reshape(1, levd, latd, nlon)


LANES = 128
LEVELS = 8
SHARES = (1, 1)


def xor_order(array, index, axis):
    size = array.shape[axis]
    bits = size.bit_length() - 1
    shape = array.shape[:axis] + (2,) * bits + array.shape[axis + 1 :]
    out = array.reshape(shape)
    for b in range(bits):
        ax = axis + bits - 1 - b
        out = jnp.where((index >> b) & 1 == 1, jnp.flip(out, ax), out)
    return out.reshape(array.shape)


def packed_rows():
    return 2 * LEVELS - 1


def spare_lanes(row, last, latd):
    index, values = row
    share = LANES - latd
    lane = lax.broadcasted_iota(jnp.int32, values.shape, 1)
    turned = pltpu.roll(last, (latd - share * index) % LANES, 1)
    return jnp.where(lane < latd, values, turned)


def last_row(rows, latd):
    share = LANES - latd
    lane = lax.broadcasted_iota(jnp.int32, rows[0].shape, 1)
    out = pltpu.roll(rows[0], LANES - latd, 1)
    for i, row in enumerate(rows[1:], 1):
        turned = pltpu.roll(row, (share * i - latd) % LANES, 1)
        out = jnp.where(lane >= share * i, turned, out)
    return out


def table_kernel(nlon, wave_ref, out):
    rows = wave_ref.shape[0]
    nblk = nlon // LANES
    wave = wave_ref[...]
    lane = lax.broadcasted_iota(jnp.int32, (rows, LANES), 1)

    def sincos(step):
        turns = (lane * step).astype(F32) * wave
        turns = turns - nlon * jnp.floor(turns * (1.0 / nlon) + 0.5)
        quarter = jnp.floor(turns * (4.0 / nlon) + 0.5)
        x = (turns - quarter * (nlon / 4.0)) * (2.0 * jnp.pi / nlon)
        y = x * x
        s = x * (1.0 + y * (-1 / 6 + y * (1 / 120 + y * (-1 / 5040 + y * (1 / 362880)))))
        c = 1.0 + y * (-1 / 2 + y * (1 / 24 + y * (-1 / 720 + y * (1 / 40320))))
        c = c - y * y * y * y * y * (1 / 3628800)
        odd = jnp.abs(quarter) == 1.0
        half = jnp.abs(quarter) == 2.0
        sine = jnp.where(odd, c * quarter, jnp.where(half, -s, s))
        cosine = jnp.where(odd, -s * quarter, jnp.where(half, -c, c))
        return cosine, sine

    cl, sl = sincos(1)
    ch, sh = sincos(LANES)
    for b in range(nblk):
        c, s = ch[:, b : b + 1], sh[:, b : b + 1]
        cols = slice(b * LANES, (b + 1) * LANES)
        out[:rows, cols] = (c * cl - s * sl).astype(BF16)
        out[rows:, cols] = (-(s * cl + c * sl)).astype(BF16)


def make_table(wave_lanes, nlon):
    return pl.pallas_call(
        functools.partial(table_kernel, nlon),
        out_shape=jax.ShapeDtypeStruct((2 * wave_lanes.shape[0], nlon), BF16),
        name="table",
    )(wave_lanes)


def dft_kernel(groups, latd, x_ref, t_ref, lat_ref, wave_ref, *rest):
    outs, (xf,) = rest[:groups], rest[groups:]
    rows = t_ref.shape[0]
    half = rows // 2
    per = half // groups
    nblk = x_ref.shape[2] // LANES

    @pl.when(pl.program_id(0) == 0)
    def _():
        xf[...] = jnp.zeros_like(xf)

    wind = jnp.broadcast_to(lat_ref[...].T[:latd, 0:1], (latd, LANES))
    wind = jnp.concatenate([wind] * nblk, axis=1)
    weight = lat_ref[2:3, :]
    factor = wave_ref[...] * lat_ref[1:2, :]

    def load(v):
        xv = x_ref[v]
        x32 = xv.astype(F32)
        xf[v % 2, 0:latd, :] = xv
        xf[v % 2, LANES : LANES + latd, :] = (x32 * (wind + x32)).astype(BF16)

    last = None
    load(LEVELS - 1)
    order = [LEVELS - 1, *range(LEVELS - 1)]
    for at, v in enumerate(order):
        if at + 1 < LEVELS:
            load(order[at + 1])
        both = lax.dot_general(
            t_ref[...], xf[v % 2], (((1,), (1,)), ((), ())), preferred_element_type=F32
        )
        plain, moved = both[:, :LANES], both[:, LANES:]
        real = (plain[:half] + factor * moved[half:]) * weight
        imag = (plain[half:] - factor * moved[:half]) * weight
        parts = [(v, real)]
        if last is None:
            last = imag
        else:
            parts.append((LEVELS + v, imag))
        for index, values in parts:
            full = spare_lanes((index, values), last, latd)
            for g in range(groups):
                outs[g][index] = full[g * per : (g + 1) * per].astype(BF16)


def dft(x, table, lat_rows, wave_lanes, groups):
    levd, latd, nlon = x.shape
    rows = table.shape[0]
    half = rows // 2
    per = half // groups
    packed = packed_rows()
    const = lambda i: (0, 0)
    block = pl.BlockSpec((packed, per, LANES), lambda i: (i, 0, 0))
    return pl.pallas_call(
        functools.partial(dft_kernel, groups, latd),
        out_shape=[jax.ShapeDtypeStruct((levd // LEVELS * packed, per, LANES), BF16)] * groups,
        grid=(levd // LEVELS,),
        in_specs=[
            pl.BlockSpec((LEVELS, latd, nlon), lambda i: (i, 0, 0)),
            pl.BlockSpec((rows, nlon), const),
            pl.BlockSpec(lat_rows.shape, const),
            pl.BlockSpec((half, LANES), const),
        ],
        out_specs=[block] * groups,
        scratch_shapes=[pltpu.VMEM((2, 2 * LANES, nlon), BF16)],
        cost_estimate=pl.CostEstimate(
            flops=4 * rows * levd * latd * nlon,
            bytes_accessed=2 * levd * latd * (nlon + rows) + 2 * rows * nlon,
            transcendentals=0,
        ),
        name="dft",
    )(x, table, lat_rows, wave_lanes)


def split3_dot(w3, x):
    hi = x.astype(BF16)
    lo = (x - hi.astype(F32)).astype(BF16)
    return jnp.dot(w3, jnp.concatenate([hi, lo, hi], axis=0), preferred_element_type=F32)


def permute_kernel(info, leg_ref, perm_ref, out):
    for j in range(leg_ref.shape[0]):
        out[j] = jnp.dot(perm_ref[...], leg_ref[j], preferred_element_type=F32).astype(BF16)


def permute_legendre(first_slot, leg, perm, count):
    _, nlat, nmodes = leg.shape
    lanes = perm.shape[0]
    step = 2 if count % 2 == 0 else 1
    return pl.pallas_call(
        permute_kernel,
        out_shape=jax.ShapeDtypeStruct((count, lanes, nmodes), BF16),
        grid_spec=pltpu.PrefetchScalarGridSpec(
            num_scalar_prefetch=1,
            grid=(count // step,),
            in_specs=[
                pl.BlockSpec((step, nlat, nmodes), lambda t, s: (s[0] // step + t, 0, 0)),
                pl.BlockSpec((lanes, nlat), lambda t, s: (0, 0)),
            ],
            out_specs=pl.BlockSpec((step, lanes, nmodes), lambda t, s: (t, 0, 0)),
        ),
        cost_estimate=pl.CostEstimate(
            flops=2 * count * lanes * nlat * nmodes,
            bytes_accessed=2 * count * (lanes + nlat) * nmodes,
            transcendentals=0,
        ),
        name="permute_legendre",
    )(first_slot, leg, perm)


def legendre_kernel(
    groups, levs, levd, latd, nmodes, info, leg_ref, w1_ref, w2_ref, mr_ref, *rest
):
    own = rest[:groups]
    other = rest[groups]
    outs = rest[groups + 1 : 2 * groups + 1]
    give = rest[2 * groups + 1]
    data, fresh_data = rest[2 * groups + 2 :]
    slots = outs[0].shape[1]
    lats = groups // levs
    nlev = levs * levd
    total = 4 * nlev
    count = leg_ref.shape[0]
    packed = packed_rows()
    t = pl.program_id(0)

    def each_group(move):
        def body(group, carry):
            for rel in range(groups):
                dz, dx = rel // levs, rel % levs
                for field in range(2):
                    base = field * nlev + dx * levd + group * LEVELS
                    rows = [
                        base + (i // LEVELS) * 2 * nlev + i % LEVELS for i in range(packed + 1)
                    ]
                    move(rel, field, dz, group * packed, rows)
            return carry

        lax.fori_loop(0, levd // LEVELS, body, 0)

    def unpack(rel, field, dz, at, rows):
        values = []
        for i in range(packed):
            value = own[rel][at + i] if field == 0 else other[rel, at + i]
            values.append(value.astype(F32)[:slots])
        values.append(last_row(values, latd))
        for row, value in zip(rows, values):
            data[dz, pl.ds(row, slots, stride=total), :] = value

    def pack(rel, field, dz, at, rows):
        last = fresh_data[dz, pl.ds(rows[-1], slots, stride=total), :]
        for i in range(packed):
            value = fresh_data[dz, pl.ds(rows[i], slots, stride=total), :]
            full = spare_lanes((i, value), last, latd).astype(BF16)
            if field == 0:
                outs[rel][at + i] = full
            else:
                give[rel, at + i, :slots] = full

    @pl.when(t == 0)
    def _():
        each_group(unpack)

    k = lax.broadcasted_iota(jnp.int32, (1, nmodes), 1)
    first = info[2, 0] == 0
    keep_own = jnp.where(first, 0.0, 1.0)
    keep_other = jnp.where(first, 1.0, 0.0)
    legs = [leg_ref[j] for j in range(count)]
    fresh = []
    for j in range(count):
        slot = t * count + j
        wave, terms = info[0, slot], info[1, slot]
        n = (wave + k).astype(F32)
        h = n * (n + 1.0) / float(nmodes * (nmodes - 1))
        scale_own = jnp.where(first, 1.0, h)
        scale_other = jnp.where(first, h, 1.0)
        denom = 1.0 + h * mr_ref[...]
        here = pl.ds(pl.multiple_of(slot * total, total), total)
        lined = jnp.concatenate([data[dz, here, :].astype(BF16) for dz in range(lats)], axis=1)
        spec = jnp.dot(lined, legs[j], preferred_element_type=F32)
        spec = jnp.where(k < terms, spec, 0.0)
        new = []
        for c in range(2):
            a = spec[c * 2 * nlev : c * 2 * nlev + nlev]
            b = spec[c * 2 * nlev + nlev : (c + 1) * 2 * nlev]
            src = jnp.concatenate([a * scale_own, b * scale_other], axis=0)
            q = split3_dot(w1_ref[...], src) / denom
            both = split3_dot(w2_ref[...], q)
            new.append(both[:nlev] + keep_own * a)
            new.append(both[nlev:] + keep_other * b)
        fresh.append(jnp.concatenate(new, axis=0).astype(BF16))
    for j in range(count):
        back = lax.dot_general(
            fresh[j], legs[j], (((1,), (1,)), ((), ())), preferred_element_type=F32
        )
        here = pl.ds(pl.multiple_of((t * count + j) * total, total), total)
        back = back * float(nmodes) ** (-0.5)
        for dz in range(lats):
            fresh_data[dz, here, :] = back[:, dz * LANES : (dz + 1) * LANES]

    @pl.when(t == pl.num_programs(0) - 1)
    def _():
        each_group(pack)


def legendre_step(info, leg, at, w1, w2, rates, own, other, levs, levd, latd):
    groups, packed, rows, _ = other.shape
    count = own[0].shape[1] // 2
    lanes, nmodes = leg.shape[1:]
    nlev = levs * levd
    const = lambda t, s: (0, 0)
    step = 2 if count % 2 == 0 else 1
    piece = pl.BlockSpec((packed, 2 * count, LANES), lambda t, s: (0, 0, 0))
    half = pl.BlockSpec((packed, count, LANES), lambda t, s: (0, 0, 0))
    stack = pl.BlockSpec((groups, packed, rows, LANES), lambda t, s: (0, 0, 0, 0))
    flops = count * 2 * 2 * nlev * 2 * nmodes * lanes * 2
    return pl.pallas_call(
        functools.partial(legendre_kernel, groups, levs, levd, latd, nmodes),
        out_shape=[jax.ShapeDtypeStruct((packed, count, LANES), BF16)] * groups
        + [jax.ShapeDtypeStruct(other.shape, BF16)],
        grid_spec=pltpu.PrefetchScalarGridSpec(
            num_scalar_prefetch=1,
            grid=(count // step,),
            in_specs=[
                pl.BlockSpec((step, lanes, nmodes), lambda t, s: (at // step + t, 0, 0)),
                pl.BlockSpec(w1.shape, const),
                pl.BlockSpec(w2.shape, const),
                pl.BlockSpec(rates.shape, const),
            ]
            + [piece] * groups
            + [pl.BlockSpec(memory_space=pltpu.VMEM)],
            out_specs=[half] * groups + [stack],
            scratch_shapes=[pltpu.VMEM((groups // levs, count * 4 * nlev, LANES), F32)] * 2,
        ),
        cost_estimate=pl.CostEstimate(
            flops=flops,
            bytes_accessed=count * 2 * (nmodes * lanes + 8 * nlev * lanes),
            transcendentals=0,
        ),
        name="legendre",
    )(info, leg, w1, w2, rates, *own, other)


def gather_kernel(groups, *refs):
    ins, out = refs[:groups], refs[-1]
    half = ins[0].shape[1] // 2
    for r in range(groups):
        out[r, :, :half] = ins[r][...].astype(F32)[:, half:].astype(BF16)


def padded(rows):
    return -(-rows // 8) * 8


def gather_halves(blocks):
    groups = len(blocks)
    packed, count, _ = blocks[0].shape
    half = padded(count // 2)
    group = packed
    return pl.pallas_call(
        functools.partial(gather_kernel, groups),
        out_shape=jax.ShapeDtypeStruct((groups, packed, half, LANES), BF16),
        grid=(packed // group,),
        in_specs=[pl.BlockSpec((group, count, LANES), lambda i: (i, 0, 0))] * groups,
        out_specs=pl.BlockSpec((groups, group, half, LANES), lambda i: (0, i, 0, 0)),
        name="gather_halves",
    )(*blocks)


def fill_kernel(groups, got, *refs):
    ins, outs = refs[:groups], refs[groups:]
    rows, half = ins[0].shape[:2]
    here = pl.ds(pl.program_id(0) * rows, rows)
    for r in range(groups):
        both = [ins[r][...].astype(F32), got[r, here].astype(F32)[:, :half]]
        outs[r][...] = jnp.concatenate(both, axis=1).astype(BF16)


def fill_halves(blocks, got):
    groups, packed, _, _ = got.shape
    half = blocks[0].shape[1]
    group = packed
    return pl.pallas_call(
        functools.partial(fill_kernel, groups),
        out_shape=[jax.ShapeDtypeStruct((packed, 2 * half, LANES), BF16)] * groups,
        grid=(packed // group,),
        in_specs=[pl.BlockSpec(memory_space=pltpu.VMEM)]
        + [pl.BlockSpec((group, half, LANES), lambda i: (i, 0, 0))] * groups,
        out_specs=[pl.BlockSpec((group, 2 * half, LANES), lambda i: (i, 0, 0))] * groups,
        name="fill_halves",
    )(got, *blocks)


def inverse_kernel(counts, latd, scale, add, *refs):
    tabs, refs = refs[: len(counts)], refs[len(counts) :]
    pieces, refs = refs[: sum(counts)], refs[sum(counts) :]
    partial = refs[0] if add else None
    out, lhs = refs[-2:]
    nlon = tabs[0].shape[1]
    packed = packed_rows()
    base, depth = 0, 0
    for tab, number in zip(tabs, counts):
        half = tab.shape[0] // 2
        group = pieces[depth : depth + number]
        rows = [
            jnp.concatenate([ref[i].astype(F32) for ref in group], axis=0) for i in range(packed)
        ]
        rows.append(last_row(rows, latd))
        for i, row in enumerate(rows):
            v, at = i % LEVELS, base + i // LEVELS * half
            lhs[v * LANES : (v + 1) * LANES, at : at + half] = row.astype(BF16).T
        base += 2 * half
        depth += number
    step = 3 * LANES
    for j in range(0, nlon, step):
        cols = slice(j, j + step)
        grid, base = None, 0
        for tab in tabs:
            rows = tab.shape[0]
            term = jnp.dot(
                lhs[:, base : base + rows], tab[:, cols], preferred_element_type=F32
            )
            grid = term if grid is None else grid + term
            base += rows
        grid = grid * scale
        for v in range(LEVELS):
            piece = grid[v * LANES : v * LANES + latd]
            if partial is not None:
                piece = piece + partial[v, :, cols]
            out[v, :, cols] = piece.astype(out.dtype)


def inverse_dft(sets, shape, partial, scale, out_dtype):
    tabs = [tab for tab, _ in sets]
    pieces = [p for _, group in sets for p in group]
    levd, latd, nlon = shape
    rows = sum(tab.shape[0] for tab in tabs)
    packed = packed_rows()
    grid_block = pl.BlockSpec((LEVELS, latd, nlon), lambda i: (i, 0, 0))
    in_specs = [pl.BlockSpec(tab.shape, lambda i: (0, 0)) for tab in tabs] + [
        pl.BlockSpec((packed, p.shape[1], LANES), lambda i: (i, 0, 0)) for p in pieces
    ]
    args = [*tabs, *pieces]
    if partial is not None:
        in_specs.append(grid_block)
        args.append(partial)
    counts = tuple(len(group) for _, group in sets)
    return pl.pallas_call(
        functools.partial(inverse_kernel, counts, latd, scale, partial is not None),
        out_shape=jax.ShapeDtypeStruct((levd, latd, nlon), out_dtype),
        grid=(levd // LEVELS,),
        in_specs=in_specs,
        out_specs=grid_block,
        scratch_shapes=[pltpu.VMEM((LEVELS * LANES, rows), BF16)],
        cost_estimate=pl.CostEstimate(
            flops=2 * rows * levd * latd * nlon,
            bytes_accessed=2 * levd * latd * (nlon + rows) + 2 * rows * nlon,
            transcendentals=0,
        ),
        name="inverse_dft",
    )(*args)


def local_fast(
    parts,
    grid_state,
    lat_order,
    slot_wave,
    truncation,
    zonal_wind,
    zonal_rate,
    quad_weight,
    legendre,
    vert_modes,
    vert_project,
    mode_rates,
    thermal_matrix,
    pressure_matrix,
):
    levd, latd, nlon = grid_state.shape[1:]
    slots = legendre.shape[0]
    nmodes = slot_wave.shape[0]
    nlat = lat_order.shape[0]
    nlev = vert_modes.shape[0]
    lats, levs = lax.axis_size("lat"), lax.axis_size("lev")
    groups = lats * levs
    z, x, f = lax.axis_index("lat"), lax.axis_index("lev"), lax.axis_index("fld")
    me = z * levs + x
    starts = [sum(parts[:i]) for i in range(len(parts))]

    waves = slot_wave.reshape(groups, 2, slots // 2)
    waves = xor_order(xor_order(waves, me, 0), f, 1)
    lat_rel = xor_order(lat_order.reshape(lats, latd), z, 0)
    lat_rel = jnp.pad(lat_rel, ((0, 0), (0, LANES - latd)), constant_values=-1)
    hits = lat_rel[0][None, :, None] == jnp.arange(nlat, dtype=jnp.int32)[None, None, :]
    zonal = jnp.stack([zonal_wind, zonal_rate, quad_weight * nlon ** (-0.5)], axis=0)
    lat_rows = jnp.sum(jnp.where(hits, zonal[:, None, :], 0.0), axis=2)
    lat_rows = jnp.pad(lat_rows, ((0, 5), (0, 0)))

    first = f == 0
    mix = jnp.dot(vert_project, thermal_matrix, precision=PRECISE)
    drop = -jnp.dot(pressure_matrix, vert_modes, precision=PRECISE)
    by_col = lambda m: xor_order(m.reshape(nlev, levs, levd), x, 1).reshape(nlev, nlev)
    by_row = lambda m: xor_order(m.reshape(levs, levd, nlev), x, 0).reshape(nlev, nlev)
    w1 = by_col(jnp.where(first, vert_project, mix)), by_col(jnp.where(first, mix, vert_project))
    w1 = jnp.concatenate(w1, axis=1)
    w2 = by_row(jnp.where(first, vert_modes, drop)), by_row(jnp.where(first, drop, vert_modes))
    w2 = jnp.concatenate(w2, axis=0)

    def three(w):
        hi = lax.reduce_precision(w, 8, 7)
        lo = (w - hi).astype(BF16)
        hi = hi.astype(BF16)
        return jnp.concatenate([hi, hi, lo], axis=1)

    w1, w2 = three(w1), three(w2)
    rates = mode_rates[:, None]
    perm = (lat_rel.reshape(-1, 1) == jnp.arange(nlat, dtype=jnp.int32)[None, :]).astype(BF16)
    my_waves = waves[0, 0]
    counts = pick_values(my_waves, truncation) - my_waves + 1

    lat_lev = ("lat", "lev")

    def exchange(blocks, order):
        out = list(blocks)
        for r in order:
            if r:
                pairs = [(i, i ^ r) for i in range(groups)]
                out[r] = lax.ppermute(blocks[r], lat_lev, pairs)
        return out

    def swap(block):
        return lax.ppermute(block, "fld", [(0, 1), (1, 0)])

    far, near = far_near(groups)
    tables, arrived = [], []
    for i, (at, part) in enumerate(zip(starts, parts)):
        w = waves[:, :, at : at + part].reshape(-1)
        lanes = jnp.broadcast_to(w.astype(F32)[:, None], (w.shape[0], LANES))
        tables.append(make_table(lanes, nlon))
        blocks = dft(grid_state[0], tables[i], lat_rows, lanes, groups)
        arrived.append(exchange(blocks, far + near))
    first_slot = jnp.full((1,), f * (slots // 2), jnp.int32)
    leg = permute_legendre(first_slot, jnp.swapaxes(legendre, 1, 2), perm, slots // 2)
    returned = []
    for i, (at, part) in enumerate(zip(starts, parts)):
        other = gather_halves(arrived[i])
        other = swap(other)
        info = jnp.stack(
            [
                my_waves[at : at + part],
                counts[at : at + part],
                jnp.full((part,), f, jnp.int32),
            ]
        )
        res = legendre_step(
            info, leg, at, w1, w2, rates, arrived[i], other, levs, levd, latd
        )
        got = swap(res[groups])
        sent = fill_halves(res[:groups], got)
        returned.append(exchange(sent, near + far))
    sets = list(zip(tables, returned))
    scale = float(nmodes) ** (-0.5)
    shape = (levd, latd, nlon)
    table, pieces = sets.pop()
    table = table.reshape(2, groups, -1, nlon)
    cut = groups // 2
    for chosen in (slice(0, cut), slice(cut, groups)):
        sets.append((table[:, chosen].reshape(-1, nlon), pieces[chosen]))
    total = inverse_dft(sets[:-1], shape, None, scale, F32)
    total = inverse_dft(sets[-1:], shape, total, scale, BF16)
    return total[None]


def far_near(groups):
    rels = tuple(range(groups))
    return rels[groups // 2 :], rels[: groups // 2]


def power_of_two(n):
    return n & (n - 1) == 0


def solution(mesh):
    in_specs = (
        P(("member", "fld"), "lev", "lat", None),
        P(),
        P(),
        P(),
        P(),
        P(),
        P(),
        P(("lat", "lev"), None, None),
        P(),
        P(),
        P(),
        P(),
        P(),
    )
    out_specs = P(("member", "fld"), "lev", "lat", None)
    lats, levs = mesh.shape["lat"], mesh.shape["lev"]

    groups = lats * levs
    small = (
        mesh.shape["fld"] == 2 and power_of_two(lats) and power_of_two(levs) and 1 < groups <= 8
    )

    def local(grid_state, *rest):
        legendre = rest[6]
        levd, latd, nlon = grid_state.shape[1:]
        share = LANES - latd
        fits = (
            legendre.shape[0] % (4 * sum(SHARES)) == 0
            and levd % LEVELS == 0
            and latd % 8 == 0
            and share > 0
            and share * (2 * LEVELS - 1) == latd
            and nlon % (3 * LANES) == 0
        )
        if small and fits:
            unit = legendre.shape[0] // (2 * sum(SHARES))
            return local_fast([unit * n for n in SHARES], grid_state, *rest)
        return local_general(grid_state, *rest)

    return jax.shard_map(local, mesh=mesh, in_specs=in_specs, out_specs=out_specs, check_vma=False)
```

```python
import functools

import jax
import jax.numpy as jnp
from jax import lax
from jax.experimental import pallas as pl
from jax.experimental.pallas import tpu as pltpu
from jax.sharding import PartitionSpec as P


PRECISE = lax.Precision.HIGHEST
BF16 = jnp.bfloat16
F32 = jnp.float32


def dft_table(wavenums, nlon):
    columns = jnp.arange(nlon, dtype=jnp.int32)
    turns = columns[:, None] * wavenums[None, :] % nlon
    angles = turns.astype(jnp.float32) * (2.0 * jnp.pi / nlon)
    return jnp.stack([jnp.cos(angles), -jnp.sin(angles)], axis=1).astype(jnp.bfloat16)


def pick_values(idents, source_table):
    hits = idents[:, None] == jnp.arange(source_table.shape[0], dtype=jnp.int32)[None, :]
    return jnp.sum(jnp.where(hits, source_table[None, :], 0), axis=1)


def layer_eigen_basis(matrix, columns):
    return jnp.einsum("skcj,ij->skci", columns, matrix, precision=PRECISE)


def analyse(legendre, fourier_data):
    return jnp.einsum("skl,slx->skx", legendre, fourier_data, preferred_element_type=jnp.float32)


def synthesise(legendre, coeffs):
    return jnp.einsum("skl,skx->slx", legendre, coeffs, preferred_element_type=jnp.float32)


def local_general(
    grid_state,
    lat_order,
    slot_wave,
    truncation,
    zonal_wind,
    zonal_rate,
    quad_weight,
    legendre,
    vert_modes,
    vert_project,
    mode_rates,
    thermal_into_spread_matrix,
    pressure_balance_matrix,
):
    levd, latd, nlon = (grid_state.shape[1], grid_state.shape[2], grid_state.shape[3])
    slots = legendre.shape[0]
    nmodes = slot_wave.shape[0]
    nlat = lat_order.shape[0]
    nlev = vert_modes.shape[0]
    lat_count = lax.axis_size("lat")
    lev_count = lax.axis_size("lev")
    lat_index = lax.axis_index("lat")
    lev_index = lax.axis_index("lev")
    unknown_position = lax.axis_index("fld")
    my_lats = lax.dynamic_slice_in_dim(lat_order, lat_index * latd, latd)
    onehot = (my_lats[:, None] == jnp.arange(nlat, dtype=jnp.int32)[None, :]).astype(jnp.float32)
    per_lat = jnp.dot(
        onehot, jnp.stack([zonal_wind, zonal_rate, quad_weight], axis=1), precision=PRECISE
    )
    values = grid_state[0].astype(jnp.float32)
    flux = (values * (per_lat[None, :, 0][:, :, None] + values)).astype(jnp.bfloat16)
    count_rows = levd * latd
    stacked = jnp.concatenate(
        [grid_state[0].reshape(count_rows, nlon), flux.reshape(count_rows, nlon)], axis=0
    )
    table = dft_table(slot_wave, nlon).reshape(nlon, 2 * nmodes)
    spectra = lax.dot_general(
        table, stacked, (((0,), (1,)), ((), ())), preferred_element_type=jnp.float32
    ) * nlon ** (-0.5)
    spectra = spectra.reshape(2, nmodes, 2 * count_rows)
    plain = spectra[:, :, :count_rows]
    moved = spectra[:, :, count_rows:]
    rate_row = jnp.tile(per_lat[:, 1], levd)[None, :]
    weight_row = jnp.tile(per_lat[:, 2], levd)[None, :]
    wave_float = slot_wave.astype(jnp.float32)[:, None]
    factor = rate_row * wave_float
    real_part = (plain[0] + factor * moved[1]) * weight_row
    imag_part = (plain[1] - factor * moved[0]) * weight_row
    fourier = jnp.stack([real_part, imag_part], axis=0).astype(jnp.bfloat16)
    arrived = lax.all_to_all(fourier, ("lat", "lev"), split_axis=1, concat_axis=2, tiled=True)
    arrived = arrived.reshape(2, slots, lat_count, lev_count, levd, latd)
    arranged = jnp.transpose(arrived, (1, 2, 5, 0, 3, 4))
    arranged = arranged.reshape(slots, nlat, 2 * nlev)
    position = jnp.zeros((nlat,), jnp.int32).at[lat_order].set(jnp.arange(nlat, dtype=jnp.int32))
    ordered = jnp.take(arranged, position, axis=1)
    owner_index = lat_index * lev_count + lev_index
    my_waves = lax.dynamic_slice_in_dim(slot_wave, owner_index * slots, slots)
    limits = pick_values(my_waves, truncation)
    counts = limits - my_waves + 1
    degree = jnp.arange(nmodes, dtype=jnp.int32)
    valid = (degree[None, :] < counts[:, None])[:, :, None]
    own_spec = jnp.where(valid, analyse(legendre, ordered), jnp.float32(0.0))
    joined_harmonic_unknowns = lax.all_gather(own_spec, "fld", axis=2, tiled=True)
    joined_harmonic_unknowns = joined_harmonic_unknowns.reshape(slots, nmodes, 2, 2, nlev)
    outflow_rate_coeffs = joined_harmonic_unknowns[:, :, 0]
    thermal_coeffs = joined_harmonic_unknowns[:, :, 1]
    n_deg = (my_waves[:, None] + degree[None, :]).astype(jnp.float32)
    elliptic_inverse_scale = (n_deg * (n_deg + 1.0) / (nmodes * (nmodes - 1)))[:, :, None, None]
    outflow_rate_source = outflow_rate_coeffs + elliptic_inverse_scale * layer_eigen_basis(
        thermal_into_spread_matrix, thermal_coeffs
    )
    projected = layer_eigen_basis(vert_project, outflow_rate_source) / (
        1.0 + elliptic_inverse_scale * mode_rates
    )
    outflow_rate_next = layer_eigen_basis(vert_modes, projected)
    thermal_next = thermal_coeffs - layer_eigen_basis(pressure_balance_matrix, outflow_rate_next)
    own_new = (
        jnp.where(unknown_position == 0, outflow_rate_next, thermal_next)
        .astype(jnp.bfloat16)
        .reshape(slots, nmodes, 2 * nlev)
    )
    back = synthesise(legendre, own_new) * nmodes ** (-0.5)
    back = jnp.take(back, lat_order, axis=1).astype(jnp.bfloat16)
    shaped = back.reshape(slots, lat_count, latd, 2, lev_count, levd)
    outgoing = jnp.transpose(shaped, (3, 0, 1, 4, 5, 2)).reshape(
        2, slots, lat_count * lev_count * count_rows
    )
    returned = lax.all_to_all(outgoing, ("lat", "lev"), split_axis=2, concat_axis=1, tiled=True)
    leading = returned.reshape(2 * nmodes, count_rows)
    grid_out = lax.dot_general(
        leading, table, (((0,), (1,)), ((), ())), preferred_element_type=jnp.float32
    ) * nmodes ** (-0.5)
    return grid_out.astype(jnp.bfloat16).reshape(1, levd, latd, nlon)


LANES = 128
LEVELS = 8
SHARES = (1, 1)


def xor_order(array, index, axis):
    size = array.shape[axis]
    bits = size.bit_length() - 1
    shape = array.shape[:axis] + (2,) * bits + array.shape[axis + 1 :]
    out = array.reshape(shape)
    for b in range(bits):
        ax = axis + bits - 1 - b
        out = jnp.where((index >> b) & 1 == 1, jnp.flip(out, ax), out)
    return out.reshape(array.shape)


def packed_rows():
    return 2 * LEVELS - 1


def spare_lanes(row, last, latd):
    index, values = row
    share = LANES - latd
    lane = lax.broadcasted_iota(jnp.int32, values.shape, 1)
    turned = pltpu.roll(last, (latd - share * index) % LANES, 1)
    return jnp.where(lane < latd, values, turned)


def last_row(rows, latd):
    share = LANES - latd
    lane = lax.broadcasted_iota(jnp.int32, rows[0].shape, 1)
    out = pltpu.roll(rows[0], LANES - latd, 1)
    for i, row in enumerate(rows[1:], 1):
        turned = pltpu.roll(row, (share * i - latd) % LANES, 1)
        out = jnp.where(lane >= share * i, turned, out)
    return out


def table_kernel(nlon, wave_ref, out):
    rows = wave_ref.shape[0]
    nblk = nlon // LANES
    wave = wave_ref[...]
    lane = lax.broadcasted_iota(jnp.int32, (rows, LANES), 1)

    def sincos(step):
        turns = (lane * step).astype(F32) * wave
        turns = turns - nlon * jnp.floor(turns * (1.0 / nlon) + 0.5)
        quarter = jnp.floor(turns * (4.0 / nlon) + 0.5)
        x = (turns - quarter * (nlon / 4.0)) * (2.0 * jnp.pi / nlon)
        y = x * x
        s = x * (1.0 + y * (-1 / 6 + y * (1 / 120 + y * (-1 / 5040 + y * (1 / 362880)))))
        c = 1.0 + y * (-1 / 2 + y * (1 / 24 + y * (-1 / 720 + y * (1 / 40320))))
        c = c - y * y * y * y * y * (1 / 3628800)
        odd = jnp.abs(quarter) == 1.0
        half = jnp.abs(quarter) == 2.0
        sine = jnp.where(odd, c * quarter, jnp.where(half, -s, s))
        cosine = jnp.where(odd, -s * quarter, jnp.where(half, -c, c))
        return cosine, sine

    cl, sl = sincos(1)
    ch, sh = sincos(LANES)
    for b in range(nblk):
        c, s = ch[:, b : b + 1], sh[:, b : b + 1]
        cols = slice(b * LANES, (b + 1) * LANES)
        out[:rows, cols] = (c * cl - s * sl).astype(BF16)
        out[rows:, cols] = (-(s * cl + c * sl)).astype(BF16)


def make_table(wave_lanes, nlon):
    return pl.pallas_call(
        functools.partial(table_kernel, nlon),
        out_shape=jax.ShapeDtypeStruct((2 * wave_lanes.shape[0], nlon), BF16),
        name="table",
    )(wave_lanes)


def dft_kernel(groups, latd, x_ref, t_ref, lat_ref, wave_ref, *rest):
    outs, (xf,) = rest[:groups], rest[groups:]
    rows = t_ref.shape[0]
    half = rows // 2
    per = half // groups
    nblk = x_ref.shape[2] // LANES

    @pl.when(pl.program_id(0) == 0)
    def _():
        xf[...] = jnp.zeros_like(xf)

    wind = jnp.broadcast_to(lat_ref[...].T[:latd, 0:1], (latd, LANES))
    wind = jnp.concatenate([wind] * nblk, axis=1)
    weight = lat_ref[2:3, :]
    factor = wave_ref[...] * lat_ref[1:2, :]

    def load(v):
        xv = x_ref[v]
        x32 = xv.astype(F32)
        xf[v % 2, 0:latd, :] = xv
        xf[v % 2, LANES : LANES + latd, :] = (x32 * (wind + x32)).astype(BF16)

    last = None
    load(LEVELS - 1)
    order = [LEVELS - 1, *range(LEVELS - 1)]
    for at, v in enumerate(order):
        if at + 1 < LEVELS:
            load(order[at + 1])
        both = lax.dot_general(
            t_ref[...], xf[v % 2], (((1,), (1,)), ((), ())), preferred_element_type=F32
        )
        plain, moved = both[:, :LANES], both[:, LANES:]
        real = (plain[:half] + factor * moved[half:]) * weight
        imag = (plain[half:] - factor * moved[:half]) * weight
        parts = [(v, real)]
        if last is None:
            last = imag
        else:
            parts.append((LEVELS + v, imag))
        for index, values in parts:
            full = spare_lanes((index, values), last, latd)
            for g in range(groups):
                outs[g][index] = full[g * per : (g + 1) * per].astype(BF16)


def dft(x, table, lat_rows, wave_lanes, groups):
    levd, latd, nlon = x.shape
    rows = table.shape[0]
    half = rows // 2
    per = half // groups
    packed = packed_rows()
    const = lambda i: (0, 0)
    block = pl.BlockSpec((packed, per, LANES), lambda i: (i, 0, 0))
    return pl.pallas_call(
        functools.partial(dft_kernel, groups, latd),
        out_shape=[jax.ShapeDtypeStruct((levd // LEVELS * packed, per, LANES), BF16)] * groups,
        grid=(levd // LEVELS,),
        in_specs=[
            pl.BlockSpec((LEVELS, latd, nlon), lambda i: (i, 0, 0)),
            pl.BlockSpec((rows, nlon), const),
            pl.BlockSpec(lat_rows.shape, const),
            pl.BlockSpec((half, LANES), const),
        ],
        out_specs=[block] * groups,
        scratch_shapes=[pltpu.VMEM((2, 2 * LANES, nlon), BF16)],
        cost_estimate=pl.CostEstimate(
            flops=4 * rows * levd * latd * nlon,
            bytes_accessed=2 * levd * latd * (nlon + rows) + 2 * rows * nlon,
            transcendentals=0,
        ),
        name="dft",
    )(x, table, lat_rows, wave_lanes)


def split3_dot(w3, x):
    hi = x.astype(BF16)
    lo = (x - hi.astype(F32)).astype(BF16)
    return jnp.dot(w3, jnp.concatenate([hi, lo, hi], axis=0), preferred_element_type=F32)


def permute_kernel(info, leg_ref, perm_ref, out):
    for j in range(leg_ref.shape[0]):
        out[j] = jnp.dot(perm_ref[...], leg_ref[j], preferred_element_type=F32).astype(BF16)


def permute_legendre(first_slot, leg, perm, count):
    _, nlat, nmodes = leg.shape
    lanes = perm.shape[0]
    step = 2 if count % 2 == 0 else 1
    return pl.pallas_call(
        permute_kernel,
        out_shape=jax.ShapeDtypeStruct((count, lanes, nmodes), BF16),
        grid_spec=pltpu.PrefetchScalarGridSpec(
            num_scalar_prefetch=1,
            grid=(count // step,),
            in_specs=[
                pl.BlockSpec((step, nlat, nmodes), lambda t, s: (s[0] // step + t, 0, 0)),
                pl.BlockSpec((lanes, nlat), lambda t, s: (0, 0)),
            ],
            out_specs=pl.BlockSpec((step, lanes, nmodes), lambda t, s: (t, 0, 0)),
        ),
        cost_estimate=pl.CostEstimate(
            flops=2 * count * lanes * nlat * nmodes,
            bytes_accessed=2 * count * (lanes + nlat) * nmodes,
            transcendentals=0,
        ),
        name="permute_legendre",
    )(first_slot, leg, perm)


def legendre_kernel(
    groups, levs, levd, latd, nmodes, info, leg_ref, w1_ref, w2_ref, mr_ref, *rest
):
    own = rest[:groups]
    other = rest[groups]
    outs = rest[groups + 1 : 2 * groups + 1]
    give = rest[2 * groups + 1]
    data, fresh_data = rest[2 * groups + 2 :]
    slots = outs[0].shape[1]
    lats = groups // levs
    nlev = levs * levd
    total = 4 * nlev
    count = leg_ref.shape[0]
    packed = packed_rows()
    t = pl.program_id(0)

    def each_group(move):
        def body(group, carry):
            for rel in range(groups):
                dz, dx = rel // levs, rel % levs
                for field in range(2):
                    base = field * nlev + dx * levd + group * LEVELS
                    rows = [
                        base + (i // LEVELS) * 2 * nlev + i % LEVELS for i in range(packed + 1)
                    ]
                    move(rel, field, dz, group * packed, rows)
            return carry

        lax.fori_loop(0, levd // LEVELS, body, 0)

    def unpack(rel, field, dz, at, rows):
        values = []
        for i in range(packed):
            value = own[rel][at + i] if field == 0 else other[rel, at + i]
            values.append(value.astype(F32)[:slots])
        values.append(last_row(values, latd))
        for row, value in zip(rows, values):
            data[dz, pl.ds(row, slots, stride=total), :] = value

    def pack(rel, field, dz, at, rows):
        last = fresh_data[dz, pl.ds(rows[-1], slots, stride=total), :]
        for i in range(packed):
            value = fresh_data[dz, pl.ds(rows[i], slots, stride=total), :]
            full = spare_lanes((i, value), last, latd).astype(BF16)
            if field == 0:
                outs[rel][at + i] = full
            else:
                give[rel, at + i, :slots] = full

    @pl.when(t == 0)
    def _():
        each_group(unpack)

    k = lax.broadcasted_iota(jnp.int32, (1, nmodes), 1)
    first = info[2, 0] == 0
    keep_own = jnp.where(first, 0.0, 1.0)
    keep_other = jnp.where(first, 1.0, 0.0)
    legs = [leg_ref[j] for j in range(count)]
    fresh = []
    for j in range(count):
        slot = t * count + j
        wave, terms = info[0, slot], info[1, slot]
        n = (wave + k).astype(F32)
        h = n * (n + 1.0) / float(nmodes * (nmodes - 1))
        scale_own = jnp.where(first, 1.0, h)
        scale_other = jnp.where(first, h, 1.0)
        denom = 1.0 + h * mr_ref[...]
        here = pl.ds(pl.multiple_of(slot * total, total), total)
        lined = jnp.concatenate([data[dz, here, :].astype(BF16) for dz in range(lats)], axis=1)
        spec = jnp.dot(lined, legs[j], preferred_element_type=F32)
        spec = jnp.where(k < terms, spec, 0.0)
        new = []
        for c in range(2):
            a = spec[c * 2 * nlev : c * 2 * nlev + nlev]
            b = spec[c * 2 * nlev + nlev : (c + 1) * 2 * nlev]
            src = jnp.concatenate([a * scale_own, b * scale_other], axis=0)
            q = split3_dot(w1_ref[...], src) / denom
            both = split3_dot(w2_ref[...], q)
            new.append(both[:nlev] + keep_own * a)
            new.append(both[nlev:] + keep_other * b)
        fresh.append(jnp.concatenate(new, axis=0).astype(BF16))
    for j in range(count):
        back = lax.dot_general(
            fresh[j], legs[j], (((1,), (1,)), ((), ())), preferred_element_type=F32
        )
        here = pl.ds(pl.multiple_of((t * count + j) * total, total), total)
        back = back * float(nmodes) ** (-0.5)
        for dz in range(lats):
            fresh_data[dz, here, :] = back[:, dz * LANES : (dz + 1) * LANES]

    @pl.when(t == pl.num_programs(0) - 1)
    def _():
        each_group(pack)


def legendre_step(info, leg, at, w1, w2, rates, own, other, levs, levd, latd):
    groups, packed, rows, _ = other.shape
    count = own[0].shape[1] // 2
    lanes, nmodes = leg.shape[1:]
    nlev = levs * levd
    const = lambda t, s: (0, 0)
    step = 2 if count % 2 == 0 else 1
    piece = pl.BlockSpec((packed, 2 * count, LANES), lambda t, s: (0, 0, 0))
    half = pl.BlockSpec((packed, count, LANES), lambda t, s: (0, 0, 0))
    stack = pl.BlockSpec((groups, packed, rows, LANES), lambda t, s: (0, 0, 0, 0))
    flops = count * 2 * 2 * nlev * 2 * nmodes * lanes * 2
    return pl.pallas_call(
        functools.partial(legendre_kernel, groups, levs, levd, latd, nmodes),
        out_shape=[jax.ShapeDtypeStruct((packed, count, LANES), BF16)] * groups
        + [jax.ShapeDtypeStruct(other.shape, BF16)],
        grid_spec=pltpu.PrefetchScalarGridSpec(
            num_scalar_prefetch=1,
            grid=(count // step,),
            in_specs=[
                pl.BlockSpec((step, lanes, nmodes), lambda t, s: (at // step + t, 0, 0)),
                pl.BlockSpec(w1.shape, const),
                pl.BlockSpec(w2.shape, const),
                pl.BlockSpec(rates.shape, const),
            ]
            + [piece] * groups
            + [pl.BlockSpec(memory_space=pltpu.VMEM)],
            out_specs=[half] * groups + [stack],
            scratch_shapes=[pltpu.VMEM((groups // levs, count * 4 * nlev, LANES), F32)] * 2,
        ),
        cost_estimate=pl.CostEstimate(
            flops=flops,
            bytes_accessed=count * 2 * (nmodes * lanes + 8 * nlev * lanes),
            transcendentals=0,
        ),
        name="legendre",
    )(info, leg, w1, w2, rates, *own, other)


def gather_kernel(groups, *refs):
    ins, out = refs[:groups], refs[-1]
    half = ins[0].shape[1] // 2
    for r in range(groups):
        out[r, :, :half] = ins[r][...].astype(F32)[:, half:].astype(BF16)


def padded(rows):
    return -(-rows // 8) * 8


def gather_halves(blocks):
    groups = len(blocks)
    packed, count, _ = blocks[0].shape
    half = padded(count // 2)
    group = packed
    return pl.pallas_call(
        functools.partial(gather_kernel, groups),
        out_shape=jax.ShapeDtypeStruct((groups, packed, half, LANES), BF16),
        grid=(packed // group,),
        in_specs=[pl.BlockSpec((group, count, LANES), lambda i: (i, 0, 0))] * groups,
        out_specs=pl.BlockSpec((groups, group, half, LANES), lambda i: (0, i, 0, 0)),
        name="gather_halves",
    )(*blocks)


def fill_kernel(groups, got, *refs):
    ins, outs = refs[:groups], refs[groups:]
    rows, half = ins[0].shape[:2]
    here = pl.ds(pl.program_id(0) * rows, rows)
    for r in range(groups):
        both = [ins[r][...].astype(F32), got[r, here].astype(F32)[:, :half]]
        outs[r][...] = jnp.concatenate(both, axis=1).astype(BF16)


def fill_halves(blocks, got):
    groups, packed, _, _ = got.shape
    half = blocks[0].shape[1]
    group = packed
    return pl.pallas_call(
        functools.partial(fill_kernel, groups),
        out_shape=[jax.ShapeDtypeStruct((packed, 2 * half, LANES), BF16)] * groups,
        grid=(packed // group,),
        in_specs=[pl.BlockSpec(memory_space=pltpu.VMEM)]
        + [pl.BlockSpec((group, half, LANES), lambda i: (i, 0, 0))] * groups,
        out_specs=[pl.BlockSpec((group, 2 * half, LANES), lambda i: (i, 0, 0))] * groups,
        name="fill_halves",
    )(got, *blocks)


def inverse_kernel(counts, latd, scale, add, *refs):
    tabs, refs = refs[: len(counts)], refs[len(counts) :]
    pieces, refs = refs[: sum(counts)], refs[sum(counts) :]
    partial = refs[0] if add else None
    out, lhs = refs[-2:]
    nlon = tabs[0].shape[1]
    packed = packed_rows()
    base, depth = 0, 0
    for tab, number in zip(tabs, counts):
        half = tab.shape[0] // 2
        group = pieces[depth : depth + number]
        rows = [
            jnp.concatenate([ref[i].astype(F32) for ref in group], axis=0) for i in range(packed)
        ]
        rows.append(last_row(rows, latd))
        for i, row in enumerate(rows):
            v, at = i % LEVELS, base + i // LEVELS * half
            lhs[v * LANES : (v + 1) * LANES, at : at + half] = row.astype(BF16).T
        base += 2 * half
        depth += number
    step = 3 * LANES
    for j in range(0, nlon, step):
        cols = slice(j, j + step)
        grid, base = None, 0
        for tab in tabs:
            rows = tab.shape[0]
            term = jnp.dot(
                lhs[:, base : base + rows], tab[:, cols], preferred_element_type=F32
            )
            grid = term if grid is None else grid + term
            base += rows
        grid = grid * scale
        for v in range(LEVELS):
            piece = grid[v * LANES : v * LANES + latd]
            if partial is not None:
                piece = piece + partial[v, :, cols].astype(F32)
            out[v, :, cols] = piece.astype(out.dtype)


def inverse_dft(sets, shape, partial, scale, out_dtype):
    tabs = [tab for tab, _ in sets]
    pieces = [p for _, group in sets for p in group]
    levd, latd, nlon = shape
    rows = sum(tab.shape[0] for tab in tabs)
    packed = packed_rows()
    grid_block = pl.BlockSpec((LEVELS, latd, nlon), lambda i: (i, 0, 0))
    in_specs = [pl.BlockSpec(tab.shape, lambda i: (0, 0)) for tab in tabs] + [
        pl.BlockSpec((packed, p.shape[1], LANES), lambda i: (i, 0, 0)) for p in pieces
    ]
    args = [*tabs, *pieces]
    if partial is not None:
        in_specs.append(grid_block)
        args.append(partial)
    counts = tuple(len(group) for _, group in sets)
    return pl.pallas_call(
        functools.partial(inverse_kernel, counts, latd, scale, partial is not None),
        out_shape=jax.ShapeDtypeStruct((levd, latd, nlon), out_dtype),
        grid=(levd // LEVELS,),
        in_specs=in_specs,
        out_specs=grid_block,
        scratch_shapes=[pltpu.VMEM((LEVELS * LANES, rows), BF16)],
        cost_estimate=pl.CostEstimate(
            flops=2 * rows * levd * latd * nlon,
            bytes_accessed=2 * levd * latd * (nlon + rows) + 2 * rows * nlon,
            transcendentals=0,
        ),
        name="inverse_dft",
    )(*args)


def local_fast(
    parts,
    grid_state,
    lat_order,
    slot_wave,
    truncation,
    zonal_wind,
    zonal_rate,
    quad_weight,
    legendre,
    vert_modes,
    vert_project,
    mode_rates,
    thermal_matrix,
    pressure_matrix,
):
    levd, latd, nlon = grid_state.shape[1:]
    slots = legendre.shape[0]
    nmodes = slot_wave.shape[0]
    nlat = lat_order.shape[0]
    nlev = vert_modes.shape[0]
    lats, levs = lax.axis_size("lat"), lax.axis_size("lev")
    groups = lats * levs
    z, x, f = lax.axis_index("lat"), lax.axis_index("lev"), lax.axis_index("fld")
    me = z * levs + x
    starts = [sum(parts[:i]) for i in range(len(parts))]

    waves = slot_wave.reshape(groups, 2, slots // 2)
    waves = xor_order(xor_order(waves, me, 0), f, 1)
    lat_rel = xor_order(lat_order.reshape(lats, latd), z, 0)
    lat_rel = jnp.pad(lat_rel, ((0, 0), (0, LANES - latd)), constant_values=-1)
    hits = lat_rel[0][None, :, None] == jnp.arange(nlat, dtype=jnp.int32)[None, None, :]
    zonal = jnp.stack([zonal_wind, zonal_rate, quad_weight * nlon ** (-0.5)], axis=0)
    lat_rows = jnp.sum(jnp.where(hits, zonal[:, None, :], 0.0), axis=2)
    lat_rows = jnp.pad(lat_rows, ((0, 5), (0, 0)))

    first = f == 0
    mix = jnp.dot(vert_project, thermal_matrix, precision=PRECISE)
    drop = -jnp.dot(pressure_matrix, vert_modes, precision=PRECISE)
    by_col = lambda m: xor_order(m.reshape(nlev, levs, levd), x, 1).reshape(nlev, nlev)
    by_row = lambda m: xor_order(m.reshape(levs, levd, nlev), x, 0).reshape(nlev, nlev)
    w1 = by_col(jnp.where(first, vert_project, mix)), by_col(jnp.where(first, mix, vert_project))
    w1 = jnp.concatenate(w1, axis=1)
    w2 = by_row(jnp.where(first, vert_modes, drop)), by_row(jnp.where(first, drop, vert_modes))
    w2 = jnp.concatenate(w2, axis=0)

    def three(w):
        hi = lax.reduce_precision(w, 8, 7)
        lo = (w - hi).astype(BF16)
        hi = hi.astype(BF16)
        return jnp.concatenate([hi, hi, lo], axis=1)

    w1, w2 = three(w1), three(w2)
    rates = mode_rates[:, None]
    perm = (lat_rel.reshape(-1, 1) == jnp.arange(nlat, dtype=jnp.int32)[None, :]).astype(BF16)
    my_waves = waves[0, 0]
    counts = pick_values(my_waves, truncation) - my_waves + 1

    lat_lev = ("lat", "lev")

    def exchange(blocks, order):
        out = list(blocks)
        for r in order:
            if r:
                pairs = [(i, i ^ r) for i in range(groups)]
                out[r] = lax.ppermute(blocks[r], lat_lev, pairs)
        return out

    def swap(block):
        return lax.ppermute(block, "fld", [(0, 1), (1, 0)])

    far, near = far_near(groups)
    tables, arrived = [], []
    for i, (at, part) in enumerate(zip(starts, parts)):
        w = waves[:, :, at : at + part].reshape(-1)
        lanes = jnp.broadcast_to(w.astype(F32)[:, None], (w.shape[0], LANES))
        tables.append(make_table(lanes, nlon))
        blocks = dft(grid_state[0], tables[i], lat_rows, lanes, groups)
        arrived.append(exchange(blocks, far + near))
    first_slot = jnp.full((1,), f * (slots // 2), jnp.int32)
    leg = permute_legendre(first_slot, jnp.swapaxes(legendre, 1, 2), perm, slots // 2)
    returned = []
    for i, (at, part) in enumerate(zip(starts, parts)):
        other = gather_halves(arrived[i])
        other = swap(other)
        info = jnp.stack(
            [
                my_waves[at : at + part],
                counts[at : at + part],
                jnp.full((part,), f, jnp.int32),
            ]
        )
        res = legendre_step(
            info, leg, at, w1, w2, rates, arrived[i], other, levs, levd, latd
        )
        got = swap(res[groups])
        sent = fill_halves(res[:groups], got)
        returned.append(exchange(sent, near + far))
    sets = list(zip(tables, returned))
    scale = float(nmodes) ** (-0.5)
    shape = (levd, latd, nlon)
    total = inverse_dft(sets[:-1], shape, None, scale, BF16)
    total = inverse_dft(sets[-1:], shape, total, scale, BF16)
    return total[None]


def far_near(groups):
    rels = tuple(range(groups))
    return rels[groups // 2 :], rels[: groups // 2]


def power_of_two(n):
    return n & (n - 1) == 0


def solution(mesh):
    in_specs = (
        P(("member", "fld"), "lev", "lat", None),
        P(),
        P(),
        P(),
        P(),
        P(),
        P(),
        P(("lat", "lev"), None, None),
        P(),
        P(),
        P(),
        P(),
        P(),
    )
    out_specs = P(("member", "fld"), "lev", "lat", None)
    lats, levs = mesh.shape["lat"], mesh.shape["lev"]

    groups = lats * levs
    small = (
        mesh.shape["fld"] == 2 and power_of_two(lats) and power_of_two(levs) and 1 < groups <= 8
    )

    def local(grid_state, *rest):
        legendre = rest[6]
        levd, latd, nlon = grid_state.shape[1:]
        share = LANES - latd
        fits = (
            legendre.shape[0] % (4 * sum(SHARES)) == 0
            and levd % LEVELS == 0
            and latd % 8 == 0
            and share > 0
            and share * (2 * LEVELS - 1) == latd
            and nlon % (3 * LANES) == 0
        )
        if small and fits:
            unit = legendre.shape[0] // (2 * sum(SHARES))
            return local_fast([unit * n for n in SHARES], grid_state, *rest)
        return local_general(grid_state, *rest)

    return jax.shard_map(local, mesh=mesh, in_specs=in_specs, out_specs=out_specs, check_vma=False)
```

```python
import functools

import jax
import jax.numpy as jnp
from jax import lax
from jax.experimental import pallas as pl
from jax.experimental.pallas import tpu as pltpu
from jax.sharding import PartitionSpec as P


PRECISE = lax.Precision.HIGHEST
BF16 = jnp.bfloat16
F32 = jnp.float32


def dft_table(wavenums, nlon):
    columns = jnp.arange(nlon, dtype=jnp.int32)
    turns = columns[:, None] * wavenums[None, :] % nlon
    angles = turns.astype(jnp.float32) * (2.0 * jnp.pi / nlon)
    return jnp.stack([jnp.cos(angles), -jnp.sin(angles)], axis=1).astype(jnp.bfloat16)


def pick_values(idents, source_table):
    hits = idents[:, None] == jnp.arange(source_table.shape[0], dtype=jnp.int32)[None, :]
    return jnp.sum(jnp.where(hits, source_table[None, :], 0), axis=1)


def layer_eigen_basis(matrix, columns):
    return jnp.einsum("skcj,ij->skci", columns, matrix, precision=PRECISE)


def analyse(legendre, fourier_data):
    return jnp.einsum("skl,slx->skx", legendre, fourier_data, preferred_element_type=jnp.float32)


def synthesise(legendre, coeffs):
    return jnp.einsum("skl,skx->slx", legendre, coeffs, preferred_element_type=jnp.float32)


def local_general(
    grid_state,
    lat_order,
    slot_wave,
    truncation,
    zonal_wind,
    zonal_rate,
    quad_weight,
    legendre,
    vert_modes,
    vert_project,
    mode_rates,
    thermal_into_spread_matrix,
    pressure_balance_matrix,
):
    levd, latd, nlon = (grid_state.shape[1], grid_state.shape[2], grid_state.shape[3])
    slots = legendre.shape[0]
    nmodes = slot_wave.shape[0]
    nlat = lat_order.shape[0]
    nlev = vert_modes.shape[0]
    lat_count = lax.axis_size("lat")
    lev_count = lax.axis_size("lev")
    lat_index = lax.axis_index("lat")
    lev_index = lax.axis_index("lev")
    unknown_position = lax.axis_index("fld")
    my_lats = lax.dynamic_slice_in_dim(lat_order, lat_index * latd, latd)
    onehot = (my_lats[:, None] == jnp.arange(nlat, dtype=jnp.int32)[None, :]).astype(jnp.float32)
    per_lat = jnp.dot(
        onehot, jnp.stack([zonal_wind, zonal_rate, quad_weight], axis=1), precision=PRECISE
    )
    values = grid_state[0].astype(jnp.float32)
    flux = (values * (per_lat[None, :, 0][:, :, None] + values)).astype(jnp.bfloat16)
    count_rows = levd * latd
    stacked = jnp.concatenate(
        [grid_state[0].reshape(count_rows, nlon), flux.reshape(count_rows, nlon)], axis=0
    )
    table = dft_table(slot_wave, nlon).reshape(nlon, 2 * nmodes)
    spectra = lax.dot_general(
        table, stacked, (((0,), (1,)), ((), ())), preferred_element_type=jnp.float32
    ) * nlon ** (-0.5)
    spectra = spectra.reshape(2, nmodes, 2 * count_rows)
    plain = spectra[:, :, :count_rows]
    moved = spectra[:, :, count_rows:]
    rate_row = jnp.tile(per_lat[:, 1], levd)[None, :]
    weight_row = jnp.tile(per_lat[:, 2], levd)[None, :]
    wave_float = slot_wave.astype(jnp.float32)[:, None]
    factor = rate_row * wave_float
    real_part = (plain[0] + factor * moved[1]) * weight_row
    imag_part = (plain[1] - factor * moved[0]) * weight_row
    fourier = jnp.stack([real_part, imag_part], axis=0).astype(jnp.bfloat16)
    arrived = lax.all_to_all(fourier, ("lat", "lev"), split_axis=1, concat_axis=2, tiled=True)
    arrived = arrived.reshape(2, slots, lat_count, lev_count, levd, latd)
    arranged = jnp.transpose(arrived, (1, 2, 5, 0, 3, 4))
    arranged = arranged.reshape(slots, nlat, 2 * nlev)
    position = jnp.zeros((nlat,), jnp.int32).at[lat_order].set(jnp.arange(nlat, dtype=jnp.int32))
    ordered = jnp.take(arranged, position, axis=1)
    owner_index = lat_index * lev_count + lev_index
    my_waves = lax.dynamic_slice_in_dim(slot_wave, owner_index * slots, slots)
    limits = pick_values(my_waves, truncation)
    counts = limits - my_waves + 1
    degree = jnp.arange(nmodes, dtype=jnp.int32)
    valid = (degree[None, :] < counts[:, None])[:, :, None]
    own_spec = jnp.where(valid, analyse(legendre, ordered), jnp.float32(0.0))
    joined_harmonic_unknowns = lax.all_gather(own_spec, "fld", axis=2, tiled=True)
    joined_harmonic_unknowns = joined_harmonic_unknowns.reshape(slots, nmodes, 2, 2, nlev)
    outflow_rate_coeffs = joined_harmonic_unknowns[:, :, 0]
    thermal_coeffs = joined_harmonic_unknowns[:, :, 1]
    n_deg = (my_waves[:, None] + degree[None, :]).astype(jnp.float32)
    elliptic_inverse_scale = (n_deg * (n_deg + 1.0) / (nmodes * (nmodes - 1)))[:, :, None, None]
    outflow_rate_source = outflow_rate_coeffs + elliptic_inverse_scale * layer_eigen_basis(
        thermal_into_spread_matrix, thermal_coeffs
    )
    projected = layer_eigen_basis(vert_project, outflow_rate_source) / (
        1.0 + elliptic_inverse_scale * mode_rates
    )
    outflow_rate_next = layer_eigen_basis(vert_modes, projected)
    thermal_next = thermal_coeffs - layer_eigen_basis(pressure_balance_matrix, outflow_rate_next)
    own_new = (
        jnp.where(unknown_position == 0, outflow_rate_next, thermal_next)
        .astype(jnp.bfloat16)
        .reshape(slots, nmodes, 2 * nlev)
    )
    back = synthesise(legendre, own_new) * nmodes ** (-0.5)
    back = jnp.take(back, lat_order, axis=1).astype(jnp.bfloat16)
    shaped = back.reshape(slots, lat_count, latd, 2, lev_count, levd)
    outgoing = jnp.transpose(shaped, (3, 0, 1, 4, 5, 2)).reshape(
        2, slots, lat_count * lev_count * count_rows
    )
    returned = lax.all_to_all(outgoing, ("lat", "lev"), split_axis=2, concat_axis=1, tiled=True)
    leading = returned.reshape(2 * nmodes, count_rows)
    grid_out = lax.dot_general(
        leading, table, (((0,), (1,)), ((), ())), preferred_element_type=jnp.float32
    ) * nmodes ** (-0.5)
    return grid_out.astype(jnp.bfloat16).reshape(1, levd, latd, nlon)


LANES = 128
LEVELS = 8
SHARES = (1, 1)


def xor_order(array, index, axis):
    size = array.shape[axis]
    bits = size.bit_length() - 1
    shape = array.shape[:axis] + (2,) * bits + array.shape[axis + 1 :]
    out = array.reshape(shape)
    for b in range(bits):
        ax = axis + bits - 1 - b
        out = jnp.where((index >> b) & 1 == 1, jnp.flip(out, ax), out)
    return out.reshape(array.shape)


def packed_rows():
    return 2 * LEVELS - 1


def spare_lanes(row, last, latd):
    index, values = row
    share = LANES - latd
    lane = lax.broadcasted_iota(jnp.int32, values.shape, 1)
    turned = pltpu.roll(last, (latd - share * index) % LANES, 1)
    return jnp.where(lane < latd, values, turned)


def last_row(rows, latd):
    share = LANES - latd
    lane = lax.broadcasted_iota(jnp.int32, rows[0].shape, 1)
    out = pltpu.roll(rows[0], LANES - latd, 1)
    for i, row in enumerate(rows[1:], 1):
        turned = pltpu.roll(row, (share * i - latd) % LANES, 1)
        out = jnp.where(lane >= share * i, turned, out)
    return out


def table_kernel(nlon, wave_ref, out):
    rows = wave_ref.shape[0]
    nblk = nlon // LANES
    wave = wave_ref[...]
    lane = lax.broadcasted_iota(jnp.int32, (rows, LANES), 1)

    def sincos(step):
        turns = (lane * step).astype(F32) * wave
        turns = turns - nlon * jnp.floor(turns * (1.0 / nlon) + 0.5)
        quarter = jnp.floor(turns * (4.0 / nlon) + 0.5)
        x = (turns - quarter * (nlon / 4.0)) * (2.0 * jnp.pi / nlon)
        y = x * x
        s = x * (1.0 + y * (-1 / 6 + y * (1 / 120 + y * (-1 / 5040 + y * (1 / 362880)))))
        c = 1.0 + y * (-1 / 2 + y * (1 / 24 + y * (-1 / 720 + y * (1 / 40320))))
        c = c - y * y * y * y * y * (1 / 3628800)
        odd = jnp.abs(quarter) == 1.0
        half = jnp.abs(quarter) == 2.0
        sine = jnp.where(odd, c * quarter, jnp.where(half, -s, s))
        cosine = jnp.where(odd, -s * quarter, jnp.where(half, -c, c))
        return cosine, sine

    cl, sl = sincos(1)
    ch, sh = sincos(LANES)
    for b in range(nblk):
        c, s = ch[:, b : b + 1], sh[:, b : b + 1]
        cols = slice(b * LANES, (b + 1) * LANES)
        out[:rows, cols] = (c * cl - s * sl).astype(BF16)
        out[rows:, cols] = (-(s * cl + c * sl)).astype(BF16)


def make_table(wave_lanes, nlon):
    return pl.pallas_call(
        functools.partial(table_kernel, nlon),
        out_shape=jax.ShapeDtypeStruct((2 * wave_lanes.shape[0], nlon), BF16),
        name="table",
    )(wave_lanes)


def dft_kernel(groups, latd, x_ref, t_ref, lat_ref, wave_ref, *rest):
    outs, (xf,) = rest[:groups], rest[groups:]
    rows = t_ref.shape[0]
    half = rows // 2
    per = half // groups
    nblk = x_ref.shape[2] // LANES

    @pl.when(pl.program_id(0) == 0)
    def _():
        xf[...] = jnp.zeros_like(xf)

    wind = jnp.broadcast_to(lat_ref[...].T[:latd, 0:1], (latd, LANES))
    wind = jnp.concatenate([wind] * nblk, axis=1)
    weight = lat_ref[2:3, :] * float(x_ref.shape[2]) ** (-0.5)
    factor = wave_ref[...] * lat_ref[1:2, :]

    def load(v):
        xv = x_ref[v]
        x32 = xv.astype(F32)
        xf[v % 2, 0:latd, :] = xv
        xf[v % 2, LANES : LANES + latd, :] = (x32 * (wind + x32)).astype(BF16)

    last = None
    load(LEVELS - 1)
    order = [LEVELS - 1, *range(LEVELS - 1)]
    for at, v in enumerate(order):
        if at + 1 < LEVELS:
            load(order[at + 1])
        both = lax.dot_general(
            t_ref[...], xf[v % 2], (((1,), (1,)), ((), ())), preferred_element_type=F32
        )
        plain, moved = both[:, :LANES], both[:, LANES:]
        real = (plain[:half] + factor * moved[half:]) * weight
        imag = (plain[half:] - factor * moved[:half]) * weight
        parts = [(v, real)]
        if last is None:
            last = imag
        else:
            parts.append((LEVELS + v, imag))
        for index, values in parts:
            full = spare_lanes((index, values), last, latd)
            for g in range(groups):
                outs[g][index] = full[g * per : (g + 1) * per].astype(BF16)


def dft(x, table, lat_rows, wave_lanes, groups):
    levd, latd, nlon = x.shape
    rows = table.shape[0]
    half = rows // 2
    per = half // groups
    packed = packed_rows()
    const = lambda i: (0, 0)
    block = pl.BlockSpec((packed, per, LANES), lambda i: (i, 0, 0))
    return pl.pallas_call(
        functools.partial(dft_kernel, groups, latd),
        out_shape=[jax.ShapeDtypeStruct((levd // LEVELS * packed, per, LANES), BF16)] * groups,
        grid=(levd // LEVELS,),
        in_specs=[
            pl.BlockSpec((LEVELS, latd, nlon), lambda i: (i, 0, 0)),
            pl.BlockSpec((rows, nlon), const),
            pl.BlockSpec(lat_rows.shape, const),
            pl.BlockSpec((half, LANES), const),
        ],
        out_specs=[block] * groups,
        scratch_shapes=[pltpu.VMEM((2, 2 * LANES, nlon), BF16)],
        cost_estimate=pl.CostEstimate(
            flops=4 * rows * levd * latd * nlon,
            bytes_accessed=2 * levd * latd * (nlon + rows) + 2 * rows * nlon,
            transcendentals=0,
        ),
        name="dft",
    )(x, table, lat_rows, wave_lanes)


def split3_dot(w3, x):
    hi = x.astype(BF16)
    lo = (x - hi.astype(F32)).astype(BF16)
    return jnp.dot(w3, jnp.concatenate([hi, lo, hi], axis=0), preferred_element_type=F32)


def permute_kernel(info, leg_ref, perm_ref, out):
    for j in range(leg_ref.shape[0]):
        out[j] = jnp.dot(perm_ref[...], leg_ref[j], preferred_element_type=F32).astype(BF16)


def permute_legendre(first_slot, leg, perm, count):
    _, nlat, nmodes = leg.shape
    lanes = perm.shape[0]
    step = 2 if count % 2 == 0 else 1
    return pl.pallas_call(
        permute_kernel,
        out_shape=jax.ShapeDtypeStruct((count, lanes, nmodes), BF16),
        grid_spec=pltpu.PrefetchScalarGridSpec(
            num_scalar_prefetch=1,
            grid=(count // step,),
            in_specs=[
                pl.BlockSpec((step, nlat, nmodes), lambda t, s: (s[0] // step + t, 0, 0)),
                pl.BlockSpec((lanes, nlat), lambda t, s: (0, 0)),
            ],
            out_specs=pl.BlockSpec((step, lanes, nmodes), lambda t, s: (t, 0, 0)),
        ),
        cost_estimate=pl.CostEstimate(
            flops=2 * count * lanes * nlat * nmodes,
            bytes_accessed=2 * count * (lanes + nlat) * nmodes,
            transcendentals=0,
        ),
        name="permute_legendre",
    )(first_slot, leg, perm)


def legendre_kernel(
    groups, levs, levd, latd, nmodes, info, leg_ref, w1_ref, w2_ref, mr_ref, *rest
):
    own = rest[:groups]
    other = rest[groups]
    outs = rest[groups + 1 : 2 * groups + 1]
    give = rest[2 * groups + 1]
    data, fresh_data = rest[2 * groups + 2 :]
    slots = outs[0].shape[1]
    lats = groups // levs
    nlev = levs * levd
    total = 4 * nlev
    count = leg_ref.shape[0]
    packed = packed_rows()
    t = pl.program_id(0)

    def each_group(move):
        def body(group, carry):
            for rel in range(groups):
                dz, dx = rel // levs, rel % levs
                for field in range(2):
                    base = field * nlev + dx * levd + group * LEVELS
                    rows = [
                        base + (i // LEVELS) * 2 * nlev + i % LEVELS for i in range(packed + 1)
                    ]
                    move(rel, field, dz, group * packed, rows)
            return carry

        lax.fori_loop(0, levd // LEVELS, body, 0)

    def unpack(rel, field, dz, at, rows):
        values = []
        for i in range(packed):
            value = own[rel][at + i] if field == 0 else other[rel, at + i]
            values.append(value.astype(F32)[:slots])
        values.append(last_row(values, latd))
        for row, value in zip(rows, values):
            data[dz, pl.ds(row, slots, stride=total), :] = value

    def pack(rel, field, dz, at, rows):
        last = fresh_data[dz, pl.ds(rows[-1], slots, stride=total), :]
        for i in range(packed):
            value = fresh_data[dz, pl.ds(rows[i], slots, stride=total), :]
            full = spare_lanes((i, value), last, latd).astype(BF16)
            if field == 0:
                outs[rel][at + i] = full
            else:
                give[rel, at + i, :slots] = full

    @pl.when(t == 0)
    def _():
        each_group(unpack)

    k = lax.broadcasted_iota(jnp.int32, (1, nmodes), 1)
    first = info[2, 0] == 0
    keep_own = jnp.where(first, 0.0, 1.0)
    keep_other = jnp.where(first, 1.0, 0.0)
    legs = [leg_ref[j] for j in range(count)]
    fresh = []
    for j in range(count):
        slot = t * count + j
        wave, terms = info[0, slot], info[1, slot]
        n = (wave + k).astype(F32)
        h = n * (n + 1.0) / float(nmodes * (nmodes - 1))
        scale_own = jnp.where(first, 1.0, h)
        scale_other = jnp.where(first, h, 1.0)
        denom = 1.0 + h * mr_ref[...]
        here = pl.ds(pl.multiple_of(slot * total, total), total)
        lined = jnp.concatenate([data[dz, here, :].astype(BF16) for dz in range(lats)], axis=1)
        spec = jnp.dot(lined, legs[j], preferred_element_type=F32)
        spec = jnp.where(k < terms, spec, 0.0)
        new = []
        for c in range(2):
            a = spec[c * 2 * nlev : c * 2 * nlev + nlev]
            b = spec[c * 2 * nlev + nlev : (c + 1) * 2 * nlev]
            src = jnp.concatenate([a * scale_own, b * scale_other], axis=0)
            q = split3_dot(w1_ref[...], src) / denom
            both = split3_dot(w2_ref[...], q)
            new.append(both[:nlev] + keep_own * a)
            new.append(both[nlev:] + keep_other * b)
        fresh.append(jnp.concatenate(new, axis=0).astype(BF16))
    for j in range(count):
        back = lax.dot_general(
            fresh[j], legs[j], (((1,), (1,)), ((), ())), preferred_element_type=F32
        )
        here = pl.ds(pl.multiple_of((t * count + j) * total, total), total)
        back = back * float(nmodes) ** (-0.5)
        for dz in range(lats):
            fresh_data[dz, here, :] = back[:, dz * LANES : (dz + 1) * LANES]

    @pl.when(t == pl.num_programs(0) - 1)
    def _():
        each_group(pack)


def legendre_step(info, leg, at, w1, w2, rates, own, other, levs, levd, latd):
    groups, packed, rows, _ = other.shape
    count = own[0].shape[1] // 2
    lanes, nmodes = leg.shape[1:]
    nlev = levs * levd
    const = lambda t, s: (0, 0)
    step = 2 if count % 2 == 0 else 1
    piece = pl.BlockSpec((packed, 2 * count, LANES), lambda t, s: (0, 0, 0))
    half = pl.BlockSpec((packed, count, LANES), lambda t, s: (0, 0, 0))
    stack = pl.BlockSpec((groups, packed, rows, LANES), lambda t, s: (0, 0, 0, 0))
    flops = count * 2 * 2 * nlev * 2 * nmodes * lanes * 2
    return pl.pallas_call(
        functools.partial(legendre_kernel, groups, levs, levd, latd, nmodes),
        out_shape=[jax.ShapeDtypeStruct((packed, count, LANES), BF16)] * groups
        + [jax.ShapeDtypeStruct(other.shape, BF16)],
        grid_spec=pltpu.PrefetchScalarGridSpec(
            num_scalar_prefetch=1,
            grid=(count // step,),
            in_specs=[
                pl.BlockSpec((step, lanes, nmodes), lambda t, s: (at // step + t, 0, 0)),
                pl.BlockSpec(w1.shape, const),
                pl.BlockSpec(w2.shape, const),
                pl.BlockSpec(rates.shape, const),
            ]
            + [piece] * groups
            + [pl.BlockSpec(memory_space=pltpu.VMEM)],
            out_specs=[half] * groups + [stack],
            scratch_shapes=[pltpu.VMEM((lanes // LANES, padded(count) * 4 * nlev, LANES), F32)] * 2,
        ),
        cost_estimate=pl.CostEstimate(
            flops=flops,
            bytes_accessed=count * 2 * (nmodes * lanes + 8 * nlev * lanes),
            transcendentals=0,
        ),
        name="legendre",
    )(info, leg, w1, w2, rates, *own, other)


def gather_kernel(groups, *refs):
    ins, out = refs[:groups], refs[-1]
    half = ins[0].shape[1] // 2
    for r in range(groups):
        out[r, :, :half] = ins[r][...].astype(F32)[:, half:].astype(BF16)


def padded(rows):
    return -(-rows // 8) * 8


def gather_halves(blocks):
    groups = len(blocks)
    packed, count, _ = blocks[0].shape
    half = padded(count // 2)
    group = packed
    return pl.pallas_call(
        functools.partial(gather_kernel, groups),
        out_shape=jax.ShapeDtypeStruct((groups, packed, half, LANES), BF16),
        grid=(packed // group,),
        in_specs=[pl.BlockSpec((group, count, LANES), lambda i: (i, 0, 0))] * groups,
        out_specs=pl.BlockSpec((groups, group, half, LANES), lambda i: (0, i, 0, 0)),
        name="gather_halves",
    )(*blocks)


def fill_kernel(groups, got, *refs):
    ins, outs = refs[:groups], refs[groups:]
    rows, half = ins[0].shape[:2]
    here = pl.ds(pl.program_id(0) * rows, rows)
    for r in range(groups):
        both = [ins[r][...].astype(F32), got[r, here].astype(F32)[:, :half]]
        outs[r][...] = jnp.concatenate(both, axis=1).astype(BF16)


def fill_halves(blocks, got):
    groups, packed, _, _ = got.shape
    half = blocks[0].shape[1]
    group = packed
    return pl.pallas_call(
        functools.partial(fill_kernel, groups),
        out_shape=[jax.ShapeDtypeStruct((packed, 2 * half, LANES), BF16)] * groups,
        grid=(packed // group,),
        in_specs=[pl.BlockSpec(memory_space=pltpu.VMEM)]
        + [pl.BlockSpec((group, half, LANES), lambda i: (i, 0, 0))] * groups,
        out_specs=[pl.BlockSpec((group, 2 * half, LANES), lambda i: (i, 0, 0))] * groups,
        name="fill_halves",
    )(got, *blocks)


def inverse_kernel(counts, latd, scale, add, *refs):
    tabs, refs = refs[: len(counts)], refs[len(counts) :]
    pieces, refs = refs[: sum(counts)], refs[sum(counts) :]
    partial = refs[0] if add else None
    out, lhs = refs[-2:]
    nlon = tabs[0].shape[1]
    packed = packed_rows()
    base, depth = 0, 0
    for tab, number in zip(tabs, counts):
        half = tab.shape[0] // 2
        group = pieces[depth : depth + number]
        rows = [
            jnp.concatenate([ref[i].astype(F32) for ref in group], axis=0) for i in range(packed)
        ]
        rows.append(last_row(rows, latd))
        for i, row in enumerate(rows):
            v, at = i % LEVELS, base + i // LEVELS * half
            lhs[v * LANES : (v + 1) * LANES, at : at + half] = row.astype(BF16).T
        base += 2 * half
        depth += number
    step = 3 * LANES
    for j in range(0, nlon, step):
        cols = slice(j, j + step)
        grid, base = None, 0
        for tab in tabs:
            rows = tab.shape[0]
            term = jnp.dot(
                lhs[:, base : base + rows], tab[:, cols], preferred_element_type=F32
            )
            grid = term if grid is None else grid + term
            base += rows
        grid = grid * scale
        for v in range(LEVELS):
            piece = grid[v * LANES : v * LANES + latd]
            if partial is not None:
                piece = piece + partial[v, :, cols].astype(F32)
            out[v, :, cols] = piece.astype(out.dtype)


def inverse_dft(sets, shape, partial, scale, out_dtype):
    tabs = [tab for tab, _ in sets]
    pieces = [p for _, group in sets for p in group]
    levd, latd, nlon = shape
    rows = sum(tab.shape[0] for tab in tabs)
    packed = packed_rows()
    grid_block = pl.BlockSpec((LEVELS, latd, nlon), lambda i: (i, 0, 0))
    in_specs = [pl.BlockSpec(tab.shape, lambda i: (0, 0)) for tab in tabs] + [
        pl.BlockSpec((packed, p.shape[1], LANES), lambda i: (i, 0, 0)) for p in pieces
    ]
    args = [*tabs, *pieces]
    if partial is not None:
        in_specs.append(grid_block)
        args.append(partial)
    counts = tuple(len(group) for _, group in sets)
    return pl.pallas_call(
        functools.partial(inverse_kernel, counts, latd, scale, partial is not None),
        out_shape=jax.ShapeDtypeStruct((levd, latd, nlon), out_dtype),
        grid=(levd // LEVELS,),
        in_specs=in_specs,
        out_specs=grid_block,
        scratch_shapes=[pltpu.VMEM((LEVELS * LANES, rows), BF16)],
        cost_estimate=pl.CostEstimate(
            flops=2 * rows * levd * latd * nlon,
            bytes_accessed=2 * levd * latd * (nlon + rows) + 2 * rows * nlon,
            transcendentals=0,
        ),
        name="inverse_dft",
    )(*args)


def local_fast(
    parts,
    grid_state,
    lat_order,
    slot_wave,
    truncation,
    zonal_wind,
    zonal_rate,
    quad_weight,
    legendre,
    vert_modes,
    vert_project,
    mode_rates,
    thermal_matrix,
    pressure_matrix,
):
    levd, latd, nlon = grid_state.shape[1:]
    slots = legendre.shape[0]
    nmodes = slot_wave.shape[0]
    nlat = lat_order.shape[0]
    nlev = vert_modes.shape[0]
    lats, levs = lax.axis_size("lat"), lax.axis_size("lev")
    groups = lats * levs
    z, x, f = lax.axis_index("lat"), lax.axis_index("lev"), lax.axis_index("fld")
    me = z * levs + x
    starts = [sum(parts[:i]) for i in range(len(parts))]

    waves = slot_wave.reshape(groups, 2, slots // 2)
    waves = xor_order(xor_order(waves, me, 0), f, 1)
    lat_rel = xor_order(lat_order.reshape(lats, latd), z, 0)
    lat_rel = jnp.pad(lat_rel, ((0, 0), (0, LANES - latd)), constant_values=-1)
    hits = lat_rel[0][None, :, None] == jnp.arange(nlat, dtype=jnp.int32)[None, None, :]
    blank = jnp.zeros_like(quad_weight)
    zonal = jnp.stack([zonal_wind, zonal_rate, quad_weight] + [blank] * 5, axis=0)
    lat_rows = jnp.sum(jnp.where(hits, zonal[:, None, :], 0.0), axis=2)

    first = f == 0
    mix = jnp.dot(vert_project, thermal_matrix, precision=PRECISE)
    drop = -jnp.dot(pressure_matrix, vert_modes, precision=PRECISE)
    by_col = lambda m: xor_order(m.reshape(nlev, levs, levd), x, 1).reshape(nlev, nlev)
    by_row = lambda m: xor_order(m.reshape(levs, levd, nlev), x, 0).reshape(nlev, nlev)
    w1 = by_col(jnp.where(first, vert_project, mix)), by_col(jnp.where(first, mix, vert_project))
    w1 = jnp.concatenate(w1, axis=1)
    w2 = by_row(jnp.where(first, vert_modes, drop)), by_row(jnp.where(first, drop, vert_modes))
    w2 = jnp.concatenate(w2, axis=0)

    def three(w):
        hi = lax.reduce_precision(w, 8, 7)
        lo = (w - hi).astype(BF16)
        hi = hi.astype(BF16)
        return jnp.concatenate([hi, hi, lo], axis=1)

    w1, w2 = three(w1), three(w2)
    rates = mode_rates[:, None]
    perm = (lat_rel.reshape(-1, 1) == jnp.arange(nlat, dtype=jnp.int32)[None, :]).astype(BF16)
    my_waves = waves[0, 0]
    counts = pick_values(my_waves, truncation) - my_waves + 1

    lat_lev = ("lat", "lev")

    def exchange(blocks, order):
        out = list(blocks)
        for r in order:
            if r:
                pairs = [(i, i ^ r) for i in range(groups)]
                out[r] = lax.ppermute(blocks[r], lat_lev, pairs)
        return out

    def swap(block):
        return lax.ppermute(block, "fld", [(0, 1), (1, 0)])

    far, near = far_near(groups)
    tables, arrived = [], []
    for i, (at, part) in enumerate(zip(starts, parts)):
        w = waves[:, :, at : at + part].reshape(-1)
        lanes = jnp.broadcast_to(w.astype(F32)[:, None], (w.shape[0], LANES))
        tables.append(make_table(lanes, nlon))
        blocks = dft(grid_state[0], tables[i], lat_rows, lanes, groups)
        arrived.append(exchange(blocks, far + near))
    first_slot = jnp.full((1,), f * (slots // 2), jnp.int32)
    leg = permute_legendre(first_slot, jnp.swapaxes(legendre, 1, 2), perm, slots // 2)
    returned = []
    for i, (at, part) in enumerate(zip(starts, parts)):
        other = gather_halves(arrived[i])
        other = swap(other)
        info = jnp.stack(
            [
                my_waves[at : at + part],
                counts[at : at + part],
                jnp.full((part,), f, jnp.int32),
            ]
        )
        res = legendre_step(
            info, leg, at, w1, w2, rates, arrived[i], other, levs, levd, latd
        )
        got = swap(res[groups])
        sent = fill_halves(res[:groups], got)
        returned.append(exchange(sent, near + far))
    sets = list(zip(tables, returned))
    scale = float(nmodes) ** (-0.5)
    shape = (levd, latd, nlon)
    total = inverse_dft(sets[:-1], shape, None, scale, BF16)
    total = inverse_dft(sets[-1:], shape, total, scale, BF16)
    return total[None]


def far_near(groups):
    rels = tuple(range(groups))
    return rels[groups // 2 :], rels[: groups // 2]


def power_of_two(n):
    return n & (n - 1) == 0


def solution(mesh):
    in_specs = (
        P(("member", "fld"), "lev", "lat", None),
        P(),
        P(),
        P(),
        P(),
        P(),
        P(),
        P(("lat", "lev"), None, None),
        P(),
        P(),
        P(),
        P(),
        P(),
    )
    out_specs = P(("member", "fld"), "lev", "lat", None)
    lats, levs = mesh.shape["lat"], mesh.shape["lev"]

    groups = lats * levs
    small = (
        mesh.shape["fld"] == 2 and power_of_two(lats) and power_of_two(levs) and 1 < groups <= 8
    )

    def local(grid_state, *rest):
        legendre = rest[6]
        levd, latd, nlon = grid_state.shape[1:]
        share = LANES - latd
        fits = (
            legendre.shape[0] % (4 * sum(SHARES)) == 0
            and levd % LEVELS == 0
            and latd % 8 == 0
            and share > 0
            and share * (2 * LEVELS - 1) == latd
            and nlon % (3 * LANES) == 0
        )
        if small and fits:
            unit = legendre.shape[0] // (2 * sum(SHARES))
            return local_fast([unit * n for n in SHARES], grid_state, *rest)
        return local_general(grid_state, *rest)

    return jax.shard_map(local, mesh=mesh, in_specs=in_specs, out_specs=out_specs, check_vma=False)
```
